32 devices in a mesh: blk: 8 (over z, x), col: 4 (over y, core).
Axes of the slice: x: 2, y: 2, z: 4, core: 2. Of those that a mesh axis runs over, the one named last changes fastest.
Arguments:
- points: bfloat16 [4096, 128], P(('blk', 'col')), may hold values from -4.5 to 4.5
- targets: float32 [4096, 32], P(('blk', 'col')), may hold values from -6 to 6
- pivots: int32 [2, 256], replicated, may hold values from 0 to 4095, as said below
Outputs:
- factor: bfloat16 [4096, 512], P(('blk', 'col'))
- solution: float32 [4096, 32], P(('blk', 'col'))
- residual: float32 [4096, 32], P(('blk', 'col'))
The draws below stay inside these ranges and needn't reach their ends.
Inputs may be any that keep to these rules, and one draw needn't show every extreme that they name: `pivots`: the 512 indices are distinct; 0 and 4095 are among them.
All inputs are finite; a program needn't handle non-finite values.
Results may differ from the reference program's by a relative error of at most 0.012.
Values may be sent and summed in bfloat16 or wider, within the bound.
A program may use at most 64 MiB of HBM per device.

```python
import jax
import jax.numpy as jnp
from jax import lax

FEATURES = 128
PIV_BLOCK = 256
RHS_COLS = 32
ITERS = 3
POINTS = 4096


def draw_points(key, part):
    row_key, value_key = jax.random.split(key, 2)
    values = jnp.clip(jax.random.normal(value_key, (POINTS, FEATURES), jnp.float32), -4.5, 4.5)
    scales = jnp.exp(jax.random.uniform(row_key, (POINTS,), jnp.float32, jnp.log(0.25), jnp.log(1.0)))
    result = values * scales[:, None]
    return jnp.clip(result, -4.5, 4.5).astype(jnp.bfloat16)


def draw_pivots(key, part):
    first_key, second_key = jax.random.split(jax.random.fold_in(key, 11))
    middle = jax.random.permutation(first_key, POINTS - 2)[:2 * PIV_BLOCK - 2].astype(jnp.int32) + 1
    ends = jnp.array([0, POINTS - 1], dtype=jnp.int32)
    chosen = jnp.concatenate([ends, middle])
    return jax.random.permutation(second_key, chosen).astype(jnp.int32).reshape(2, PIV_BLOCK)


def levels(key, extent, shards, low, largest):
    def one(axis_at, shards_of):
        heights = jax.random.uniform(jax.random.fold_in(jax.random.fold_in(key, 6), axis_at), (shards_of,), jnp.float32, low / len(shards), largest / len(shards))
        return jnp.repeat(jnp.exp(heights), extent[axis_at] // shards_of).reshape((-1,) + (1,) * (len(extent) - axis_at - 1))

    factor_of = one(*shards[0])
    for cut in shards[1:]:
        factor_of = factor_of * one(*cut)
    return factor_of


def noise(own_key, dims, width, bound, cuts=(), held_as=jnp.bfloat16):
    drawn = jax.random.normal(own_key, dims, jnp.float32) * width
    if len(cuts) > 0:
        drawn = levels(own_key, dims, cuts, -0.22, 0.18) * drawn
    return jnp.clip(drawn, min=-bound, max=bound).astype(held_as)


def setup_inputs(seed: int = 0) -> dict:
    keys = jax.random.split(jax.random.key(seed), 4)
    return {
        "points": draw_points(jax.random.fold_in(keys[3], 71), 0),
        "targets": noise(keys[1], (POINTS, RHS_COLS), 1.0, 6.0, ((0, 32),), jnp.float32),
        "pivots": draw_pivots(jax.random.fold_in(keys[3], 71), 0),
    }


noise_level = 0.5
jitter_level = 0.05
highest = lax.Precision.HIGHEST

def squared_norms(point_rows):
    wide_rows = point_rows.astype(jnp.float32)
    return jnp.sum(wide_rows * wide_rows, axis=1)

def kernel_block(left_rows, left_norms, right_rows, right_norms):
    inner = lax.dot_general(left_rows.astype(jnp.float32), right_rows.astype(jnp.float32), (((1,), (1,)), ((), ())), preferred_element_type=jnp.float32)
    distance = left_norms[:, None] + right_norms[None, :] - 2.0 * inner
    return jnp.exp(-2.0 * distance / FEATURES)

def lower_solve(lower_factor, right_rows):
    return jax.scipy.linalg.solve_triangular(lower_factor, right_rows.T, lower=True).T

def build_factor(point_rows, first_pick, second_pick):
    row_norms = squared_norms(point_rows)
    first_norms = squared_norms(first_pick)
    second_norms = squared_norms(second_pick)
    identity_piv = jnp.eye(first_pick.shape[0], dtype=jnp.float32)
    first_chol = jnp.linalg.cholesky(kernel_block(first_pick, first_norms, first_pick, first_norms) + jitter_level * identity_piv)
    first_coef = lower_solve(first_chol, kernel_block(point_rows, row_norms, first_pick, first_norms))
    shared_coef = lower_solve(first_chol, kernel_block(second_pick, second_norms, first_pick, first_norms))
    schur_block = kernel_block(second_pick, second_norms, second_pick, second_norms) + jitter_level * identity_piv - jnp.dot(shared_coef, shared_coef.T, precision=highest)
    second_chol = jnp.linalg.cholesky(schur_block)
    second_cross = kernel_block(point_rows, row_norms, second_pick, second_norms) - jnp.dot(first_coef, shared_coef.T, precision=highest)
    second_coef = lower_solve(second_chol, second_cross)
    return jnp.concatenate([first_coef, second_coef], axis=1)

def reference(points, targets, pivots):
    wide_factor = build_factor(points, points[pivots[0]], points[pivots[1]])
    factor = wide_factor.astype(jnp.bfloat16)
    gram = lax.dot_general(wide_factor, wide_factor, (((0,), (0,)), ((), ())), precision=highest)
    gram = gram + noise_level * jnp.eye(2 * PIV_BLOCK, dtype=jnp.float32)
    gram_chol = jnp.linalg.cholesky(gram)
    row_norms = squared_norms(points)

    def precondition(residual_now):
        projection = lax.dot_general(wide_factor, residual_now, (((0,), (0,)), ((), ())), precision=highest)
        coefficients = jax.scipy.linalg.cho_solve((gram_chol, True), projection)
        return (residual_now - jnp.dot(wide_factor, coefficients, precision=highest)) / noise_level
    block_rows = min(POINTS, 512)
    block_count = POINTS // block_rows

    def kernel_product(directions):

        def one_block(operands):
            weights = kernel_block(operands[0], operands[1], points, row_norms)
            return jnp.dot(weights, directions, precision=highest)
        stacked = lax.map(one_block, (points.reshape(block_count, block_rows, FEATURES), row_norms.reshape(block_count, block_rows)))
        return stacked.reshape(POINTS, RHS_COLS) + noise_level * directions
    solution = jnp.zeros_like(targets)
    residual = targets
    direction_now = precondition(residual)
    inner_now = jnp.sum(residual * direction_now, axis=0)
    for step_index in range(ITERS):
        image = kernel_product(direction_now)
        step_size = inner_now / jnp.sum(direction_now * image, axis=0)
        solution = solution + step_size * direction_now
        residual = residual - step_size * image
        if step_index + 1 < ITERS:
            scaled = precondition(residual)
            inner_next = jnp.sum(residual * scaled, axis=0)
            direction_now = scaled + inner_next / inner_now * direction_now
            inner_now = inner_next
    return (factor, solution, residual)
```

```python
import functools

import jax
import jax.numpy as jnp
from jax import lax
from jax.experimental import pallas as pl
from jax.experimental.pallas import tpu as pltpu
from jax.sharding import PartitionSpec as P

FEATURES = 128
ITERS = 3
LANES = 128


noise_level = 0.5
jitter_level = 0.05
highest = lax.Precision.HIGHEST
MESH = pl.DeviceIdType.MESH


def squared_norms(point_rows):
    wide_rows = point_rows.astype(jnp.float32)
    return jnp.sum(wide_rows * wide_rows, axis=1)


def kernel_block(left_rows, left_norms, right_rows, right_norms):
    inner = lax.dot_general(
        left_rows, right_rows, (((1,), (1,)), ((), ())), preferred_element_type=jnp.float32
    )
    distance = left_norms[:, None] + right_norms[None, :] - 2.0 * inner
    return jnp.exp(-2.0 * distance / FEATURES)


def lower_inverse_rows(rows):
    count = len(rows)
    lane = lax.broadcasted_iota(jnp.int32, (8, LANES), 1)
    sub = lax.broadcasted_iota(jnp.int32, (8, LANES), 0)

    def full_of(values):
        return jnp.broadcast_to(values, (8, LANES))

    rows = list(rows)
    done = []
    for p in range(count):
        base = 8 * p
        inside = (lane >= base) & (lane < base + 8)
        cols = [full_of(rows[p][:, base + c : base + c + 1]) for c in range(8)]
        forward = jnp.where(inside, jnp.where(lane == sub + base, 1.0, 0.0), rows[p])
        pivots = jnp.ones((8, LANES), jnp.float32)
        recips, spread_rows, coefs = [], [], []
        for j in range(8):
            pivot = full_of(cols[j][j : j + 1])
            recip = 1.0 / pivot
            pivots = jnp.where(sub == j, pivot, pivots)
            below = jnp.where(sub > j, cols[j] * recip, 0.0)
            spread_row = full_of(forward[j : j + 1])
            forward = forward - below * spread_row
            coef = {c: full_of(cols[c][j : j + 1]) for c in range(j + 1, 8)}
            for c in range(j + 1, 8):
                cols[c] = cols[c] - below * coef[c]
            recips.append(recip)
            spread_rows.append(spread_row)
            coefs.append(coef)
        done.append(jnp.where(lane <= sub + base, forward, 0.0) * lax.rsqrt(pivots))
        for v in range(p + 1, count):
            own = [full_of(rows[v][:, base + c : base + c + 1]) for c in range(8)]
            new = jnp.where(inside, 0.0, rows[v])
            for j in range(8):
                multiplier = own[j] * recips[j]
                new = new - multiplier * spread_rows[j]
                for c in range(j + 1, 8):
                    own[c] = own[c] - multiplier * coefs[j][c]
            rows[v] = new
    return done


def chol_kernel(matrix_ref, out_ref, work):
    blocks = matrix_ref.shape[0] // LANES
    work[...] = matrix_ref[...]
    row_at = lax.broadcasted_iota(jnp.int32, (LANES, LANES), 0)
    col_at = lax.broadcasted_iota(jnp.int32, (LANES, LANES), 1)
    lane_at = lax.broadcasted_iota(jnp.int32, (LANES, matrix_ref.shape[1]), 1)

    def one_block(j, carry):
        at = pl.multiple_of(j * LANES, LANES)
        here_rows = pl.ds(at, LANES)
        inverse = jnp.concatenate(
            lower_inverse_rows(
                [work[pl.ds(at + 8 * v, 8), pl.ds(at, LANES)] for v in range(LANES // 8)]
            ),
            axis=0,
        )
        work[here_rows, pl.ds(at, LANES)] = jnp.where(row_at == col_at, 1.0, 0.0)
        side = jnp.dot(
            inverse, work[here_rows, :], precision=highest, preferred_element_type=jnp.float32
        )
        out_ref[here_rows, :] = jnp.where(lane_at < at + LANES, side, 0.0)
        work[here_rows, :] = side

        def below(i, inner):
            to = pl.multiple_of(i * LANES, LANES)
            rows = work[pl.ds(to, LANES), :]
            rows = jnp.where((lane_at >= at) & (lane_at < at + LANES), 0.0, rows)
            work[pl.ds(to, LANES), :] = rows - lax.dot_general(
                work[here_rows, pl.ds(to, LANES)],
                side,
                (((0,), (0,)), ((), ())),
                precision=highest,
                preferred_element_type=jnp.float32,
            )
            return inner

        lax.fori_loop(j + 1, blocks, below, 0)
        return carry

    lax.fori_loop(0, blocks, one_block, 0)


def chol_inverse(matrix):
    vmem = pl.BlockSpec(memory_space=pltpu.VMEM)
    return pl.pallas_call(
        chol_kernel,
        out_shape=jax.ShapeDtypeStruct(matrix.shape, jnp.float32),
        in_specs=[vmem],
        out_specs=vmem,
        scratch_shapes=[pltpu.VMEM(matrix.shape, jnp.float32)],
        name="chol_inverse",
    )(matrix)


def build_factor(point_rows, picked):
    picked_norms = squared_norms(picked)
    identity = jnp.eye(picked.shape[0], dtype=jnp.float32)
    inverse = chol_inverse(
        kernel_block(picked, picked_norms, picked, picked_norms) + jitter_level * identity
    )
    cross = kernel_block(point_rows, squared_norms(point_rows), picked, picked_norms)
    return jnp.dot(cross, inverse.T, precision=highest)


def upper_blocks(count):
    return [(j, i) for i in range(count) for j in range(i + 1)]


def pack_upper(matrix):
    count = matrix.shape[0] // LANES
    return jnp.concatenate(
        [
            matrix[i * LANES : (i + 1) * LANES, j * LANES : (j + 1) * LANES]
            for i, j in upper_blocks(count)
        ],
        axis=0,
    )


def unpack_upper(packed, order):
    count = order // LANES
    blocks = {
        at: packed[k * LANES : (k + 1) * LANES] for k, at in enumerate(upper_blocks(count))
    }
    empty = jnp.zeros((LANES, LANES), packed.dtype)
    return jnp.concatenate(
        [
            jnp.concatenate([blocks.get((i, j), empty) for j in range(count)], axis=1)
            for i in range(count)
        ],
        axis=0,
    )


def here(width):
    return lax.axis_index("blk") * width + lax.axis_index("col")


def coords(index, width):
    return (lax.div(index, width), lax.rem(index, width))


def greet(n, width, me):
    barrier = pltpu.get_barrier_semaphore()

    def hello(i, carry):
        peer = lax.rem(me + i, n)
        pl.semaphore_signal(
            barrier, inc=1, device_id=coords(peer, width), device_id_type=MESH
        )
        return carry

    lax.fori_loop(1, n, hello, 0)
    pl.semaphore_wait(barrier, n - 1)


def spread(n, width, me, src, dst, send_sem, recv_sem):
    def push(i, carry):
        peer = lax.rem(me + i, n)
        pltpu.make_async_remote_copy(
            src_ref=src(peer, i),
            dst_ref=dst(peer, i),
            send_sem=send_sem,
            recv_sem=recv_sem,
            device_id=coords(peer, width),
            device_id_type=MESH,
        ).start()
        return carry

    lax.fori_loop(1, n, push, 0)


def drain(ref, sem):
    pltpu.make_async_copy(ref, ref, sem).wait()


def gather_kernel(n, width, own_ref, all_ref, send_sem, recv_sem, own_sem):
    me = here(width)
    keep = pltpu.make_async_copy(own_ref, all_ref.at[me], own_sem)
    keep.start()
    greet(n, width, me)
    spread(
        n, width, me, lambda peer, i: own_ref, lambda peer, i: all_ref.at[me], send_sem, recv_sem
    )
    drain(all_ref.at[pl.ds(0, n - 1)], recv_sem)
    drain(all_ref.at[pl.ds(0, n - 1)], send_sem)
    keep.wait()


def gather_all(own, n, width):
    vmem = pl.BlockSpec(memory_space=pltpu.VMEM)
    return pl.pallas_call(
        functools.partial(gather_kernel, n, width),
        out_shape=jax.ShapeDtypeStruct((n,) + own.shape, own.dtype),
        in_specs=[vmem],
        out_specs=vmem,
        scratch_shapes=[pltpu.SemaphoreType.DMA] * 3,
        compiler_params=pltpu.CompilerParams(collective_id=0, has_side_effects=True),
        name="gather_points",
    )(own)


def reduce_kernel(n, width, part_ref, out_ref, got_ref, send_sem, recv_sem, send2_sem, recv2_sem):
    me = here(width)
    greet(n, width, me)
    spread(
        n,
        width,
        me,
        lambda peer, i: part_ref.at[peer],
        lambda peer, i: got_ref.at[i - 1],
        send_sem,
        recv_sem,
    )
    drain(got_ref, recv_sem)
    total = lax.fori_loop(0, n - 1, lambda i, acc: acc + got_ref[i], part_ref[me])
    out_ref[me] = total
    spread(
        n,
        width,
        me,
        lambda peer, i: out_ref.at[me],
        lambda peer, i: out_ref.at[me],
        send2_sem,
        recv2_sem,
    )
    drain(got_ref, send_sem)
    drain(got_ref, recv2_sem)
    drain(got_ref, send2_sem)


def reduce_all(part, n, width):
    vmem = pl.BlockSpec(memory_space=pltpu.VMEM)
    pieces = part.reshape(n, part.shape[0] // n, part.shape[1])
    summed = pl.pallas_call(
        functools.partial(reduce_kernel, n, width),
        out_shape=jax.ShapeDtypeStruct(pieces.shape, pieces.dtype),
        in_specs=[vmem],
        out_specs=vmem,
        scratch_shapes=[pltpu.VMEM((n - 1,) + pieces.shape[1:], pieces.dtype)]
        + [pltpu.SemaphoreType.DMA] * 4,
        compiler_params=pltpu.CompilerParams(collective_id=1, has_side_effects=True),
        name="sum_gram",
    )(pieces)
    return summed.reshape(part.shape)


def cg_kernel(
    n,
    width,
    owners,
    tile_ref,
    rhs_ref,
    wide_ref,
    inverse_ref,
    sol_ref,
    res_ref,
    dirs,
    put,
    got,
    ans,
    kept_proj,
    kept_squares,
    kept_rz,
    dir_send,
    dir_recv,
    put_send,
    put_recv,
    ans_send,
    ans_recv,
):
    me = here(width)
    rhs_count, row_count = rhs_ref.shape
    per = rhs_count // owners
    order = wide_ref.shape[1]
    lanes = order // LANES
    all_own = owners == n
    greet(n, width, me)

    def only_owners(body):
        if all_own:
            body()
        else:
            pl.when(me < owners)(body)

    def wide_sum(values):
        return jnp.broadcast_to(jnp.sum(values, axis=1, keepdims=True), (values.shape[0], LANES))

    def to_owners(k, proj, sums):
        for q in range(lanes):
            put[k, :, q, :] = proj[:, q * LANES : (q + 1) * LANES]
        for s, value in enumerate(sums):
            put[k, :, lanes + s, :] = value

        def push(i, carry):
            peer = lax.rem(me + i, owners)

            def go():
                pltpu.make_async_remote_copy(
                    src_ref=put.at[k, pl.ds(peer * per, per)],
                    dst_ref=got.at[k, lax.rem(me - peer + n, n) - 1],
                    send_sem=put_send.at[k],
                    recv_sem=put_recv.at[k],
                    device_id=coords(peer, width),
                    device_id_type=MESH,
                ).start()

            if all_own:
                go()
            else:
                pl.when(peer != me)(go)
            return carry

        lax.fori_loop(1 if all_own else 0, owners, push, 0)

    def finish_put(k):
        if all_own:
            drain(put.at[k, pl.ds(0, (owners - 1) * per)], put_send.at[k])
        else:

            @pl.when(me < owners)
            def _():
                drain(put.at[k, pl.ds(0, (owners - 1) * per)], put_send.at[k])

            @pl.when(me >= owners)
            def _():
                drain(put.at[k], put_send.at[k])

    def collect(k):
        drain(got.at[k], put_recv.at[k])
        start = put[k, pl.ds(me * per, per)]
        return lax.fori_loop(0, n - 1, lambda i, acc: acc + got[k, i], start)

    def answer(k, rows):
        for s, value in enumerate(rows):
            ans[k, pl.ds(me * per, per), s, :] = value
        spread(
            n,
            width,
            me,
            lambda peer, i: ans.at[k, pl.ds(me * per, per)],
            lambda peer, i: ans.at[k, pl.ds(me * per, per)],
            ans_send.at[k],
            ans_recv.at[k],
        )

    def await_answer(k):
        if all_own:
            drain(ans.at[k, pl.ds(0, (owners - 1) * per)], ans_recv.at[k])
        else:

            @pl.when(me < owners)
            def _():
                drain(ans.at[k, pl.ds(0, (owners - 1) * per)], ans_recv.at[k])

            @pl.when(me >= owners)
            def _():
                drain(ans.at[k], ans_recv.at[k])

    def finish_answer(k):
        def body():
            def one(i, carry):
                drain(ans.at[k, pl.ds(0, per)], ans_send.at[k])
                return carry

            lax.fori_loop(1, n, one, 0)

        only_owners(body)

    def solve(proj):
        half = lax.dot_general(
            proj,
            inverse_ref[...],
            (((1,), (1,)), ((), ())),
            precision=highest,
            preferred_element_type=jnp.float32,
        )
        coef = jnp.dot(
            half, inverse_ref[...], precision=highest, preferred_element_type=jnp.float32
        )
        return coef, wide_sum(half * half)

    def split(row):
        return [row[:, q * LANES : (q + 1) * LANES] for q in range(lanes)]

    def project(rows):
        return jnp.dot(rows, wide_ref[...], precision=highest, preferred_element_type=jnp.float32)

    def joined(packed):
        return jnp.concatenate([packed[:, q, :] for q in range(lanes)], axis=1)

    def precondition(residual, k):
        packed = ans[k]
        back = lax.dot_general(
            joined(packed),
            wide_ref[...],
            (((1,), (1,)), ((), ())),
            precision=highest,
            preferred_element_type=jnp.float32,
        )
        return (residual - back) * (1.0 / noise_level)

    residual = rhs_ref[...]
    solution = jnp.zeros_like(residual)
    to_owners(0, project(residual), [wide_sum(residual * residual)])

    def first_answer():
        total = collect(0)
        proj = joined(total)
        squares = total[:, lanes, :]
        coef, covered = solve(proj)
        kept_proj[...] = proj
        kept_squares[...] = squares
        kept_rz[...] = (squares - covered) * (1.0 / noise_level)
        answer(0, split(coef))

    def later_answer(k, last):
        total = collect(k)
        rz_before = kept_rz[...]
        size = rz_before / total[:, lanes, :]
        if last:
            answer(k, [size] * (lanes + 2))
            return
        along, image_squares = total[:, lanes + 1, :], total[:, lanes + 2, :]
        size_row = jnp.concatenate([size] * lanes, axis=1)
        proj = kept_proj[...] - size_row * joined(total)
        squares = kept_squares[...] - 2.0 * size * along + size * size * image_squares
        coef, covered = solve(proj)
        rz = (squares - covered) * (1.0 / noise_level)
        kept_proj[...] = proj
        kept_squares[...] = squares
        kept_rz[...] = rz
        answer(k, split(coef) + [size, rz / rz_before])

    only_owners(first_answer)
    await_answer(0)
    direction = precondition(residual, 0)

    for step_index in range(ITERS):
        last = step_index + 1 == ITERS
        dirs[step_index, me] = direction
        spread(
            n,
            width,
            me,
            lambda peer, i: dirs.at[step_index, me],
            lambda peer, i: dirs.at[step_index, me],
            dir_send.at[step_index],
            dir_recv.at[step_index],
        )
        drain(dirs.at[step_index, pl.ds(0, n - 1)], dir_recv.at[step_index])

        def multiply(j, acc):
            return acc + jnp.dot(
                dirs[step_index, j],
                tile_ref[j],
                precision=highest,
                preferred_element_type=jnp.float32,
            )

        image = lax.fori_loop(0, n, multiply, noise_level * direction, unroll=4)
        k = step_index + 1
        sums = [wide_sum(direction * image)]
        if last:
            to_owners(k, jnp.zeros((rhs_count, order), jnp.float32), sums)
        else:
            to_owners(
                k, project(image), sums + [wide_sum(residual * image), wide_sum(image * image)]
            )
        only_owners(functools.partial(later_answer, k, last))
        await_answer(k)
        size = ans[k, :, lanes, :]
        solution = solution + size * direction
        residual = residual - size * image
        if not last:
            direction = precondition(residual, k) + ans[k, :, lanes + 1, :] * direction
    sol_ref[...] = solution
    res_ref[...] = residual
    for step_index in range(ITERS):
        drain(dirs.at[step_index, pl.ds(0, n - 1)], dir_send.at[step_index])
    for k in range(ITERS + 1):
        finish_put(k)
        finish_answer(k)


def solve_cg(tile, targets_t, wide_factor, inverse, n, width):
    rhs_count, row_count = targets_t.shape
    owners = min(n, rhs_count)
    per = rhs_count // owners
    order = wide_factor.shape[1]
    rows = -(-(order // LANES + 3) // 8) * 8
    vmem = pl.BlockSpec(memory_space=pltpu.VMEM)
    f32 = jnp.float32
    return pl.pallas_call(
        functools.partial(cg_kernel, n, width, owners),
        out_shape=[jax.ShapeDtypeStruct((rhs_count, row_count), f32)] * 2,
        in_specs=[vmem] * 4,
        out_specs=[vmem] * 2,
        scratch_shapes=[
            pltpu.VMEM((ITERS, n, rhs_count, row_count), f32),
            pltpu.VMEM((ITERS + 1, rhs_count, rows, LANES), f32),
            pltpu.VMEM((ITERS + 1, n - 1, per, rows, LANES), f32),
            pltpu.VMEM((ITERS + 1, rhs_count, rows, LANES), f32),
            pltpu.VMEM((per, order), f32),
            pltpu.VMEM((per, LANES), f32),
            pltpu.VMEM((per, LANES), f32),
            pltpu.SemaphoreType.DMA((ITERS,)),
            pltpu.SemaphoreType.DMA((ITERS,)),
        ]
        + [pltpu.SemaphoreType.DMA((ITERS + 1,))] * 4,
        compiler_params=pltpu.CompilerParams(collective_id=2, has_side_effects=True),
        name="conjugate_gradients",
    )(tile.reshape(n, row_count, row_count), targets_t, wide_factor, inverse)


def per_device(n, width, points, targets, pivots):
    piv_count = pivots.shape[1]
    all_points = gather_all(points, n, width)
    all_points = all_points.reshape(-1, points.shape[1])
    picked = all_points[pivots.reshape(-1)]
    wide_factor = build_factor(points, picked)
    factor = wide_factor.astype(jnp.bfloat16)
    local_gram = lax.dot_general(
        wide_factor, wide_factor, (((0,), (0,)), ((), ())), precision=highest
    )
    order = 2 * piv_count
    gram = unpack_upper(reduce_all(pack_upper(local_gram), n, width), order)
    inverse = chol_inverse(gram + noise_level * jnp.eye(order, dtype=jnp.float32))
    tile = kernel_block(all_points, squared_norms(all_points), points, squared_norms(points))
    solution_t, residual_t = solve_cg(tile, targets.T, wide_factor, inverse, n, width)
    return (factor, solution_t.T, residual_t.T)


def solution(mesh):
    n, width = mesh.size, mesh.shape["col"]
    return jax.shard_map(
        functools.partial(per_device, n, width),
        mesh=mesh,
        in_specs=(P(("blk", "col"), None), P(("blk", "col"), None), P()),
        out_specs=(P(("blk", "col"), None), P(("blk", "col"), None), P(("blk", "col"), None)),
        check_vma=False,
    )
```

```python
import functools

import jax
import jax.numpy as jnp
from jax import lax
from jax.experimental import pallas as pl
from jax.experimental.pallas import tpu as pltpu
from jax.sharding import PartitionSpec as P

FEATURES = 128
ITERS = 3
LANES = 128


noise_level = 0.5
jitter_level = 0.05
highest = lax.Precision.HIGHEST
MESH = pl.DeviceIdType.MESH


def dot_t(left, right):
    return lax.dot_general(
        left,
        right,
        (((1,), (1,)), ((), ())),
        precision=highest,
        preferred_element_type=jnp.float32,
    )


def column_norms(point_rows):
    wide_rows = point_rows.astype(jnp.float32)
    return jnp.sum(wide_rows * wide_rows, axis=1, keepdims=True)


def row_norms(point_rows):
    wide_rows = point_rows.astype(jnp.float32)
    return dot_t(jnp.ones((8, wide_rows.shape[1]), jnp.float32), wide_rows * wide_rows)[0:1]


def kernel_block(left_rows, left_norms, right_rows, right_norms):
    inner = lax.dot_general(
        left_rows, right_rows, (((1,), (1,)), ((), ())), preferred_element_type=jnp.float32
    )
    distance = left_norms + right_norms - 2.0 * inner
    return jnp.exp(-2.0 * distance / FEATURES)


def lower_inverse_rows(rows):
    count = len(rows)
    lane = lax.broadcasted_iota(jnp.int32, (8, LANES), 1)
    sub = lax.broadcasted_iota(jnp.int32, (8, LANES), 0)

    def full_of(values):
        return jnp.broadcast_to(values, (8, LANES))

    rows = list(rows)
    done = []
    for p in range(count):
        base = 8 * p
        inside = (lane >= base) & (lane < base + 8)
        cols = [full_of(rows[p][:, base + c : base + c + 1]) for c in range(8)]
        forward = jnp.where(inside, jnp.where(lane == sub + base, 1.0, 0.0), rows[p])
        pivots = jnp.ones((8, LANES), jnp.float32)
        recips, spread_rows, coefs = [], [], []
        for j in range(8):
            pivot = full_of(cols[j][j : j + 1])
            recip = 1.0 / pivot
            pivots = jnp.where(sub == j, pivot, pivots)
            below = jnp.where(sub > j, cols[j] * recip, 0.0)
            spread_row = full_of(forward[j : j + 1])
            forward = forward - below * spread_row
            coef = {c: full_of(cols[c][j : j + 1]) for c in range(j + 1, 8)}
            for c in range(j + 1, 8):
                cols[c] = cols[c] - below * coef[c]
            recips.append(recip)
            spread_rows.append(spread_row)
            coefs.append(coef)
        done.append(jnp.where(lane <= sub + base, forward, 0.0) * lax.rsqrt(pivots))
        for v in range(p + 1, count):
            own = [full_of(rows[v][:, base + c : base + c + 1]) for c in range(8)]
            new = jnp.where(inside, 0.0, rows[v])
            for j in range(8):
                multiplier = own[j] * recips[j]
                new = new - multiplier * spread_rows[j]
                for c in range(j + 1, 8):
                    own[c] = own[c] - multiplier * coefs[j][c]
            rows[v] = new
    return done


def invert_lower(work, out_ref):
    order = work.shape[0]
    blocks = order // LANES
    row_at = lax.broadcasted_iota(jnp.int32, (LANES, LANES), 0)
    col_at = lax.broadcasted_iota(jnp.int32, (LANES, LANES), 1)
    lane_at = lax.broadcasted_iota(jnp.int32, (LANES, order), 1)

    def one_block(j, carry):
        at = pl.multiple_of(j * LANES, LANES)
        here_rows = pl.ds(at, LANES)
        inverse = jnp.concatenate(
            lower_inverse_rows(
                [work[pl.ds(at + 8 * v, 8), pl.ds(at, LANES)] for v in range(LANES // 8)]
            ),
            axis=0,
        )
        work[here_rows, pl.ds(at, LANES)] = jnp.where(row_at == col_at, 1.0, 0.0)
        side = jnp.dot(
            inverse, work[here_rows, :], precision=highest, preferred_element_type=jnp.float32
        )
        out_ref[here_rows, :] = jnp.where(lane_at < at + LANES, side, 0.0)
        work[here_rows, :] = side

        def below(i, inner):
            to = pl.multiple_of(i * LANES, LANES)
            rows = work[pl.ds(to, LANES), :]
            rows = jnp.where((lane_at >= at) & (lane_at < at + LANES), 0.0, rows)
            work[pl.ds(to, LANES), :] = rows - lax.dot_general(
                work[here_rows, pl.ds(to, LANES)],
                side,
                (((0,), (0,)), ((), ())),
                precision=highest,
                preferred_element_type=jnp.float32,
            )
            return inner

        lax.fori_loop(j + 1, blocks, below, 0)
        return carry

    lax.fori_loop(0, blocks, one_block, 0)


def shifted(matrix, level):
    row_at = lax.broadcasted_iota(jnp.int32, matrix.shape, 0)
    col_at = lax.broadcasted_iota(jnp.int32, matrix.shape, 1)
    return matrix + jnp.where(row_at == col_at, level, 0.0)


def pivot_kernel(picked_ref, out_ref, work):
    picked = picked_ref[...]
    work[...] = shifted(
        kernel_block(picked, column_norms(picked), picked, row_norms(picked)), jitter_level
    )
    invert_lower(work, out_ref)


def gram_kernel(gram_ref, out_ref, work):
    work[...] = shifted(gram_ref[...], noise_level)
    invert_lower(work, out_ref)


def chol_inverse(kernel, operand, order, name):
    vmem = pl.BlockSpec(memory_space=pltpu.VMEM)
    return pl.pallas_call(
        kernel,
        out_shape=jax.ShapeDtypeStruct((order, order), jnp.float32),
        in_specs=[vmem],
        out_specs=vmem,
        scratch_shapes=[pltpu.VMEM((order, order), jnp.float32)],
        name=name,
    )(operand)


def here(width):
    return lax.axis_index("blk") * width + lax.axis_index("col")


def coords(index, width):
    return (lax.div(index, width), lax.rem(index, width))


def greet(n, width, me):
    barrier = pltpu.get_barrier_semaphore()

    def hello(i, carry):
        peer = lax.rem(me + i, n)
        pl.semaphore_signal(
            barrier, inc=1, device_id=coords(peer, width), device_id_type=MESH
        )
        return carry

    lax.fori_loop(1, n, hello, 0)
    pl.semaphore_wait(barrier, n - 1)


def spread(n, width, me, src, dst, send_sem, recv_sem):
    def push(i, carry):
        peer = lax.rem(me + i, n)
        pltpu.make_async_remote_copy(
            src_ref=src(peer, i),
            dst_ref=dst(peer, i),
            send_sem=send_sem,
            recv_sem=recv_sem,
            device_id=coords(peer, width),
            device_id_type=MESH,
        ).start()
        return carry

    lax.fori_loop(1, n, push, 0)


def drain(ref, sem):
    pltpu.make_async_copy(ref, ref, sem).wait()


def flip(index, bits):
    moved = index
    weight = 1
    while weight <= bits:
        if bits & weight:
            moved = moved + weight * (1 - 2 * lax.rem(lax.div(index, weight), 2))
        weight *= 2
    return moved


class Relay:
    def __init__(self, n, width, me, blocks, own, send_sem, recv_sems, pair_sem):
        self.n, self.width, self.me = n, width, me
        self.blocks, self.own = blocks, own
        self.send_sem, self.recv_sems, self.pair_sem = send_sem, recv_sems, pair_sem
        self.plane = 2 * width
        self.lines = n // self.plane

    def send(self, src_ref, source, peer, recv_sem):
        pltpu.make_async_remote_copy(
            src_ref=src_ref,
            dst_ref=self.blocks.at[source],
            send_sem=self.send_sem,
            recv_sem=recv_sem,
            device_id=coords(peer, self.width),
            device_id_type=MESH,
        ).start()

    def fan(self, src_ref, source, i):
        for q in range(2, self.plane, 2):
            sem = self.recv_sems.at[self.lines * (q // 2) + i]
            self.send(src_ref, source, flip(self.me, q), sem)
        self.send(src_ref, source, flip(self.me, 1), self.pair_sem)

    def start(self):
        def along(i, carry):
            peer = lax.rem(self.me + self.plane * i, self.n)
            self.send(self.own, self.me, peer, self.recv_sems.at[i])
            return carry

        lax.fori_loop(1, self.lines, along, 0)
        self.fan(self.own, self.me, 0)

    def relay_lines(self):
        def one(i, carry):
            source = lax.rem(self.me - self.plane * i + self.n, self.n)
            drain(self.blocks.at[source], self.recv_sems.at[i])
            self.fan(self.blocks.at[source], source, i)
            return carry

        lax.fori_loop(1, self.lines, one, 0)

    def relay_plane(self):
        for q in range(2, self.plane, 2):

            def one(i, carry, q=q):
                source = lax.rem(flip(self.me, q) - self.plane * i + self.n, self.n)
                ref = self.blocks.at[source]
                drain(ref, self.recv_sems.at[self.lines * (q // 2) + i])
                self.send(ref, source, flip(self.me, 1), self.pair_sem)
                return carry

            lax.fori_loop(0, self.lines, one, 0)

    def finish(self):
        drain(self.blocks.at[pl.ds(0, self.n // 2)], self.pair_sem)

    def finish_sends(self):
        drain(self.blocks.at[pl.ds(0, self.n - 1)], self.send_sem)


def gather_kernel(
    n, width, points_ref, targets_ref, all_points, all_targets, send_sem, recv_sems, pair_sem, own_sem
):
    me = here(width)
    keeps = [
        pltpu.make_async_copy(points_ref, all_points.at[me], own_sem.at[0]),
        pltpu.make_async_copy(targets_ref, all_targets.at[me], own_sem.at[1]),
    ]
    for keep in keeps:
        keep.start()
    greet(n, width, me)
    relays = [
        Relay(n, width, me, blocks, own, send_sem.at[k], recv_sems.at[k], pair_sem.at[k])
        for k, (blocks, own) in enumerate([(all_points, points_ref), (all_targets, targets_ref)])
    ]
    for relay in relays:
        relay.start()
    for relay in relays:
        relay.relay_lines()
    for relay in relays:
        relay.relay_plane()
    for relay in relays:
        relay.finish()
    for relay in relays:
        relay.finish_sends()
    for keep in keeps:
        keep.wait()


def gather_all(points, targets_t, n, width):
    vmem = pl.BlockSpec(memory_space=pltpu.VMEM)
    return pl.pallas_call(
        functools.partial(gather_kernel, n, width),
        out_shape=[jax.ShapeDtypeStruct((n,) + v.shape, v.dtype) for v in (points, targets_t)],
        in_specs=[vmem] * 2,
        out_specs=[vmem] * 2,
        scratch_shapes=[
            pltpu.SemaphoreType.DMA((2,)),
            pltpu.SemaphoreType.DMA((2, n // 2)),
            pltpu.SemaphoreType.DMA((2,)),
            pltpu.SemaphoreType.DMA((2,)),
        ],
        compiler_params=pltpu.CompilerParams(collective_id=0, has_side_effects=True),
        name="gather_points",
    )(points, targets_t)


def sweep_kernel(
    n,
    width,
    points_ref,
    targets_ref,
    picked_ref,
    inverse_ref,
    factor_ref,
    wide_ref,
    tile_ref,
    gram_ref,
    proj_ref,
    zed_ref,
    image_ref,
    square_ref,
    gram_part,
    proj_part,
    zed_part,
    gram_got,
    proj_got,
    zed_got,
    send_sem,
    recv_sem,
):
    me = here(width)
    core, pair = lax.rem(me, 2), lax.div(me, 2)
    other = 1 - core
    partner = flip(me, 1)
    barrier = pltpu.get_barrier_semaphore()
    pl.semaphore_signal(barrier, inc=1, device_id=coords(partner, width), device_id_type=MESH)
    order = inverse_ref.shape[0]
    half = order // 2
    chunk = min(4, n // 2)
    picked = picked_ref[...]
    picked_column = column_norms(picked)
    own = points_ref[pair, core]
    beside = points_ref[pair, other]
    own_column, beside_column = column_norms(own), column_norms(beside)
    own_cross = kernel_block(own, own_column, picked, row_norms(picked))
    wide = jnp.concatenate(
        [
            dot_t(own_cross[:, :half], inverse_ref[:half, :half]),
            dot_t(own_cross, inverse_ref[half:, :]),
        ],
        axis=1,
    )
    wide_ref[...] = wide
    factor_ref[...] = wide.astype(jnp.bfloat16)
    own_targets = targets_ref[pair, core]
    image_ref[...] = noise_level * own_targets
    square_ref[...] = jnp.zeros_like(square_ref)
    zed_ref[...] = noise_level * wide
    for ref in (gram_part, proj_part, zed_part):
        ref[...] = jnp.zeros_like(ref)

    def step(i, carry):
        at = i * chunk
        near = jnp.concatenate([points_ref[at + t, core] for t in range(chunk)], axis=0)
        far = jnp.concatenate([points_ref[at + t, other] for t in range(chunk)], axis=0)
        near_targets = jnp.concatenate([targets_ref[at + t, core] for t in range(chunk)], axis=1)
        far_targets = jnp.concatenate([targets_ref[at + t, other] for t in range(chunk)], axis=1)
        near_row, far_row = row_norms(near), row_norms(far)
        cross = kernel_block(picked, picked_column, near, near_row)
        own_near = kernel_block(own, own_column, near, near_row)
        own_far = kernel_block(own, own_column, far, far_row)
        beside_near = kernel_block(beside, beside_column, near, near_row)
        size = own.shape[0]
        for t in range(chunk):
            tile_ref[at + t, core] = own_near[:, t * size : (t + 1) * size]
            tile_ref[at + t, other] = own_far[:, t * size : (t + 1) * size]
        top = jnp.dot(
            inverse_ref[:half, :half],
            cross[:half],
            precision=highest,
            preferred_element_type=jnp.float32,
        )
        low = jnp.dot(
            inverse_ref[half:, :], cross, precision=highest, preferred_element_type=jnp.float32
        )
        both = jnp.concatenate([top, low], axis=0)
        gram_part[:half, :] += dot_t(top, both)
        gram_part[half:, half:] += dot_t(low, low)
        proj_part[...] += dot_t(near_targets, both)
        zed_ref[...] += dot_t(own_near, both)
        zed_part[...] += dot_t(beside_near, both)
        image_ref[...] += dot_t(near_targets, own_near) + dot_t(far_targets, own_far)
        squares = near_targets * near_targets + far_targets * far_targets
        for t in range(chunk):
            square_ref[...] += squares[:, t * size : (t + 1) * size]
        return carry

    lax.fori_loop(0, n // 2 // chunk, step, 0)
    pl.semaphore_wait(barrier, 1)
    copies = []
    for k, (src, dst) in enumerate(
        [
            (gram_part.at[:half, :], gram_got.at[:half, :]),
            (gram_part.at[half:, half:], gram_got.at[half:, half:]),
            (proj_part, proj_got),
            (zed_part, zed_got),
        ]
    ):
        copy = pltpu.make_async_remote_copy(
            src_ref=src,
            dst_ref=dst,
            send_sem=send_sem.at[k],
            recv_sem=recv_sem.at[k],
            device_id=coords(partner, width),
            device_id_type=MESH,
        )
        copy.start()
        copies.append(copy)
    square_ref[...] = jnp.broadcast_to(
        jnp.sum(square_ref[...], axis=1, keepdims=True), square_ref.shape
    )
    gram_ref[half:, :half] = jnp.zeros((order - half, half), jnp.float32)
    copies[0].wait_recv()
    gram_ref[:half, :] = gram_part[:half, :] + gram_got[:half, :]
    copies[1].wait_recv()
    gram_ref[half:, half:] = gram_part[half:, half:] + gram_got[half:, half:]
    copies[2].wait_recv()
    proj_ref[...] = proj_part[...] + proj_got[...]
    copies[3].wait_recv()
    zed_ref[...] += zed_got[...]
    for copy in copies:
        copy.wait_send()


def sweep(all_points, all_targets, picked, inverse, n, width):
    rows, rhs_count, order = all_points.shape[1], all_targets.shape[1], picked.shape[0]
    vmem = pl.BlockSpec(memory_space=pltpu.VMEM)
    f32 = jnp.float32
    partial = [
        pltpu.VMEM((order, order), f32),
        pltpu.VMEM((rhs_count, order), f32),
        pltpu.VMEM((rows, order), f32),
    ]
    factor, wide, tile, *rest = pl.pallas_call(
        functools.partial(sweep_kernel, n, width),
        out_shape=[
            jax.ShapeDtypeStruct(shape, dtype)
            for shape, dtype in [
                ((rows, order), jnp.bfloat16),
                ((rows, order), f32),
                ((n // 2, 2, rows, rows), f32),
                ((order, order), f32),
                ((rhs_count, order), f32),
                ((rows, order), f32),
                ((rhs_count, rows), f32),
                ((rhs_count, rows), f32),
            ]
        ],
        in_specs=[vmem] * 4,
        out_specs=[vmem] * 8,
        scratch_shapes=partial * 2 + [pltpu.SemaphoreType.DMA((4,))] * 2,
        compiler_params=pltpu.CompilerParams(
            collective_id=1, has_side_effects=True, vmem_limit_bytes=60 * 2**20
        ),
        name="sweep_points",
    )(
        all_points.reshape((n // 2, 2) + all_points.shape[1:]),
        all_targets.reshape((n // 2, 2) + all_targets.shape[1:]),
        picked,
        inverse,
    )
    return [factor, wide, tile.reshape(n, rows, rows)] + rest


def cg_kernel(
    n,
    width,
    owners,
    tile_ref,
    rhs_ref,
    wide_ref,
    zed_ref,
    inverse_ref,
    proj_ref,
    image_ref,
    square_ref,
    sol_ref,
    res_ref,
    dirs,
    put,
    got,
    ans,
    kept_proj,
    kept_squares,
    kept_rz,
    all_rz,
    dir_send,
    dir_recv,
    dir_pair,
    put_send,
    put_recv,
    ans_send,
    ans_recv,
):
    me = here(width)
    rhs_count, row_count = rhs_ref.shape
    per = rhs_count // owners
    order = wide_ref.shape[1]
    lanes = order // LANES
    all_own = owners == n
    greet(n, width, me)

    def only_owners(body):
        if all_own:
            body()
        else:
            pl.when(me < owners)(body)

    def wide_sum(values):
        return jnp.broadcast_to(jnp.sum(values, axis=1, keepdims=True), (values.shape[0], LANES))

    def to_owners(k, proj, sums):
        for q in range(lanes):
            put[k, :, q, :] = proj[:, q * LANES : (q + 1) * LANES]
        for s, value in enumerate(sums):
            put[k, :, lanes + s, :] = value

        def push(i, carry):
            peer = lax.rem(me + i, owners)

            def go():
                pltpu.make_async_remote_copy(
                    src_ref=put.at[k, pl.ds(peer * per, per)],
                    dst_ref=got.at[k, lax.rem(me - peer + n, n) - 1],
                    send_sem=put_send.at[k],
                    recv_sem=put_recv.at[k],
                    device_id=coords(peer, width),
                    device_id_type=MESH,
                ).start()

            if all_own:
                go()
            else:
                pl.when(peer != me)(go)
            return carry

        lax.fori_loop(1 if all_own else 0, owners, push, 0)

    def finish_put(k):
        if all_own:
            drain(put.at[k, pl.ds(0, (owners - 1) * per)], put_send.at[k])
        else:

            @pl.when(me < owners)
            def _():
                drain(put.at[k, pl.ds(0, (owners - 1) * per)], put_send.at[k])

            @pl.when(me >= owners)
            def _():
                drain(put.at[k], put_send.at[k])

    def collect(k):
        drain(got.at[k], put_recv.at[k])
        start = put[k, pl.ds(me * per, per)]
        return lax.fori_loop(0, n - 1, lambda i, acc: acc + got[k, i], start)

    def answer(k, rows):
        for s, value in enumerate(rows):
            ans[k, pl.ds(me * per, per), s, :] = value
        spread(
            n,
            width,
            me,
            lambda peer, i: ans.at[k, pl.ds(me * per, per)],
            lambda peer, i: ans.at[k, pl.ds(me * per, per)],
            ans_send.at[k],
            ans_recv.at[k],
        )

    def await_answer(k):
        if all_own:
            drain(ans.at[k, pl.ds(0, (owners - 1) * per)], ans_recv.at[k])
        else:

            @pl.when(me < owners)
            def _():
                drain(ans.at[k, pl.ds(0, (owners - 1) * per)], ans_recv.at[k])

            @pl.when(me >= owners)
            def _():
                drain(ans.at[k], ans_recv.at[k])

    def finish_answer(k):
        def body():
            def one(i, carry):
                drain(ans.at[k, pl.ds(0, per)], ans_send.at[k])
                return carry

            lax.fori_loop(1, n, one, 0)

        only_owners(body)

    def solve(proj):
        half = dot_t(proj, inverse_ref[...])
        coef = jnp.dot(
            half, inverse_ref[...], precision=highest, preferred_element_type=jnp.float32
        )
        return coef, wide_sum(half * half)

    def split(row):
        return [row[:, q * LANES : (q + 1) * LANES] for q in range(lanes)]

    def project(rows):
        return jnp.dot(rows, wide_ref[...], precision=highest, preferred_element_type=jnp.float32)

    def joined(packed):
        return jnp.concatenate([packed[:, q, :] for q in range(lanes)], axis=1)

    def preconditioned(coef, residual, applied):
        direction = (residual - dot_t(coef, wide_ref[...])) * (1.0 / noise_level)
        image = (applied - dot_t(coef, zed_ref[...])) * (1.0 / noise_level)
        return direction, image

    def multiplied(k, image):
        def one(j, acc):
            return acc + dot_t(dirs[k, j], tile_ref[j])

        return lax.fori_loop(0, n, one, noise_level * image, unroll=4)

    residual = rhs_ref[...]
    applied = image_ref[...]
    solution = jnp.zeros_like(residual)
    coef, covered = solve(proj_ref[...])
    all_rz[...] = (square_ref[...] - covered) * (1.0 / noise_level)
    direction, image = preconditioned(coef, residual, applied)

    def keep_own():
        rows = pl.ds(me * per, per)
        kept_proj[...] = proj_ref[rows, :]
        kept_squares[...] = square_ref[rows, :]
        kept_rz[...] = all_rz[rows, :]

    only_owners(keep_own)

    def later_answer(k, last):
        total = collect(k)
        rz_before = kept_rz[...]
        size = rz_before / total[:, lanes, :]
        if last:
            answer(k, [size] * (lanes + 2))
            return
        along, image_squares = total[:, lanes + 1, :], total[:, lanes + 2, :]
        size_row = jnp.concatenate([size] * lanes, axis=1)
        proj = kept_proj[...] - size_row * joined(total)
        squares = kept_squares[...] - 2.0 * size * along + size * size * image_squares
        coef, covered = solve(proj)
        rz = (squares - covered) * (1.0 / noise_level)
        kept_proj[...] = proj
        kept_squares[...] = squares
        kept_rz[...] = rz
        answer(k, split(coef) + [size, rz / rz_before])

    relays = []
    for k in range(ITERS):
        last = k + 1 == ITERS
        sums = [wide_sum(direction * image)]
        if last:
            to_owners(k, jnp.zeros((rhs_count, order), jnp.float32), sums)
        else:
            dirs[k, me] = image
            relay = Relay(
                n,
                width,
                me,
                dirs.at[k],
                dirs.at[k, me],
                dir_send.at[k],
                dir_recv.at[k],
                dir_pair.at[k],
            )
            relays.append(relay)
            relay.start()
            to_owners(
                k, project(image), sums + [wide_sum(residual * image), wide_sum(image * image)]
            )
            relay.relay_lines()
        only_owners(functools.partial(later_answer, k, last))
        if not last:
            relay.relay_plane()
            relay.finish()
            twice = multiplied(k, image)
        await_answer(k)
        size = ans[k, :, lanes, :]
        solution = solution + size * direction
        residual = residual - size * image
        if not last:
            ratio = ans[k, :, lanes + 1, :]
            applied = applied - size * twice
            fresh, fresh_image = preconditioned(joined(ans[k]), residual, applied)
            direction = fresh + ratio * direction
            image = fresh_image + ratio * image
    sol_ref[...] = solution
    res_ref[...] = residual
    for relay in relays:
        relay.finish_sends()
    for k in range(ITERS):
        finish_put(k)
        finish_answer(k)


def solve_cg(tile, targets_t, wide_factor, zed, inverse, proj, image, squares, n, width):
    rhs_count, row_count = targets_t.shape
    owners = min(n, rhs_count)
    per = rhs_count // owners
    order = wide_factor.shape[1]
    rows = -(-(order // LANES + 3) // 8) * 8
    vmem = pl.BlockSpec(memory_space=pltpu.VMEM)
    f32 = jnp.float32
    return pl.pallas_call(
        functools.partial(cg_kernel, n, width, owners),
        out_shape=[jax.ShapeDtypeStruct((rhs_count, row_count), f32)] * 2,
        in_specs=[vmem] * 8,
        out_specs=[vmem] * 2,
        scratch_shapes=[
            pltpu.VMEM((ITERS - 1, n, rhs_count, row_count), f32),
            pltpu.VMEM((ITERS, rhs_count, rows, LANES), f32),
            pltpu.VMEM((ITERS, n - 1, per, rows, LANES), f32),
            pltpu.VMEM((ITERS, rhs_count, rows, LANES), f32),
            pltpu.VMEM((per, order), f32),
            pltpu.VMEM((per, LANES), f32),
            pltpu.VMEM((per, LANES), f32),
            pltpu.VMEM((rhs_count, LANES), f32),
            pltpu.SemaphoreType.DMA((ITERS - 1,)),
            pltpu.SemaphoreType.DMA((ITERS - 1, n // 2)),
            pltpu.SemaphoreType.DMA((ITERS - 1,)),
        ]
        + [pltpu.SemaphoreType.DMA((ITERS,))] * 4,
        compiler_params=pltpu.CompilerParams(
            collective_id=2, has_side_effects=True, vmem_limit_bytes=60 * 2**20
        ),
        name="conjugate_gradients",
    )(tile, targets_t, wide_factor, zed, inverse, proj, image, squares)


def per_device(n, width, points, targets, pivots):
    targets_t = targets.T
    all_points, all_targets = gather_all(points, targets_t, n, width)
    picked = all_points.reshape(-1, points.shape[1])[pivots.reshape(-1)]
    order = picked.shape[0]
    inverse = chol_inverse(pivot_kernel, picked, order, "pivot_inverse")
    factor, wide, tile, gram, proj, zed, image, squares = sweep(
        all_points, all_targets, picked, inverse, n, width
    )
    gram_inverse = chol_inverse(gram_kernel, gram, order, "gram_inverse")
    solution_t, residual_t = solve_cg(
        tile, targets_t, wide, zed, gram_inverse, proj, image, squares, n, width
    )
    return (factor, solution_t.T, residual_t.T)


def solution(mesh):
    n, width = mesh.size, mesh.shape["col"]
    return jax.shard_map(
        functools.partial(per_device, n, width),
        mesh=mesh,
        in_specs=(P(("blk", "col"), None), P(("blk", "col"), None), P()),
        out_specs=(P(("blk", "col"), None), P(("blk", "col"), None), P(("blk", "col"), None)),
        check_vma=False,
    )
```

```python
import functools

import jax
import jax.numpy as jnp
from jax import lax
from jax.experimental import pallas as pl
from jax.experimental.pallas import tpu as pltpu
from jax.sharding import PartitionSpec as P

FEATURES = 128
ITERS = 3
LANES = 128


noise_level = 0.5
jitter_level = 0.05
highest = lax.Precision.HIGHEST
MESH = pl.DeviceIdType.MESH


def dot_t(left, right):
    return lax.dot_general(
        left,
        right,
        (((1,), (1,)), ((), ())),
        precision=highest,
        preferred_element_type=jnp.float32,
    )


def column_norms(point_rows):
    wide_rows = point_rows.astype(jnp.float32)
    return jnp.sum(wide_rows * wide_rows, axis=1, keepdims=True)


def row_norms(point_rows):
    wide_rows = point_rows.astype(jnp.float32)
    return dot_t(jnp.ones((8, wide_rows.shape[1]), jnp.float32), wide_rows * wide_rows)[0:1]


def kernel_block(left_rows, left_norms, right_rows, right_norms):
    inner = lax.dot_general(
        left_rows, right_rows, (((1,), (1,)), ((), ())), preferred_element_type=jnp.float32
    )
    distance = left_norms + right_norms - 2.0 * inner
    return jnp.exp(-2.0 * distance / FEATURES)


def lower_inverse_rows(rows):
    count = len(rows)
    group = max(count // 2, 1)
    lane = lax.broadcasted_iota(jnp.int32, (8, LANES), 1)
    sub = lax.broadcasted_iota(jnp.int32, (8, LANES), 0)

    def full_of(values):
        return jnp.broadcast_to(values, (8, LANES))

    def columns(row, base):
        return [full_of(row[:, base + c : base + c + 1]) for c in range(8)]

    rows = list(rows)
    done = []
    for start in range(0, count, group):
        end = start + group
        whole = []
        ahead = columns(rows[start], 8 * start)
        for p in range(start, end):
            base = 8 * p
            inside = (lane >= base) & (lane < base + 8)
            cols = ahead
            forward = jnp.where(inside, jnp.where(lane == sub + base, 1.0, 0.0), rows[p])
            pivots = jnp.ones((8, LANES), jnp.float32)
            recips, spread_rows, coefs = [], [], []
            more = p + 1 < end
            if more:
                own = columns(rows[p + 1], base)
                ahead = columns(rows[p + 1], base + 8)
                following = jnp.where(inside, 0.0, rows[p + 1])
            for j in range(8):
                pivot = full_of(cols[j][j : j + 1])
                recip = 1.0 / pivot
                pivots = jnp.where(sub == j, pivot, pivots)
                below = jnp.where(sub > j, cols[j] * recip, 0.0)
                spread_row = full_of(forward[j : j + 1])
                forward = forward - below * spread_row
                coef = {c: full_of(cols[c][j : j + 1]) for c in range(j + 1, 8)}
                for c in range(j + 1, 8):
                    cols[c] = cols[c] - below * coef[c]
                if more:
                    multiplier = own[j] * recip
                    for c in range(j + 1, 8):
                        own[c] = own[c] - multiplier * coef[c]
                    for c in range(8):
                        ahead[c] = ahead[c] - multiplier * full_of(own[j][c : c + 1])
                    following = following - multiplier * spread_row
                recips.append(recip)
                spread_rows.append(spread_row)
                coefs.append(coef)
            scaled = forward * lax.rsqrt(pivots)
            lower = lane <= sub + base
            done.append(jnp.where(lower, scaled, 0.0))
            whole.append(jnp.where(lower | (lane >= 8 * end), scaled, 0.0))
            if more:
                rows[p + 1] = following
            for v in range(p + 2, end):
                own_v = columns(rows[v], base)
                new = jnp.where(inside, 0.0, rows[v])
                for j in range(8):
                    multiplier = own_v[j] * recips[j]
                    new = new - multiplier * spread_rows[j]
                    for c in range(j + 1, 8):
                        own_v[c] = own_v[c] - multiplier * coefs[j][c]
                rows[v] = new
        if end < count:
            side = jnp.concatenate(whole, axis=0)
            both = lax.dot_general(
                side,
                side,
                (((0,), (0,)), ((), ())),
                precision=highest,
                preferred_element_type=jnp.float32,
            )
            inside = (lane >= 8 * start) & (lane < 8 * end)
            for v in range(end, count):
                rows[v] = jnp.where(inside, 0.0, rows[v]) - both[8 * v : 8 * v + 8]
    return done


def invert_lower(work, out_ref):
    order = work.shape[0]
    blocks = order // LANES
    row_at = lax.broadcasted_iota(jnp.int32, (LANES, LANES), 0)
    col_at = lax.broadcasted_iota(jnp.int32, (LANES, LANES), 1)
    lane_at = lax.broadcasted_iota(jnp.int32, (LANES, order), 1)

    def one_block(j, carry):
        at = pl.multiple_of(j * LANES, LANES)
        here_rows = pl.ds(at, LANES)
        inverse = jnp.concatenate(
            lower_inverse_rows(
                [work[pl.ds(at + 8 * v, 8), pl.ds(at, LANES)] for v in range(LANES // 8)]
            ),
            axis=0,
        )
        work[here_rows, pl.ds(at, LANES)] = jnp.where(row_at == col_at, 1.0, 0.0)
        side = jnp.dot(
            inverse, work[here_rows, :], precision=highest, preferred_element_type=jnp.float32
        )
        out_ref[here_rows, :] = jnp.where(lane_at < at + LANES, side, 0.0)
        work[here_rows, :] = side

        def below(i, inner):
            to = pl.multiple_of(i * LANES, LANES)
            rows = work[pl.ds(to, LANES), :]
            rows = jnp.where((lane_at >= at) & (lane_at < at + LANES), 0.0, rows)
            work[pl.ds(to, LANES), :] = rows - lax.dot_general(
                work[here_rows, pl.ds(to, LANES)],
                side,
                (((0,), (0,)), ((), ())),
                precision=highest,
                preferred_element_type=jnp.float32,
            )
            return inner

        lax.fori_loop(j + 1, blocks, below, 0)
        return carry

    lax.fori_loop(0, blocks, one_block, 0)


def shifted(matrix, level):
    row_at = lax.broadcasted_iota(jnp.int32, matrix.shape, 0)
    col_at = lax.broadcasted_iota(jnp.int32, matrix.shape, 1)
    return matrix + jnp.where(row_at == col_at, level, 0.0)


def pivot_kernel(picked_ref, out_ref, work):
    picked = picked_ref[...]
    work[...] = shifted(
        kernel_block(picked, column_norms(picked), picked, row_norms(picked)), jitter_level
    )
    invert_lower(work, out_ref)


def gram_kernel(gram_ref, out_ref, work):
    work[...] = shifted(gram_ref[...], noise_level)
    invert_lower(work, out_ref)


def chol_inverse(kernel, operand, order, name):
    vmem = pl.BlockSpec(memory_space=pltpu.VMEM)
    return pl.pallas_call(
        kernel,
        out_shape=jax.ShapeDtypeStruct((order, order), jnp.float32),
        in_specs=[vmem],
        out_specs=vmem,
        scratch_shapes=[pltpu.VMEM((order, order), jnp.float32)],
        name=name,
    )(operand)


def here(width):
    return lax.axis_index("blk") * width + lax.axis_index("col")


def coords(index, width):
    return (lax.div(index, width), lax.rem(index, width))


def greet(n, width, me):
    barrier = pltpu.get_barrier_semaphore()

    def hello(i, carry):
        peer = lax.rem(me + i, n)
        pl.semaphore_signal(
            barrier, inc=1, device_id=coords(peer, width), device_id_type=MESH
        )
        return carry

    lax.fori_loop(1, n, hello, 0)
    pl.semaphore_wait(barrier, n - 1)


def spread(n, width, me, src, dst, send_sem, recv_sem):
    def push(i, carry):
        peer = lax.rem(me + i, n)
        pltpu.make_async_remote_copy(
            src_ref=src(peer, i),
            dst_ref=dst(peer, i),
            send_sem=send_sem,
            recv_sem=recv_sem,
            device_id=coords(peer, width),
            device_id_type=MESH,
        ).start()
        return carry

    lax.fori_loop(1, n, push, 0)


def drain(ref, sem):
    pltpu.make_async_copy(ref, ref, sem).wait()


def flip(index, bits):
    moved = index
    weight = 1
    while weight <= bits:
        if bits & weight:
            moved = moved + weight * (1 - 2 * lax.rem(lax.div(index, weight), 2))
        weight *= 2
    return moved


class Relay:
    def __init__(self, n, width, me, blocks, own, send_sem, recv_sems, pair_sem):
        self.n, self.width, self.me = n, width, me
        self.blocks, self.own = blocks, own
        self.send_sem, self.recv_sems, self.pair_sem = send_sem, recv_sems, pair_sem
        self.plane = 2 * width
        self.lines = n // self.plane

    def send(self, src_ref, source, peer, recv_sem):
        pltpu.make_async_remote_copy(
            src_ref=src_ref,
            dst_ref=self.blocks.at[source],
            send_sem=self.send_sem,
            recv_sem=recv_sem,
            device_id=coords(peer, self.width),
            device_id_type=MESH,
        ).start()

    def fan(self, src_ref, source, i):
        for q in range(2, self.plane, 2):
            sem = self.recv_sems.at[self.lines * (q // 2) + i]
            self.send(src_ref, source, flip(self.me, q), sem)
        self.send(src_ref, source, flip(self.me, 1), self.pair_sem)

    def start(self):
        def along(i, carry):
            peer = lax.rem(self.me + self.plane * i, self.n)
            self.send(self.own, self.me, peer, self.recv_sems.at[i])
            return carry

        lax.fori_loop(1, self.lines, along, 0)
        self.fan(self.own, self.me, 0)

    def relay_lines(self):
        def one(i, carry):
            source = lax.rem(self.me - self.plane * i + self.n, self.n)
            drain(self.blocks.at[source], self.recv_sems.at[i])
            self.fan(self.blocks.at[source], source, i)
            return carry

        lax.fori_loop(1, self.lines, one, 0)

    def relay_plane(self):
        for q in range(2, self.plane, 2):

            def one(i, carry, q=q):
                source = lax.rem(flip(self.me, q) - self.plane * i + self.n, self.n)
                ref = self.blocks.at[source]
                drain(ref, self.recv_sems.at[self.lines * (q // 2) + i])
                self.send(ref, source, flip(self.me, 1), self.pair_sem)
                return carry

            lax.fori_loop(0, self.lines, one, 0)

    def finish(self):
        drain(self.blocks.at[pl.ds(0, self.n // 2)], self.pair_sem)

    def finish_sends(self):
        drain(self.blocks.at[pl.ds(0, self.n - 1)], self.send_sem)


def gather_kernel(
    n, width, points_ref, targets_ref, all_points, all_targets, send_sem, recv_sems, pair_sem, own_sem
):
    me = here(width)
    keeps = [
        pltpu.make_async_copy(points_ref, all_points.at[me], own_sem.at[0]),
        pltpu.make_async_copy(targets_ref, all_targets.at[me], own_sem.at[1]),
    ]
    for keep in keeps:
        keep.start()
    greet(n, width, me)
    relays = [
        Relay(n, width, me, blocks, own, send_sem.at[k], recv_sems.at[k], pair_sem.at[k])
        for k, (blocks, own) in enumerate([(all_points, points_ref), (all_targets, targets_ref)])
    ]
    for relay in relays:
        relay.start()
    for relay in relays:
        relay.relay_lines()
    for relay in relays:
        relay.relay_plane()
    for relay in relays:
        relay.finish()
    for relay in relays:
        relay.finish_sends()
    for keep in keeps:
        keep.wait()


def gather_all(points, targets_t, n, width):
    vmem = pl.BlockSpec(memory_space=pltpu.VMEM)
    return pl.pallas_call(
        functools.partial(gather_kernel, n, width),
        out_shape=[jax.ShapeDtypeStruct((n,) + v.shape, v.dtype) for v in (points, targets_t)],
        in_specs=[vmem] * 2,
        out_specs=[vmem] * 2,
        scratch_shapes=[
            pltpu.SemaphoreType.DMA((2,)),
            pltpu.SemaphoreType.DMA((2, n // 2)),
            pltpu.SemaphoreType.DMA((2,)),
            pltpu.SemaphoreType.DMA((2,)),
        ],
        compiler_params=pltpu.CompilerParams(collective_id=0, has_side_effects=True),
        name="gather_points",
    )(points, targets_t)


def sweep_kernel(
    n,
    width,
    points_ref,
    targets_ref,
    picked_ref,
    inverse_ref,
    factor_ref,
    wide_ref,
    tile_ref,
    gram_ref,
    proj_ref,
    zed_ref,
    image_ref,
    square_ref,
    left_part,
    right_part,
    left_got,
    right_got,
    send_sem,
    recv_sem,
):
    me = here(width)
    core, pair = lax.rem(me, 2), lax.div(me, 2)
    other = 1 - core
    partner = flip(me, 1)
    barrier = pltpu.get_barrier_semaphore()
    pl.semaphore_signal(barrier, inc=1, device_id=coords(partner, width), device_id_type=MESH)
    order = inverse_ref.shape[0]
    half = order // 2
    chunk = min(4, n // 2)
    picked = picked_ref[...]
    picked_column = column_norms(picked)
    own = points_ref[pair, core]
    beside = points_ref[pair, other]
    own_column, beside_column = column_norms(own), column_norms(beside)
    own_cross = kernel_block(own, own_column, picked, row_norms(picked))
    wide = jnp.concatenate(
        [
            dot_t(own_cross[:, :half], inverse_ref[:half, :half]),
            dot_t(own_cross, inverse_ref[half:, :]),
        ],
        axis=1,
    )
    wide_ref[...] = wide
    factor_ref[...] = wide.astype(jnp.bfloat16)
    own_targets = targets_ref[pair, core]
    image_ref[...] = noise_level * own_targets
    square_ref[...] = jnp.zeros_like(square_ref)
    for ref in (left_part, right_part):
        ref[...] = jnp.zeros_like(ref)

    def step(i, carry):
        at = i * chunk
        near = jnp.concatenate([points_ref[at + t, core] for t in range(chunk)], axis=0)
        far = jnp.concatenate([points_ref[at + t, other] for t in range(chunk)], axis=0)
        near_targets = jnp.concatenate([targets_ref[at + t, core] for t in range(chunk)], axis=1)
        far_targets = jnp.concatenate([targets_ref[at + t, other] for t in range(chunk)], axis=1)
        near_row, far_row = row_norms(near), row_norms(far)
        cross = kernel_block(picked, picked_column, near, near_row)
        own_near = kernel_block(own, own_column, near, near_row)
        own_far = kernel_block(own, own_column, far, far_row)
        beside_near = kernel_block(beside, beside_column, near, near_row)
        size = own.shape[0]
        for t in range(chunk):
            tile_ref[at + t, core] = own_near[:, t * size : (t + 1) * size]
            tile_ref[at + t, other] = own_far[:, t * size : (t + 1) * size]
        first = jnp.dot(
            inverse_ref[:, :half],
            cross[:half],
            precision=highest,
            preferred_element_type=jnp.float32,
        )
        top = first[:half]
        low = first[half:] + jnp.dot(
            inverse_ref[half:, half:],
            cross[half:],
            precision=highest,
            preferred_element_type=jnp.float32,
        )
        extra = [own_near, beside_near, near_targets]
        left_part[...] += dot_t(jnp.concatenate([top] + extra, axis=0), top)
        right_part[...] += dot_t(jnp.concatenate([top, low] + extra, axis=0), low)
        image_ref[...] += dot_t(near_targets, own_near) + dot_t(far_targets, own_far)
        squares = near_targets * near_targets + far_targets * far_targets
        for t in range(chunk):
            square_ref[...] += squares[:, t * size : (t + 1) * size]
        return carry

    lax.fori_loop(0, n // 2 // chunk, step, 0)
    pl.semaphore_wait(barrier, 1)
    size = own.shape[0]
    sides = [(left_part, left_got, half, 0), (right_part, right_got, order, half)]
    copies = []
    for part, got, tall, _ in sides:
        for rows in (pl.ds(0, tall), pl.ds(tall + size, part.shape[0] - tall - size)):
            copy = pltpu.make_async_remote_copy(
                src_ref=part.at[rows],
                dst_ref=got.at[rows],
                send_sem=send_sem.at[len(copies)],
                recv_sem=recv_sem.at[len(copies)],
                device_id=coords(partner, width),
                device_id_type=MESH,
            )
            copy.start()
            copies.append(copy)
    square_ref[...] = jnp.broadcast_to(
        jnp.sum(square_ref[...], axis=1, keepdims=True), square_ref.shape
    )
    gram_ref[half:, :half] = jnp.zeros((order - half, half), jnp.float32)
    for copy in copies:
        copy.wait_recv()
    for part, got, tall, at in sides:
        lanes = slice(at, at + part.shape[1])
        gram_ref[:tall, lanes] = part[:tall] + got[:tall]
        zed_ref[:, lanes] = (
            noise_level * wide_ref[:, lanes]
            + part[tall : tall + size]
            + got[tall + size : tall + 2 * size]
        )
        proj_ref[:, lanes] = part[tall + 2 * size :] + got[tall + 2 * size :]
    for copy in copies:
        copy.wait_send()


def sweep(all_points, all_targets, picked, inverse, n, width):
    rows, rhs_count, order = all_points.shape[1], all_targets.shape[1], picked.shape[0]
    vmem = pl.BlockSpec(memory_space=pltpu.VMEM)
    f32 = jnp.float32
    half = order // 2
    extra = 2 * rows + rhs_count
    partial = [
        pltpu.VMEM((half + extra, half), f32),
        pltpu.VMEM((order + extra, order - half), f32),
    ]
    factor, wide, tile, *rest = pl.pallas_call(
        functools.partial(sweep_kernel, n, width),
        out_shape=[
            jax.ShapeDtypeStruct(shape, dtype)
            for shape, dtype in [
                ((rows, order), jnp.bfloat16),
                ((rows, order), f32),
                ((n // 2, 2, rows, rows), f32),
                ((order, order), f32),
                ((rhs_count, order), f32),
                ((rows, order), f32),
                ((rhs_count, rows), f32),
                ((rhs_count, rows), f32),
            ]
        ],
        in_specs=[vmem] * 4,
        out_specs=[vmem] * 8,
        scratch_shapes=partial * 2 + [pltpu.SemaphoreType.DMA((4,))] * 2,
        compiler_params=pltpu.CompilerParams(
            collective_id=1, has_side_effects=True, vmem_limit_bytes=60 * 2**20
        ),
        name="sweep_points",
    )(
        all_points.reshape((n // 2, 2) + all_points.shape[1:]),
        all_targets.reshape((n // 2, 2) + all_targets.shape[1:]),
        picked,
        inverse,
    )
    return [factor, wide, tile.reshape(n, rows, rows)] + rest


def cg_kernel(
    n,
    width,
    owners,
    tile_ref,
    rhs_ref,
    wide_ref,
    zed_ref,
    inverse_ref,
    proj_ref,
    image_ref,
    square_ref,
    sol_ref,
    res_ref,
    dirs,
    put,
    got,
    ans,
    kept_proj,
    kept_squares,
    kept_rz,
    all_rz,
    dir_send,
    dir_recv,
    dir_pair,
    put_send,
    put_recv,
    ans_send,
    ans_recv,
):
    me = here(width)
    rhs_count, row_count = rhs_ref.shape
    per = rhs_count // owners
    order = wide_ref.shape[1]
    lanes = order // LANES
    all_own = owners == n
    greet(n, width, me)

    def only_owners(body):
        if all_own:
            body()
        else:
            pl.when(me < owners)(body)

    def wide_sum(values):
        return jnp.broadcast_to(jnp.sum(values, axis=1, keepdims=True), (values.shape[0], LANES))

    def to_owners(k, proj, sums):
        for q in range(lanes):
            put[k, :, q, :] = proj[:, q * LANES : (q + 1) * LANES]
        for s, value in enumerate(sums):
            put[k, :, lanes + s, :] = value

        def push(i, carry):
            peer = lax.rem(me + i, owners)

            def go():
                pltpu.make_async_remote_copy(
                    src_ref=put.at[k, pl.ds(peer * per, per)],
                    dst_ref=got.at[k, lax.rem(me - peer + n, n) - 1],
                    send_sem=put_send.at[k],
                    recv_sem=put_recv.at[k],
                    device_id=coords(peer, width),
                    device_id_type=MESH,
                ).start()

            if all_own:
                go()
            else:
                pl.when(peer != me)(go)
            return carry

        lax.fori_loop(1 if all_own else 0, owners, push, 0)

    def finish_put(k):
        if all_own:
            drain(put.at[k, pl.ds(0, (owners - 1) * per)], put_send.at[k])
        else:

            @pl.when(me < owners)
            def _():
                drain(put.at[k, pl.ds(0, (owners - 1) * per)], put_send.at[k])

            @pl.when(me >= owners)
            def _():
                drain(put.at[k], put_send.at[k])

    def collect(k):
        drain(got.at[k], put_recv.at[k])
        start = put[k, pl.ds(me * per, per)]
        return lax.fori_loop(0, n - 1, lambda i, acc: acc + got[k, i], start)

    def answer(k, rows):
        for s, value in enumerate(rows):
            ans[k, pl.ds(me * per, per), s, :] = value
        spread(
            n,
            width,
            me,
            lambda peer, i: ans.at[k, pl.ds(me * per, per)],
            lambda peer, i: ans.at[k, pl.ds(me * per, per)],
            ans_send.at[k],
            ans_recv.at[k],
        )

    def await_answer(k):
        if all_own:
            drain(ans.at[k, pl.ds(0, (owners - 1) * per)], ans_recv.at[k])
        else:

            @pl.when(me < owners)
            def _():
                drain(ans.at[k, pl.ds(0, (owners - 1) * per)], ans_recv.at[k])

            @pl.when(me >= owners)
            def _():
                drain(ans.at[k], ans_recv.at[k])

    def finish_answer(k):
        def body():
            def one(i, carry):
                drain(ans.at[k, pl.ds(0, per)], ans_send.at[k])
                return carry

            lax.fori_loop(1, n, one, 0)

        only_owners(body)

    def solve(proj):
        half = dot_t(proj, inverse_ref[...])
        coef = jnp.dot(
            half, inverse_ref[...], precision=highest, preferred_element_type=jnp.float32
        )
        return coef, wide_sum(half * half)

    def split(row):
        return [row[:, q * LANES : (q + 1) * LANES] for q in range(lanes)]

    def project(rows):
        return jnp.dot(rows, wide_ref[...], precision=highest, preferred_element_type=jnp.float32)

    def joined(packed):
        return jnp.concatenate([packed[:, q, :] for q in range(lanes)], axis=1)

    def preconditioned(coef, residual, applied):
        direction = (residual - dot_t(coef, wide_ref[...])) * (1.0 / noise_level)
        image = (applied - dot_t(coef, zed_ref[...])) * (1.0 / noise_level)
        return direction, image

    def multiplied(k, image):
        def one(j, acc):
            return acc + dot_t(dirs[k, j], tile_ref[j])

        return lax.fori_loop(0, n, one, noise_level * image, unroll=4)

    residual = rhs_ref[...]
    applied = image_ref[...]
    solution = jnp.zeros_like(residual)
    coef, covered = solve(proj_ref[...])
    all_rz[...] = (square_ref[...] - covered) * (1.0 / noise_level)
    direction, image = preconditioned(coef, residual, applied)

    def keep_own():
        rows = pl.ds(me * per, per)
        kept_proj[...] = proj_ref[rows, :]
        kept_squares[...] = square_ref[rows, :]
        kept_rz[...] = all_rz[rows, :]

    only_owners(keep_own)

    def later_answer(k, last):
        total = collect(k)
        rz_before = kept_rz[...]
        size = rz_before / total[:, lanes, :]
        if last:
            answer(k, [size] * (lanes + 2))
            return
        along, image_squares = total[:, lanes + 1, :], total[:, lanes + 2, :]
        size_row = jnp.concatenate([size] * lanes, axis=1)
        proj = kept_proj[...] - size_row * joined(total)
        squares = kept_squares[...] - 2.0 * size * along + size * size * image_squares
        coef, covered = solve(proj)
        rz = (squares - covered) * (1.0 / noise_level)
        kept_proj[...] = proj
        kept_squares[...] = squares
        kept_rz[...] = rz
        answer(k, split(coef) + [size, rz / rz_before])

    relays = []
    for k in range(ITERS):
        last = k + 1 == ITERS
        sums = [wide_sum(direction * image)]
        if last:
            to_owners(k, jnp.zeros((rhs_count, order), jnp.float32), sums)
        else:
            dirs[k, me] = image
            relay = Relay(
                n,
                width,
                me,
                dirs.at[k],
                dirs.at[k, me],
                dir_send.at[k],
                dir_recv.at[k],
                dir_pair.at[k],
            )
            relays.append(relay)
            relay.start()
            to_owners(
                k, project(image), sums + [wide_sum(residual * image), wide_sum(image * image)]
            )
            relay.relay_lines()
        only_owners(functools.partial(later_answer, k, last))
        if not last:
            relay.relay_plane()
            relay.finish()
            twice = multiplied(k, image)
        await_answer(k)
        size = ans[k, :, lanes, :]
        solution = solution + size * direction
        residual = residual - size * image
        if not last:
            ratio = ans[k, :, lanes + 1, :]
            applied = applied - size * twice
            fresh, fresh_image = preconditioned(joined(ans[k]), residual, applied)
            direction = fresh + ratio * direction
            image = fresh_image + ratio * image
    sol_ref[...] = solution
    res_ref[...] = residual
    for relay in relays:
        relay.finish_sends()
    for k in range(ITERS):
        finish_put(k)
        finish_answer(k)


def solve_cg(tile, targets_t, wide_factor, zed, inverse, proj, image, squares, n, width):
    rhs_count, row_count = targets_t.shape
    owners = min(n, rhs_count)
    per = rhs_count // owners
    order = wide_factor.shape[1]
    rows = -(-(order // LANES + 3) // 8) * 8
    vmem = pl.BlockSpec(memory_space=pltpu.VMEM)
    f32 = jnp.float32
    return pl.pallas_call(
        functools.partial(cg_kernel, n, width, owners),
        out_shape=[jax.ShapeDtypeStruct((rhs_count, row_count), f32)] * 2,
        in_specs=[vmem] * 8,
        out_specs=[vmem] * 2,
        scratch_shapes=[
            pltpu.VMEM((ITERS - 1, n, rhs_count, row_count), f32),
            pltpu.VMEM((ITERS, rhs_count, rows, LANES), f32),
            pltpu.VMEM((ITERS, n - 1, per, rows, LANES), f32),
            pltpu.VMEM((ITERS, rhs_count, rows, LANES), f32),
            pltpu.VMEM((per, order), f32),
            pltpu.VMEM((per, LANES), f32),
            pltpu.VMEM((per, LANES), f32),
            pltpu.VMEM((rhs_count, LANES), f32),
            pltpu.SemaphoreType.DMA((ITERS - 1,)),
            pltpu.SemaphoreType.DMA((ITERS - 1, n // 2)),
            pltpu.SemaphoreType.DMA((ITERS - 1,)),
        ]
        + [pltpu.SemaphoreType.DMA((ITERS,))] * 4,
        compiler_params=pltpu.CompilerParams(
            collective_id=2, has_side_effects=True, vmem_limit_bytes=60 * 2**20
        ),
        name="conjugate_gradients",
    )(tile, targets_t, wide_factor, zed, inverse, proj, image, squares)


def per_device(n, width, points, targets, pivots):
    targets_t = targets.T
    all_points, all_targets = gather_all(points, targets_t, n, width)
    picked = all_points.reshape(-1, points.shape[1])[pivots.reshape(-1)]
    order = picked.shape[0]
    inverse = chol_inverse(pivot_kernel, picked, order, "pivot_inverse")
    factor, wide, tile, gram, proj, zed, image, squares = sweep(
        all_points, all_targets, picked, inverse, n, width
    )
    gram_inverse = chol_inverse(gram_kernel, gram, order, "gram_inverse")
    solution_t, residual_t = solve_cg(
        tile, targets_t, wide, zed, gram_inverse, proj, image, squares, n, width
    )
    return (factor, solution_t.T, residual_t.T)


def solution(mesh):
    n, width = mesh.size, mesh.shape["col"]
    return jax.shard_map(
        functools.partial(per_device, n, width),
        mesh=mesh,
        in_specs=(P(("blk", "col"), None), P(("blk", "col"), None), P()),
        out_specs=(P(("blk", "col"), None), P(("blk", "col"), None), P(("blk", "col"), None)),
        check_vma=False,
    )
```

```python
import functools

import jax
import jax.numpy as jnp
from jax import lax
from jax.experimental import pallas as pl
from jax.experimental.pallas import tpu as pltpu
from jax.sharding import PartitionSpec as P

FEATURES = 128
ITERS = 3
LANES = 128


noise_level = 0.5
jitter_level = 0.05
highest = lax.Precision.HIGHEST
MESH = pl.DeviceIdType.MESH


def dot_t(left, right):
    return lax.dot_general(
        left,
        right,
        (((1,), (1,)), ((), ())),
        precision=highest,
        preferred_element_type=jnp.float32,
    )


def column_norms(point_rows):
    wide_rows = point_rows.astype(jnp.float32)
    return jnp.sum(wide_rows * wide_rows, axis=1, keepdims=True)


def row_norms(point_rows):
    wide_rows = point_rows.astype(jnp.float32)
    return dot_t(jnp.ones((8, wide_rows.shape[1]), jnp.float32), wide_rows * wide_rows)[0:1]


def kernel_block(left_rows, left_norms, right_rows, right_norms):
    inner = lax.dot_general(
        left_rows, right_rows, (((1,), (1,)), ((), ())), preferred_element_type=jnp.float32
    )
    distance = left_norms + right_norms - 2.0 * inner
    return jnp.exp(-2.0 * distance / FEATURES)


def lower_inverse_rows(rows):
    count = len(rows)
    group = max(count // 2, 1)
    lane = lax.broadcasted_iota(jnp.int32, (8, LANES), 1)
    sub = lax.broadcasted_iota(jnp.int32, (8, LANES), 0)

    def full_of(values):
        return jnp.broadcast_to(values, (8, LANES))

    def columns(row, base):
        return [full_of(row[:, base + c : base + c + 1]) for c in range(8)]

    rows = list(rows)
    done = []
    for start in range(0, count, group):
        end = start + group
        whole = []
        ahead = columns(rows[start], 8 * start)
        for p in range(start, end):
            base = 8 * p
            inside = (lane >= base) & (lane < base + 8)
            cols = ahead
            forward = jnp.where(inside, jnp.where(lane == sub + base, 1.0, 0.0), rows[p])
            pivots = jnp.ones((8, LANES), jnp.float32)
            recips, spread_rows, coefs = [], [], []
            more = p + 1 < end
            if more:
                own = columns(rows[p + 1], base)
                ahead = columns(rows[p + 1], base + 8)
                following = jnp.where(inside, 0.0, rows[p + 1])
            for j in range(8):
                pivot = full_of(cols[j][j : j + 1])
                recip = 1.0 / pivot
                pivots = jnp.where(sub == j, pivot, pivots)
                below = jnp.where(sub > j, cols[j] * recip, 0.0)
                spread_row = full_of(forward[j : j + 1])
                forward = forward - below * spread_row
                coef = {c: full_of(cols[c][j : j + 1]) for c in range(j + 1, 8)}
                for c in range(j + 1, 8):
                    cols[c] = cols[c] - below * coef[c]
                if more:
                    multiplier = own[j] * recip
                    for c in range(j + 1, 8):
                        own[c] = own[c] - multiplier * coef[c]
                    for c in range(8):
                        ahead[c] = ahead[c] - multiplier * full_of(own[j][c : c + 1])
                    following = following - multiplier * spread_row
                recips.append(recip)
                spread_rows.append(spread_row)
                coefs.append(coef)
            scaled = forward * lax.rsqrt(pivots)
            lower = lane <= sub + base
            done.append(jnp.where(lower, scaled, 0.0))
            whole.append(jnp.where(lower | (lane >= 8 * end), scaled, 0.0))
            if more:
                rows[p + 1] = following
            for v in range(p + 2, end):
                own_v = columns(rows[v], base)
                new = jnp.where(inside, 0.0, rows[v])
                for j in range(8):
                    multiplier = own_v[j] * recips[j]
                    new = new - multiplier * spread_rows[j]
                    for c in range(j + 1, 8):
                        own_v[c] = own_v[c] - multiplier * coefs[j][c]
                rows[v] = new
        if end < count:
            side = jnp.concatenate(whole, axis=0)
            both = lax.dot_general(
                side,
                side,
                (((0,), (0,)), ((), ())),
                precision=highest,
                preferred_element_type=jnp.float32,
            )
            inside = (lane >= 8 * start) & (lane < 8 * end)
            for v in range(end, count):
                rows[v] = jnp.where(inside, 0.0, rows[v]) - both[8 * v : 8 * v + 8]
    return done


def invert_lower(work, out_ref, beside=None):
    order = work.shape[0]
    blocks = order // LANES
    row_at = lax.broadcasted_iota(jnp.int32, (LANES, LANES), 0)
    col_at = lax.broadcasted_iota(jnp.int32, (LANES, LANES), 1)
    lane_at = lax.broadcasted_iota(jnp.int32, (LANES, order), 1)

    def one_block(j, carry):
        at = pl.multiple_of(j * LANES, LANES)
        here_rows = pl.ds(at, LANES)
        inverse = jnp.concatenate(
            lower_inverse_rows(
                [work[pl.ds(at + 8 * v, 8), pl.ds(at, LANES)] for v in range(LANES // 8)]
            ),
            axis=0,
        )
        work[here_rows, pl.ds(at, LANES)] = jnp.where(row_at == col_at, 1.0, 0.0)
        side = jnp.dot(
            inverse, work[here_rows, :], precision=highest, preferred_element_type=jnp.float32
        )
        out_ref[here_rows, :] = jnp.where(lane_at < at + LANES, side, 0.0)
        work[here_rows, :] = side

        def below(i, inner):
            to = pl.multiple_of(i * LANES, LANES)
            rows = work[pl.ds(to, LANES), :]
            rows = jnp.where((lane_at >= at) & (lane_at < at + LANES), 0.0, rows)
            work[pl.ds(to, LANES), :] = rows - lax.dot_general(
                work[here_rows, pl.ds(to, LANES)],
                side,
                (((0,), (0,)), ((), ())),
                precision=highest,
                preferred_element_type=jnp.float32,
            )
            return inner

        lax.fori_loop(j + 1, blocks, below, 0)
        if beside is not None:
            beside(j)
        return carry

    lax.fori_loop(0, blocks, one_block, 0)


def shifted(matrix, level):
    row_at = lax.broadcasted_iota(jnp.int32, matrix.shape, 0)
    col_at = lax.broadcasted_iota(jnp.int32, matrix.shape, 1)
    return matrix + jnp.where(row_at == col_at, level, 0.0)


def pivot_kernel(
    n, width, picked_ref, targets_ref, out_ref, all_targets, work, send_sem, recv_sems, pair_sem
):
    me = here(width)
    hello(n, width, me)
    all_targets[me] = targets_ref[...]
    relay = Relay(
        n, width, me, all_targets, all_targets.at[me], send_sem, recv_sems, pair_sem
    )
    picked = picked_ref[...].astype(jnp.bfloat16)
    work[...] = shifted(
        kernel_block(picked, column_norms(picked), picked, row_norms(picked)), jitter_level
    )

    def begin():
        all_here(n)
        relay.start()

    def beside(j):
        pl.when(j == 0)(begin)
        pl.when(j == 1)(relay.relay_lines)
        pl.when(j == 2)(relay.relay_plane)

    invert_lower(work, out_ref, beside)
    relay.finish()
    relay.finish_sends()


def pivot_inverse(picked, targets_t, n, width):
    order = picked.shape[0]
    vmem = pl.BlockSpec(memory_space=pltpu.VMEM)
    f32 = jnp.float32
    return pl.pallas_call(
        functools.partial(pivot_kernel, n, width),
        out_shape=[
            jax.ShapeDtypeStruct((order, order), f32),
            jax.ShapeDtypeStruct((n,) + targets_t.shape, f32),
        ],
        in_specs=[vmem] * 2,
        out_specs=[vmem] * 2,
        scratch_shapes=[
            pltpu.VMEM((order, order), f32),
            pltpu.SemaphoreType.DMA,
            pltpu.SemaphoreType.DMA((n // 2,)),
            pltpu.SemaphoreType.DMA,
        ],
        compiler_params=pltpu.CompilerParams(collective_id=3, has_side_effects=True),
        name="pivot_inverse",
    )(picked, targets_t)


def gram_kernel(gram_ref, out_ref, work):
    work[...] = shifted(gram_ref[...], noise_level)
    invert_lower(work, out_ref)


def gram_inverse(gram):
    vmem = pl.BlockSpec(memory_space=pltpu.VMEM)
    return pl.pallas_call(
        gram_kernel,
        out_shape=jax.ShapeDtypeStruct(gram.shape, jnp.float32),
        in_specs=[vmem],
        out_specs=vmem,
        scratch_shapes=[pltpu.VMEM(gram.shape, jnp.float32)],
        name="gram_inverse",
    )(gram)


def here(width):
    return lax.axis_index("blk") * width + lax.axis_index("col")


def coords(index, width):
    return (lax.div(index, width), lax.rem(index, width))


def hello(n, width, me):
    barrier = pltpu.get_barrier_semaphore()

    def one(i, carry):
        peer = lax.rem(me + i, n)
        pl.semaphore_signal(
            barrier, inc=1, device_id=coords(peer, width), device_id_type=MESH
        )
        return carry

    lax.fori_loop(1, n, one, 0)


def all_here(n):
    pl.semaphore_wait(pltpu.get_barrier_semaphore(), n - 1)


def spread(n, width, me, src, dst, send_sem, recv_sem):
    def push(i, carry):
        peer = lax.rem(me + i, n)
        pltpu.make_async_remote_copy(
            src_ref=src(peer, i),
            dst_ref=dst(peer, i),
            send_sem=send_sem,
            recv_sem=recv_sem,
            device_id=coords(peer, width),
            device_id_type=MESH,
        ).start()
        return carry

    lax.fori_loop(1, n, push, 0)


def drain(ref, sem):
    pltpu.make_async_copy(ref, ref, sem).wait()


def flip(index, bits):
    moved = index
    weight = 1
    while weight <= bits:
        if bits & weight:
            moved = moved + weight * (1 - 2 * lax.rem(lax.div(index, weight), 2))
        weight *= 2
    return moved


class Relay:
    def __init__(self, n, width, me, blocks, own, send_sem, recv_sems, pair_sem):
        self.n, self.width, self.me = n, width, me
        self.blocks, self.own = blocks, own
        self.send_sem, self.recv_sems, self.pair_sem = send_sem, recv_sems, pair_sem
        self.plane = 2 * width
        self.lines = n // self.plane

    def send(self, src_ref, source, peer, recv_sem):
        pltpu.make_async_remote_copy(
            src_ref=src_ref,
            dst_ref=self.blocks.at[source],
            send_sem=self.send_sem,
            recv_sem=recv_sem,
            device_id=coords(peer, self.width),
            device_id_type=MESH,
        ).start()

    def fan(self, src_ref, source, i):
        for q in range(2, self.plane, 2):
            sem = self.recv_sems.at[self.lines * (q // 2) + i]
            self.send(src_ref, source, flip(self.me, q), sem)
        self.send(src_ref, source, flip(self.me, 1), self.pair_sem)

    def start(self):
        def along(i, carry):
            peer = lax.rem(self.me + self.plane * i, self.n)
            self.send(self.own, self.me, peer, self.recv_sems.at[i])
            return carry

        lax.fori_loop(1, self.lines, along, 0)
        self.fan(self.own, self.me, 0)

    def relay_lines(self):
        def one(i, carry):
            source = lax.rem(self.me - self.plane * i + self.n, self.n)
            drain(self.blocks.at[source], self.recv_sems.at[i])
            self.fan(self.blocks.at[source], source, i)
            return carry

        lax.fori_loop(1, self.lines, one, 0)

    def relay_plane(self, *offsets):
        for q in offsets or range(2, self.plane, 2):

            def one(i, carry, q=q):
                source = lax.rem(flip(self.me, q) - self.plane * i + self.n, self.n)
                ref = self.blocks.at[source]
                drain(ref, self.recv_sems.at[self.lines * (q // 2) + i])
                self.send(ref, source, flip(self.me, 1), self.pair_sem)
                return carry

            lax.fori_loop(0, self.lines, one, 0)

    def finish(self):
        drain(self.blocks.at[pl.ds(0, self.n // 2)], self.pair_sem)

    def finish_sends(self):
        drain(self.blocks.at[pl.ds(0, self.n - 1)], self.send_sem)


def gather_kernel(
    n,
    width,
    points_ref,
    pivots_ref,
    all_points,
    picked_ref,
    send_sem,
    recv_sems,
    pair_sem,
    own_sem,
):
    me = here(width)
    hello(n, width, me)
    keep = pltpu.make_async_copy(points_ref, all_points.at[me], own_sem)
    keep.start()
    relay = Relay(n, width, me, all_points, points_ref, send_sem, recv_sems, pair_sem)
    rows = points_ref.shape[0]
    order = picked_ref.shape[0]
    pivots = pivots_ref[...].astype(jnp.float32)
    in_row = jnp.concatenate([pivots[k : k + 1] for k in range(pivots.shape[0])], axis=1)
    in_column = jnp.broadcast_to(in_row, (8, order)).T
    chosen = jnp.broadcast_to(in_column[:, 0:1], (order, rows))
    row_at = lax.broadcasted_iota(jnp.int32, (order, rows), 1).astype(jnp.float32)
    together = min(4, relay.lines)
    picked_ref[...] = jnp.zeros_like(picked_ref)
    all_here(n)
    relay.start()

    def pick(group):
        def one(i, carry):
            sources = [group + relay.plane * (together * i + t) for t in range(together)]
            hits = [
                jnp.where(chosen - (rows * source).astype(jnp.float32) == row_at, 1.0, 0.0).astype(jnp.bfloat16)
                for source in sources
            ]
            found = jnp.concatenate([all_points[source] for source in sources], axis=0)
            picked_ref[...] += jnp.dot(
                jnp.concatenate(hits, axis=1), found, preferred_element_type=jnp.float32
            )
            return carry

        lax.fori_loop(0, relay.lines // together, one, 0)

    def low(bits):
        return lax.rem(flip(me, bits), relay.plane)

    relay.relay_lines()
    keep.wait()
    pick(low(0))
    for q in range(2, relay.plane, 2):
        relay.relay_plane(q)
        pick(low(q))
    relay.finish()
    for q in range(0, relay.plane, 2):
        pick(low(q + 1))
    relay.finish_sends()


def gather_all(points, pivots, n, width):
    vmem = pl.BlockSpec(memory_space=pltpu.VMEM)
    order = pivots.shape[0] * pivots.shape[1]
    return pl.pallas_call(
        functools.partial(gather_kernel, n, width),
        out_shape=[
            jax.ShapeDtypeStruct((n,) + points.shape, points.dtype),
            jax.ShapeDtypeStruct((order, points.shape[1]), jnp.float32),
        ],
        in_specs=[vmem] * 2,
        out_specs=[vmem] * 2,
        scratch_shapes=[
            pltpu.SemaphoreType.DMA,
            pltpu.SemaphoreType.DMA((n // 2,)),
            pltpu.SemaphoreType.DMA,
            pltpu.SemaphoreType.DMA,
        ],
        compiler_params=pltpu.CompilerParams(collective_id=0, has_side_effects=True),
        name="gather_points",
    )(points, pivots)


def sweep_kernel(
    n,
    width,
    points_ref,
    targets_ref,
    picked_ref,
    inverse_ref,
    wide_ref,
    tile_ref,
    gram_ref,
    proj_ref,
    zed_ref,
    image_ref,
    square_ref,
    left_part,
    right_part,
    left_got,
    right_got,
    send_sem,
    recv_sem,
):
    me = here(width)
    core, pair = lax.rem(me, 2), lax.div(me, 2)
    other = 1 - core
    partner = flip(me, 1)
    barrier = pltpu.get_barrier_semaphore()
    pl.semaphore_signal(barrier, inc=1, device_id=coords(partner, width), device_id_type=MESH)
    order = inverse_ref.shape[0]
    half = order // 2
    chunk = min(4, n // 2)
    picked = picked_ref[...].astype(jnp.bfloat16)
    picked_column = column_norms(picked)
    own = points_ref[pair, core]
    beside = points_ref[pair, other]
    own_column, beside_column = column_norms(own), column_norms(beside)
    own_cross = kernel_block(own, own_column, picked, row_norms(picked))
    wide = jnp.concatenate(
        [
            dot_t(own_cross[:, :half], inverse_ref[:half, :half]),
            dot_t(own_cross, inverse_ref[half:, :]),
        ],
        axis=1,
    )
    wide_ref[...] = wide
    own_targets = targets_ref[pair, core]
    image_ref[...] = noise_level * own_targets
    square_ref[...] = jnp.zeros_like(square_ref)
    for ref in (left_part, right_part):
        ref[...] = jnp.zeros_like(ref)

    def step(i, carry):
        at = i * chunk
        near = jnp.concatenate([points_ref[at + t, core] for t in range(chunk)], axis=0)
        far = jnp.concatenate([points_ref[at + t, other] for t in range(chunk)], axis=0)
        near_targets = jnp.concatenate([targets_ref[at + t, core] for t in range(chunk)], axis=1)
        far_targets = jnp.concatenate([targets_ref[at + t, other] for t in range(chunk)], axis=1)
        near_row, far_row = row_norms(near), row_norms(far)
        cross = kernel_block(picked, picked_column, near, near_row)
        own_near = kernel_block(own, own_column, near, near_row)
        own_far = kernel_block(own, own_column, far, far_row)
        beside_near = kernel_block(beside, beside_column, near, near_row)
        size = own.shape[0]
        for t in range(chunk):
            tile_ref[at + t, core] = own_near[:, t * size : (t + 1) * size]
            tile_ref[at + t, other] = own_far[:, t * size : (t + 1) * size]
        first = jnp.dot(
            inverse_ref[:, :half],
            cross[:half],
            precision=highest,
            preferred_element_type=jnp.float32,
        )
        top = first[:half]
        low = first[half:] + jnp.dot(
            inverse_ref[half:, half:],
            cross[half:],
            precision=highest,
            preferred_element_type=jnp.float32,
        )
        extra = [own_near, beside_near, near_targets]
        left_part[...] += dot_t(jnp.concatenate([top] + extra, axis=0), top)
        right_part[...] += dot_t(jnp.concatenate([top, low] + extra, axis=0), low)
        image_ref[...] += dot_t(near_targets, own_near) + dot_t(far_targets, own_far)
        squares = near_targets * near_targets + far_targets * far_targets
        for t in range(chunk):
            square_ref[...] += squares[:, t * size : (t + 1) * size]
        return carry

    lax.fori_loop(0, n // 2 // chunk, step, 0)
    pl.semaphore_wait(barrier, 1)
    size = own.shape[0]
    sides = [(left_part, left_got, half, 0), (right_part, right_got, order, half)]
    copies = []
    for part, got, tall, _ in sides:
        for rows in (pl.ds(0, tall), pl.ds(tall + size, part.shape[0] - tall - size)):
            copy = pltpu.make_async_remote_copy(
                src_ref=part.at[rows],
                dst_ref=got.at[rows],
                send_sem=send_sem.at[len(copies)],
                recv_sem=recv_sem.at[len(copies)],
                device_id=coords(partner, width),
                device_id_type=MESH,
            )
            copy.start()
            copies.append(copy)
    square_ref[...] = jnp.broadcast_to(
        jnp.sum(square_ref[...], axis=1, keepdims=True), square_ref.shape
    )
    gram_ref[half:, :half] = jnp.zeros((order - half, half), jnp.float32)
    for copy in copies:
        copy.wait_recv()
    for part, got, tall, at in sides:
        lanes = slice(at, at + part.shape[1])
        gram_ref[:tall, lanes] = part[:tall] + got[:tall]
        zed_ref[:, lanes] = (
            noise_level * wide_ref[:, lanes]
            + part[tall : tall + size]
            + got[tall + size : tall + 2 * size]
        )
        proj_ref[:, lanes] = part[tall + 2 * size :] + got[tall + 2 * size :]
    for copy in copies:
        copy.wait_send()


def sweep(all_points, all_targets, picked, inverse, n, width):
    rows, rhs_count, order = all_points.shape[1], all_targets.shape[1], picked.shape[0]
    vmem = pl.BlockSpec(memory_space=pltpu.VMEM)
    f32 = jnp.float32
    half = order // 2
    extra = 2 * rows + rhs_count
    partial = [
        pltpu.VMEM((half + extra, half), f32),
        pltpu.VMEM((order + extra, order - half), f32),
    ]
    wide, tile, *rest = pl.pallas_call(
        functools.partial(sweep_kernel, n, width),
        out_shape=[
            jax.ShapeDtypeStruct(shape, dtype)
            for shape, dtype in [
                ((rows, order), f32),
                ((n // 2, 2, rows, rows), f32),
                ((order, order), f32),
                ((rhs_count, order), f32),
                ((rows, order), f32),
                ((rhs_count, rows), f32),
                ((rhs_count, rows), f32),
            ]
        ],
        in_specs=[vmem] * 4,
        out_specs=[vmem] * 7,
        scratch_shapes=partial * 2 + [pltpu.SemaphoreType.DMA((4,))] * 2,
        compiler_params=pltpu.CompilerParams(
            collective_id=1, has_side_effects=True, vmem_limit_bytes=60 * 2**20
        ),
        name="sweep_points",
    )(
        all_points.reshape((n // 2, 2) + all_points.shape[1:]),
        all_targets.reshape((n // 2, 2) + all_targets.shape[1:]),
        picked,
        inverse,
    )
    return [wide, tile.reshape(n, rows, rows)] + rest


def cg_kernel(
    n,
    width,
    owners,
    tile_ref,
    rhs_ref,
    wide_ref,
    zed_ref,
    inverse_ref,
    proj_ref,
    image_ref,
    square_ref,
    sol_ref,
    res_ref,
    dirs,
    put,
    got,
    ans,
    kept_proj,
    kept_squares,
    kept_rz,
    all_rz,
    ends,
    dir_send,
    dir_recv,
    dir_pair,
    put_send,
    put_recv,
    ans_send,
    ans_recv,
    end_send,
    end_recv,
):
    me = here(width)
    rhs_count, row_count = rhs_ref.shape
    per = rhs_count // owners
    order = wide_ref.shape[1]
    lanes = order // LANES
    first_owner = (n - owners) // 2
    rank = me - first_owner
    owning = (rank >= 0) & (rank < owners)
    own_rows = pl.ds(rank * per, per)
    hello(n, width, me)

    def only_owners(body):
        pl.when(owning)(body)

    def wide_sum(values):
        return jnp.broadcast_to(jnp.sum(values, axis=1, keepdims=True), (values.shape[0], LANES))

    def to_owners(k, proj, sums):
        for q in range(lanes):
            put[k, :, q, :] = proj[:, q * LANES : (q + 1) * LANES]
        for s, value in enumerate(sums):
            put[k, :, lanes + s, :] = value

        def push(i, carry):
            turn = lax.rem(me + i, owners)
            peer = first_owner + turn

            @pl.when(peer != me)
            def _():
                pltpu.make_async_remote_copy(
                    src_ref=put.at[k, pl.ds(turn * per, per)],
                    dst_ref=got.at[k, lax.rem(me - peer + n, n) - 1],
                    send_sem=put_send.at[k],
                    recv_sem=put_recv.at[k],
                    device_id=coords(peer, width),
                    device_id_type=MESH,
                ).start()

            return carry

        lax.fori_loop(0, owners, push, 0)

    def drain_others(ref, sem):
        @pl.when(owning)
        def _():
            drain(ref.at[pl.ds(0, (owners - 1) * per)], sem)

        @pl.when(jnp.logical_not(owning))
        def _():
            drain(ref, sem)

    def finish_put(k):
        drain_others(put.at[k], put_send.at[k])

    def collect(k):
        drain(got.at[k], put_recv.at[k])
        start = put[k, own_rows]
        return lax.fori_loop(0, n - 1, lambda i, acc: acc + got[k, i], start)

    def answer(k, rows):
        for s, value in enumerate(rows):
            ans[k, own_rows, s, :] = value
        spread(
            n,
            width,
            me,
            lambda peer, i: ans.at[k, own_rows],
            lambda peer, i: ans.at[k, own_rows],
            ans_send.at[k],
            ans_recv.at[k],
        )

    def await_answer(k):
        drain_others(ans.at[k], ans_recv.at[k])

    def finish_answer(k):
        def body():
            def one(i, carry):
                drain(ans.at[k, pl.ds(0, per)], ans_send.at[k])
                return carry

            lax.fori_loop(1, n, one, 0)

        only_owners(body)

    def solve(proj):
        half = dot_t(proj, inverse_ref[...])
        coef = jnp.dot(
            half, inverse_ref[...], precision=highest, preferred_element_type=jnp.float32
        )
        return coef, wide_sum(half * half)

    def split(row):
        return [row[:, q * LANES : (q + 1) * LANES] for q in range(lanes)]

    def project(rows):
        return jnp.dot(rows, wide_ref[...], precision=highest, preferred_element_type=jnp.float32)

    def joined(packed):
        return jnp.concatenate([packed[:, q, :] for q in range(lanes)], axis=1)

    def preconditioned(coef, residual, applied):
        direction = (residual - dot_t(coef, wide_ref[...])) * (1.0 / noise_level)
        image = (applied - dot_t(coef, zed_ref[...])) * (1.0 / noise_level)
        return direction, image

    def multiplied(k, image):
        def one(j, acc):
            return acc + dot_t(dirs[k, j], tile_ref[j])

        return lax.fori_loop(0, n, one, noise_level * image, unroll=4)

    residual = rhs_ref[...]
    applied = image_ref[...]
    solution = jnp.zeros_like(residual)
    coef, covered = solve(proj_ref[...])
    all_rz[...] = (square_ref[...] - covered) * (1.0 / noise_level)
    direction, image = preconditioned(coef, residual, applied)

    def keep_own():
        for t in range(per):
            row = pl.ds(rank * per + t, 1)
            kept_proj[t : t + 1, :] = proj_ref[row, :]
            kept_squares[t : t + 1, :] = square_ref[row, :]
            kept_rz[t : t + 1, :] = all_rz[row, :]

    only_owners(keep_own)
    all_here(n)

    def later_answer(k):
        total = collect(k)
        size = kept_rz[...] / total[:, lanes, :]
        along, image_squares = total[:, lanes + 1, :], total[:, lanes + 2, :]
        size_row = jnp.concatenate([size] * lanes, axis=1)
        proj = kept_proj[...] - size_row * joined(total)
        squares = kept_squares[...] - 2.0 * size * along + size * size * image_squares
        coef, covered = solve(proj)
        rz = (squares - covered) * (1.0 / noise_level)
        kept_proj[...] = proj
        kept_squares[...] = squares
        kept_rz[...] = rz
        answer(k, split(coef) + [size, rz])

    def last_sums(values):
        ends[me, 0:1, 0:rhs_count] = dot_t(jnp.ones((8, row_count), jnp.float32), values)[0:1]
        spread(
            n,
            width,
            me,
            lambda peer, i: ends.at[me, pl.ds(0, 1)],
            lambda peer, i: ends.at[me, pl.ds(0, 1)],
            end_send,
            end_recv,
        )
        others = ends.at[pl.ds(0, n - 1), pl.ds(0, 1)]
        drain(others, end_recv)
        total = lax.fori_loop(1, n, lambda i, acc: acc + ends[i, 0:1, :], ends[0, 0:1, :])
        lane_at = lax.broadcasted_iota(jnp.int32, (rhs_count, LANES), 1)
        row_at = lax.broadcasted_iota(jnp.int32, (rhs_count, LANES), 0)
        spread_out = jnp.broadcast_to(total, (rhs_count, LANES))
        drain(others, end_send)
        return wide_sum(jnp.where(lane_at == row_at, spread_out, 0.0))

    relays = []
    for k in range(ITERS - 1):
        dirs[k, me] = image
        relay = Relay(
            n,
            width,
            me,
            dirs.at[k],
            dirs.at[k, me],
            dir_send.at[k],
            dir_recv.at[k],
            dir_pair.at[k],
        )
        relays.append(relay)
        relay.start()
        to_owners(
            k,
            project(image),
            [wide_sum(direction * image), wide_sum(residual * image), wide_sum(image * image)],
        )
        relay.relay_lines()
        only_owners(functools.partial(later_answer, k))
        relay.relay_plane()
        relay.finish()
        twice = multiplied(k, image)
        await_answer(k)
        size = ans[k, :, lanes, :]
        rz = ans[k, :, lanes + 1, :]
        ratio = rz / all_rz[...]
        all_rz[...] = rz
        solution = solution + size * direction
        residual = residual - size * image
        applied = applied - size * twice
        fresh, fresh_image = preconditioned(joined(ans[k]), residual, applied)
        direction = fresh + ratio * direction
        image = fresh_image + ratio * image
    size = all_rz[...] / last_sums(direction * image)
    solution = solution + size * direction
    residual = residual - size * image
    sol_ref[...] = solution
    res_ref[...] = residual
    for relay in relays:
        relay.finish_sends()
    for k in range(ITERS - 1):
        finish_put(k)
        finish_answer(k)


def solve_cg(tile, targets_t, wide_factor, zed, inverse, proj, image, squares, n, width):
    rhs_count, row_count = targets_t.shape
    owners = min(n // 2, rhs_count)
    per = rhs_count // owners
    order = wide_factor.shape[1]
    rows = -(-(order // LANES + 3) // 8) * 8
    vmem = pl.BlockSpec(memory_space=pltpu.VMEM)
    f32 = jnp.float32
    return pl.pallas_call(
        functools.partial(cg_kernel, n, width, owners),
        out_shape=[jax.ShapeDtypeStruct((rhs_count, row_count), f32)] * 2,
        in_specs=[vmem] * 8,
        out_specs=[vmem] * 2,
        scratch_shapes=[
            pltpu.VMEM((ITERS - 1, n, rhs_count, row_count), f32),
            pltpu.VMEM((ITERS - 1, rhs_count, rows, LANES), f32),
            pltpu.VMEM((ITERS - 1, n - 1, per, rows, LANES), f32),
            pltpu.VMEM((ITERS - 1, rhs_count, rows, LANES), f32),
            pltpu.VMEM((per, order), f32),
            pltpu.VMEM((per, LANES), f32),
            pltpu.VMEM((per, LANES), f32),
            pltpu.VMEM((rhs_count, LANES), f32),
            pltpu.VMEM((n, 8, LANES), f32),
            pltpu.SemaphoreType.DMA((ITERS - 1,)),
            pltpu.SemaphoreType.DMA((ITERS - 1, n // 2)),
            pltpu.SemaphoreType.DMA((ITERS - 1,)),
        ]
        + [pltpu.SemaphoreType.DMA((ITERS - 1,))] * 4
        + [pltpu.SemaphoreType.DMA] * 2,
        compiler_params=pltpu.CompilerParams(
            collective_id=2, has_side_effects=True, vmem_limit_bytes=60 * 2**20
        ),
        name="conjugate_gradients",
    )(tile, targets_t, wide_factor, zed, inverse, proj, image, squares)


def finish_kernel(wide_ref, solution_ref, residual_ref, factor_ref, solution_out, residual_out):
    factor_ref[...] = wide_ref[...].astype(jnp.bfloat16)
    solution_out[...] = solution_ref[...]
    residual_out[...] = residual_ref[...]


def finish(wide, solution_t, residual_t):
    vmem = pl.BlockSpec(memory_space=pltpu.VMEM)
    flat = jax.ShapeDtypeStruct(solution_t.shape, jnp.float32)
    return pl.pallas_call(
        finish_kernel,
        out_shape=[jax.ShapeDtypeStruct(wide.shape, jnp.bfloat16), flat, flat],
        in_specs=[vmem] * 3,
        out_specs=[vmem] * 3,
        name="finish_outputs",
    )(wide, solution_t, residual_t)


def per_device(n, width, points, targets, pivots):
    targets_t = targets.T
    all_points, picked = gather_all(points, pivots, n, width)
    inverse, all_targets = pivot_inverse(picked, targets_t, n, width)
    wide, tile, gram, proj, zed, image, squares = sweep(
        all_points, all_targets, picked, inverse, n, width
    )
    solution_t, residual_t = solve_cg(
        tile, targets_t, wide, zed, gram_inverse(gram), proj, image, squares, n, width
    )
    factor, solution_t, residual_t = finish(wide, solution_t, residual_t)
    return (factor, solution_t.T, residual_t.T)


def solution(mesh):
    n, width = mesh.size, mesh.shape["col"]
    return jax.shard_map(
        functools.partial(per_device, n, width),
        mesh=mesh,
        in_specs=(P(("blk", "col"), None), P(("blk", "col"), None), P()),
        out_specs=(P(("blk", "col"), None), P(("blk", "col"), None), P(("blk", "col"), None)),
        check_vma=False,
    )
```

```python
import functools

import jax
import jax.numpy as jnp
from jax import lax
from jax.experimental import pallas as pl
from jax.experimental.pallas import tpu as pltpu
from jax.sharding import PartitionSpec as P

FEATURES = 128
ITERS = 3
LANES = 128


noise_level = 0.5
jitter_level = 0.05
highest = lax.Precision.HIGHEST
MESH = pl.DeviceIdType.MESH


def dot_t(left, right):
    return lax.dot_general(
        left,
        right,
        (((1,), (1,)), ((), ())),
        precision=highest,
        preferred_element_type=jnp.float32,
    )


def pieces(values):
    high = values.astype(jnp.bfloat16)
    rest = values - high.astype(jnp.float32)
    middle = rest.astype(jnp.bfloat16)
    low = (rest - middle.astype(jnp.float32)).astype(jnp.bfloat16)
    return high, middle, low


def split_dot(stacked, refs, side):
    step = stacked.shape[0] // 3
    parts = [
        lax.dot_general(
            stacked[: (3 - k) * step],
            refs[k],
            (((1,), (side,)), ((), ())),
            preferred_element_type=jnp.float32,
        )
        for k in range(3)
    ]
    total = parts[0][2 * step :] + parts[1][step : 2 * step] + parts[2]
    return parts[0][:step] + (parts[0][step : 2 * step] + parts[1][:step] + total)


def stack(values):
    return jnp.concatenate(pieces(values), axis=0)


def column_norms(point_rows):
    wide_rows = point_rows.astype(jnp.float32)
    return jnp.sum(wide_rows * wide_rows, axis=1, keepdims=True)


def row_norms(point_rows):
    wide_rows = point_rows.astype(jnp.float32)
    return dot_t(jnp.ones((8, wide_rows.shape[1]), jnp.float32), wide_rows * wide_rows)[0:1]


def kernel_block(left_rows, left_norms, right_rows, right_norms):
    inner = lax.dot_general(
        left_rows, right_rows, (((1,), (1,)), ((), ())), preferred_element_type=jnp.float32
    )
    distance = left_norms + right_norms - 2.0 * inner
    return jnp.exp(-2.0 * distance / FEATURES)


def lower_inverse_rows(rows):
    count = len(rows)
    group = max(count // 2, 1)
    lane = lax.broadcasted_iota(jnp.int32, (8, LANES), 1)
    sub = lax.broadcasted_iota(jnp.int32, (8, LANES), 0)

    def full_of(values):
        return jnp.broadcast_to(values, (8, LANES))

    def columns(row, base):
        return [full_of(row[:, base + c : base + c + 1]) for c in range(8)]

    rows = list(rows)
    done = []
    for start in range(0, count, group):
        end = start + group
        whole = []
        ahead = columns(rows[start], 8 * start)
        pivot = full_of(ahead[0][0:1])
        for p in range(start, end):
            base = 8 * p
            inside = (lane >= base) & (lane < base + 8)
            cols = ahead
            forward = jnp.where(inside, jnp.where(lane == sub + base, 1.0, 0.0), rows[p])
            pivots = jnp.ones((8, LANES), jnp.float32)
            recips, spread_rows, coefs = [], [], []
            more = p + 1 < end
            if more:
                own = columns(rows[p + 1], base)
                ahead = columns(rows[p + 1], base + 8)
                following = jnp.where(inside, 0.0, rows[p + 1])
            for j in range(8):
                recip = 1.0 / pivot
                pivots = jnp.where(sub == j, pivot, pivots)
                coef = {c: full_of(cols[c][j : j + 1]) for c in range(j + 1, 8)}
                if j < 7:
                    square = full_of(cols[j][j + 1 : j + 2]) * coef[j + 1]
                    pivot = full_of(cols[j + 1][j + 1 : j + 2]) - square * recip
                elif more:
                    corner = full_of(own[7][0:1])
                    pivot = full_of(ahead[0][0:1]) - corner * corner * recip
                scaled = cols[j] * recip
                below = jnp.where(sub > j, scaled, 0.0)
                spread_row = full_of(forward[j : j + 1])
                forward = forward - below * spread_row
                for c in range(j + 1, 8):
                    cols[c] = cols[c] - scaled * coef[c]
                if more:
                    multiplier = own[j] * recip
                    for c in range(j + 1, 8):
                        own[c] = own[c] - multiplier * coef[c]
                    for c in range(8):
                        ahead[c] = ahead[c] - multiplier * full_of(own[j][c : c + 1])
                    following = following - multiplier * spread_row
                recips.append(recip)
                spread_rows.append(spread_row)
                coefs.append(coef)
            scaled = forward * lax.rsqrt(pivots)
            lower = lane <= sub + base
            done.append(jnp.where(lower, scaled, 0.0))
            whole.append(jnp.where(lower | (lane >= 8 * end), scaled, 0.0))
            if more:
                rows[p + 1] = following
            for v in range(p + 2, end):
                own_v = columns(rows[v], base)
                new = jnp.where(inside, 0.0, rows[v])
                for j in range(8):
                    multiplier = own_v[j] * recips[j]
                    new = new - multiplier * spread_rows[j]
                    for c in range(j + 1, 8):
                        own_v[c] = own_v[c] - multiplier * coefs[j][c]
                rows[v] = new
        if end < count:
            side = jnp.concatenate(whole, axis=0)
            both = lax.dot_general(side, side, (((0,), (0,)), ((), ())), precision=highest, preferred_element_type=jnp.float32)
            inside = (lane >= 8 * start) & (lane < 8 * end)
            for v in range(end, count):
                rows[v] = jnp.where(inside, 0.0, rows[v]) - both[8 * v : 8 * v + 8]
    return done

def invert_lower(work, out_ref, beside=None):
    order = work.shape[0]
    blocks = order // LANES
    row_at = lax.broadcasted_iota(jnp.int32, (LANES, LANES), 0)
    col_at = lax.broadcasted_iota(jnp.int32, (LANES, LANES), 1)

    def one_block(j, carry):
        at = pl.multiple_of(j * LANES, LANES)
        inverse = jnp.concatenate(
            lower_inverse_rows(
                [work[pl.ds(at + 8 * v, 8), pl.ds(at, LANES)] for v in range(LANES // 8)]
            ),
            axis=0,
        )
        work[pl.ds(at, LANES), pl.ds(at, LANES)] = jnp.where(row_at == col_at, 1.0, 0.0)

        def combine(k):
            low, high = k * LANES, (k + 1) * LANES
            side = jnp.dot(inverse, work[low:high, :], precision=highest, preferred_element_type=jnp.float32)
            out_ref[low:high, :high] = side[:, :high]
            if high < order:
                out_ref[low:high, high:] = jnp.zeros((LANES, order - high), jnp.float32)
                change = lax.dot_general(side[:, high:], side, (((0,), (0,)), ((), ())), precision=highest, preferred_element_type=jnp.float32)
                if low: work[high:, :low] -= change[:, :low]
                work[high:, low:high] = -change[:, low:high]
                work[high:, high:] -= change[:, high:]

        for k in range(blocks):
            pl.when(j == k)(functools.partial(combine, k))
        if beside is not None:
            beside(j)
        return carry

    lax.fori_loop(0, blocks, one_block, 0)


def shifted(matrix, level):
    row_at = lax.broadcasted_iota(jnp.int32, matrix.shape, 0)
    col_at = lax.broadcasted_iota(jnp.int32, matrix.shape, 1)
    return matrix + jnp.where(row_at == col_at, level, 0.0)


def pivot_kernel(
    n, width, picked_ref, targets_ref, out_ref, all_targets, work, send_sem, recv_sems, pair_sem
):
    me = here(width)
    hello(n, width, me)
    all_targets[me] = targets_ref[...]
    relay = Relay(
        n, width, me, all_targets, all_targets.at[me], send_sem, recv_sems, pair_sem
    )
    picked = picked_ref[...].astype(jnp.bfloat16)
    work[...] = shifted(
        kernel_block(picked, column_norms(picked), picked, row_norms(picked)), jitter_level
    )

    def begin():
        all_here(n)
        relay.start()

    def beside(j):
        pl.when(j == 0)(begin)
        pl.when(j == 1)(relay.relay_lines)
        pl.when(j == 2)(relay.relay_plane)

    invert_lower(work, out_ref, beside)
    relay.finish()
    relay.finish_sends()


def pivot_inverse(picked, targets_t, n, width):
    order = picked.shape[0]
    vmem = pl.BlockSpec(memory_space=pltpu.VMEM)
    f32 = jnp.float32
    return pl.pallas_call(
        functools.partial(pivot_kernel, n, width),
        out_shape=[
            jax.ShapeDtypeStruct((order, order), f32),
            jax.ShapeDtypeStruct((n,) + targets_t.shape, f32),
        ],
        in_specs=[vmem] * 2,
        out_specs=[vmem] * 2,
        scratch_shapes=[
            pltpu.VMEM((order, order), f32),
            pltpu.SemaphoreType.DMA,
            pltpu.SemaphoreType.DMA((n // 2,)),
            pltpu.SemaphoreType.DMA,
        ],
        compiler_params=pltpu.CompilerParams(collective_id=3, has_side_effects=True),
        name="pivot_inverse",
    )(picked, targets_t)


def gram_kernel(gram_ref, split_ref, work, out_ref):
    work[...] = shifted(gram_ref[...], noise_level)
    invert_lower(work, out_ref)
    for k, piece in enumerate(pieces(out_ref[...])):
        split_ref[k] = piece


def gram_inverse(gram):
    vmem = pl.BlockSpec(memory_space=pltpu.VMEM)
    return pl.pallas_call(
        gram_kernel,
        out_shape=jax.ShapeDtypeStruct((3,) + gram.shape, jnp.bfloat16),
        in_specs=[vmem],
        out_specs=vmem,
        scratch_shapes=[pltpu.VMEM(gram.shape, jnp.float32)] * 2,
        name="gram_inverse",
    )(gram)


def here(width):
    return lax.axis_index("blk") * width + lax.axis_index("col")


def coords(index, width):
    return (lax.div(index, width), lax.rem(index, width))


def hello(n, width, me):
    barrier = pltpu.get_barrier_semaphore()

    def one(i, carry):
        peer = lax.rem(me + i, n)
        pl.semaphore_signal(
            barrier, inc=1, device_id=coords(peer, width), device_id_type=MESH
        )
        return carry

    lax.fori_loop(1, n, one, 0)


def all_here(n):
    pl.semaphore_wait(pltpu.get_barrier_semaphore(), n - 1)


def spread(n, width, me, src, dst, send_sem, recv_sem):
    def push(i, carry):
        peer = lax.rem(me + i, n)
        pltpu.make_async_remote_copy(
            src_ref=src(peer, i),
            dst_ref=dst(peer, i),
            send_sem=send_sem,
            recv_sem=recv_sem,
            device_id=coords(peer, width),
            device_id_type=MESH,
        ).start()
        return carry

    lax.fori_loop(1, n, push, 0)


def drain(ref, sem):
    pltpu.make_async_copy(ref, ref, sem).wait()


def flip(index, bits):
    moved = index
    weight = 1
    while weight <= bits:
        if bits & weight:
            moved = moved + weight * (1 - 2 * lax.rem(lax.div(index, weight), 2))
        weight *= 2
    return moved


class Relay:
    def __init__(self, n, width, me, blocks, own, send_sem, recv_sems, pair_sem):
        self.n, self.width, self.me = n, width, me
        self.blocks, self.own = blocks, own
        self.send_sem, self.recv_sems, self.pair_sem = send_sem, recv_sems, pair_sem
        self.plane = 2 * width
        self.lines = n // self.plane

    def send(self, src_ref, source, peer, recv_sem):
        pltpu.make_async_remote_copy(
            src_ref=src_ref,
            dst_ref=self.blocks.at[source],
            send_sem=self.send_sem,
            recv_sem=recv_sem,
            device_id=coords(peer, self.width),
            device_id_type=MESH,
        ).start()

    def fan(self, src_ref, source, i):
        for q in range(2, self.plane, 2):
            sem = self.recv_sems.at[self.lines * (q // 2) + i]
            self.send(src_ref, source, flip(self.me, q), sem)
        self.send(src_ref, source, flip(self.me, 1), self.pair_sem)

    def start(self):
        def along(i, carry):
            peer = lax.rem(self.me + self.plane * i, self.n)
            self.send(self.own, self.me, peer, self.recv_sems.at[i])
            return carry

        lax.fori_loop(1, self.lines, along, 0)
        self.fan(self.own, self.me, 0)

    def relay_lines(self):
        def one(i, carry):
            source = lax.rem(self.me - self.plane * i + self.n, self.n)
            drain(self.blocks.at[source], self.recv_sems.at[i])
            self.fan(self.blocks.at[source], source, i)
            return carry

        lax.fori_loop(1, self.lines, one, 0)

    def relay_plane(self, *offsets):
        for q in offsets or range(2, self.plane, 2):

            def one(i, carry, q=q):
                source = lax.rem(flip(self.me, q) - self.plane * i + self.n, self.n)
                ref = self.blocks.at[source]
                drain(ref, self.recv_sems.at[self.lines * (q // 2) + i])
                self.send(ref, source, flip(self.me, 1), self.pair_sem)
                return carry

            lax.fori_loop(0, self.lines, one, 0)

    def finish(self):
        drain(self.blocks.at[pl.ds(0, self.n // 2)], self.pair_sem)

    def finish_sends(self):
        drain(self.blocks.at[pl.ds(0, self.n - 1)], self.send_sem)


def gather_kernel(
    n,
    width,
    points_ref,
    pivots_ref,
    all_points,
    picked_ref,
    send_sem,
    recv_sems,
    pair_sem,
    own_sem,
):
    me = here(width)
    hello(n, width, me)
    keep = pltpu.make_async_copy(points_ref, all_points.at[me], own_sem)
    keep.start()
    relay = Relay(n, width, me, all_points, points_ref, send_sem, recv_sems, pair_sem)
    rows = points_ref.shape[0]
    order = picked_ref.shape[0]
    pivots = pivots_ref[...].astype(jnp.float32)
    in_row = jnp.concatenate([pivots[k : k + 1] for k in range(pivots.shape[0])], axis=1)
    in_column = jnp.broadcast_to(in_row, (8, order)).T
    chosen = jnp.broadcast_to(in_column[:, 0:1], (order, rows))
    row_at = lax.broadcasted_iota(jnp.int32, (order, rows), 1).astype(jnp.float32)
    together = min(4, relay.lines)
    picked_ref[...] = jnp.zeros_like(picked_ref)
    all_here(n)
    relay.start()

    def pick(group):
        def one(i, carry):
            sources = [group + relay.plane * (together * i + t) for t in range(together)]
            hits = [
                jnp.where(chosen - (rows * source).astype(jnp.float32) == row_at, 1.0, 0.0).astype(jnp.bfloat16)
                for source in sources
            ]
            found = jnp.concatenate([all_points[source] for source in sources], axis=0)
            picked_ref[...] += jnp.dot(
                jnp.concatenate(hits, axis=1), found, preferred_element_type=jnp.float32
            )
            return carry

        lax.fori_loop(0, relay.lines // together, one, 0)

    def low(bits):
        return lax.rem(flip(me, bits), relay.plane)

    relay.relay_lines()
    keep.wait()
    pick(low(0))
    for q in range(2, relay.plane, 2):
        relay.relay_plane(q)
        pick(low(q))
    relay.finish()
    for q in range(0, relay.plane, 2):
        pick(low(q + 1))
    relay.finish_sends()


def gather_all(points, pivots, n, width):
    vmem = pl.BlockSpec(memory_space=pltpu.VMEM)
    order = pivots.shape[0] * pivots.shape[1]
    return pl.pallas_call(
        functools.partial(gather_kernel, n, width),
        out_shape=[
            jax.ShapeDtypeStruct((n,) + points.shape, points.dtype),
            jax.ShapeDtypeStruct((order, points.shape[1]), jnp.float32),
        ],
        in_specs=[vmem] * 2,
        out_specs=[vmem] * 2,
        scratch_shapes=[
            pltpu.SemaphoreType.DMA,
            pltpu.SemaphoreType.DMA((n // 2,)),
            pltpu.SemaphoreType.DMA,
            pltpu.SemaphoreType.DMA,
        ],
        compiler_params=pltpu.CompilerParams(collective_id=0, has_side_effects=True),
        name="gather_points",
    )(points, pivots)


def sweep_kernel(
    n,
    width,
    points_ref,
    targets_ref,
    picked_ref,
    inverse_ref,
    wide_ref,
    tile_ref,
    gram_ref,
    proj_ref,
    zed_ref,
    image_ref,
    square_ref,
    left_part,
    right_part,
    left_got,
    right_got,
    crossed,
    send_sem,
    recv_sem,
):
    me = here(width)
    core, pair = lax.rem(me, 2), lax.div(me, 2)
    other = 1 - core
    partner = flip(me, 1)
    barrier = pltpu.get_barrier_semaphore()
    pl.semaphore_signal(barrier, inc=1, device_id=coords(partner, width), device_id_type=MESH)
    order = inverse_ref.shape[0]
    half = order // 2
    chunk = min(4, n // 2)
    picked = picked_ref[...].astype(jnp.bfloat16)
    picked_column = column_norms(picked)
    own = points_ref[pair, core]
    beside = points_ref[pair, other]
    own_column, beside_column = column_norms(own), column_norms(beside)
    own_targets = targets_ref[pair, core]
    image_ref[...] = noise_level * own_targets
    square_ref[...] = jnp.zeros_like(square_ref)
    for ref in (left_part, right_part):
        ref[...] = jnp.zeros_like(ref)

    steps = n // 2 // chunk

    def cross_of(i):
        at = i * chunk
        near = jnp.concatenate([points_ref[at + t, core] for t in range(chunk)], axis=0)
        return kernel_block(picked, picked_column, near, row_norms(near))

    crossed[...] = cross_of(0)

    def step(i, carry):
        at = i * chunk
        cross = crossed[...]
        near = jnp.concatenate([points_ref[at + t, core] for t in range(chunk)], axis=0)
        far = jnp.concatenate([points_ref[at + t, other] for t in range(chunk)], axis=0)
        near_targets = jnp.concatenate([targets_ref[at + t, core] for t in range(chunk)], axis=1)
        far_targets = jnp.concatenate([targets_ref[at + t, other] for t in range(chunk)], axis=1)
        near_row, far_row = row_norms(near), row_norms(far)
        own_near = kernel_block(own, own_column, near, near_row)
        own_far = kernel_block(own, own_column, far, far_row)
        beside_near = kernel_block(beside, beside_column, near, near_row)
        size = own.shape[0]
        for t in range(chunk):
            tile_ref[at + t, core] = own_near[:, t * size : (t + 1) * size]
            tile_ref[at + t, other] = own_far[:, t * size : (t + 1) * size]
        first = jnp.dot(
            inverse_ref[:, :half],
            cross[:half],
            precision=highest,
            preferred_element_type=jnp.float32,
        )
        top = first[:half]
        low = first[half:] + jnp.dot(
            inverse_ref[half:, half:],
            cross[half:],
            precision=highest,
            preferred_element_type=jnp.float32,
        )
        crossed[...] = cross_of(jnp.minimum(i + 1, steps - 1))
        extra = [own_near, beside_near, near_targets]
        left_part[...] += dot_t(jnp.concatenate([top] + extra, axis=0), top)
        right_part[...] += dot_t(jnp.concatenate([top, low] + extra, axis=0), low)
        image_ref[...] += split_dot(
            stack(jnp.concatenate([near_targets, far_targets], axis=1)),
            pieces(jnp.concatenate([own_near, own_far], axis=1)),
            1,
        )
        squares = near_targets * near_targets + far_targets * far_targets
        for t in range(chunk):
            square_ref[...] += squares[:, t * size : (t + 1) * size]

        @pl.when(i == lax.div(pair, chunk))
        def _():
            for t in range(chunk):

                @pl.when(lax.rem(pair, chunk) == t)
                def _(t=t):
                    for rows, value in ((slice(0, half), top), (slice(half, order), low)):
                        wide_ref[:, rows] = value[:, t * size : (t + 1) * size].T

        return carry

    lax.fori_loop(0, steps, step, 0)
    pl.semaphore_wait(barrier, 1)
    size = own.shape[0]
    sides = [(left_part, left_got, half, 0), (right_part, right_got, order, half)]
    copies = []
    for part, got, tall, _ in sides:
        for rows in (pl.ds(0, tall), pl.ds(tall + size, part.shape[0] - tall - size)):
            copy = pltpu.make_async_remote_copy(
                src_ref=part.at[rows],
                dst_ref=got.at[rows],
                send_sem=send_sem.at[len(copies)],
                recv_sem=recv_sem.at[len(copies)],
                device_id=coords(partner, width),
                device_id_type=MESH,
            )
            copy.start()
            copies.append(copy)
    square_ref[...] = jnp.broadcast_to(
        jnp.sum(square_ref[...], axis=1, keepdims=True), square_ref.shape
    )
    gram_ref[half:, :half] = jnp.zeros((order - half, half), jnp.float32)
    for copy in copies:
        copy.wait_recv()
    for part, got, tall, at in sides:
        lanes = slice(at, at + part.shape[1])
        gram_ref[:tall, lanes] = part[:tall] + got[:tall]
        zed_ref[:, lanes] = (
            noise_level * wide_ref[:, lanes]
            + part[tall : tall + size]
            + got[tall + size : tall + 2 * size]
        )
        proj_ref[:, lanes] = part[tall + 2 * size :] + got[tall + 2 * size :]
    for copy in copies:
        copy.wait_send()


def sweep(all_points, all_targets, picked, inverse, n, width):
    rows, rhs_count, order = all_points.shape[1], all_targets.shape[1], picked.shape[0]
    vmem = pl.BlockSpec(memory_space=pltpu.VMEM)
    f32 = jnp.float32
    half = order // 2
    extra = 2 * rows + rhs_count
    partial = [
        pltpu.VMEM((half + extra, half), f32),
        pltpu.VMEM((order + extra, order - half), f32),
    ]
    wide, tile, *rest = pl.pallas_call(
        functools.partial(sweep_kernel, n, width),
        out_shape=[
            jax.ShapeDtypeStruct(shape, dtype)
            for shape, dtype in [
                ((rows, order), f32),
                ((n // 2, 2, rows, rows), f32),
                ((order, order), f32),
                ((rhs_count, order), f32),
                ((rows, order), f32),
                ((rhs_count, rows), f32),
                ((rhs_count, rows), f32),
            ]
        ],
        in_specs=[vmem] * 4,
        out_specs=[vmem] * 7,
        scratch_shapes=partial * 2
        + [pltpu.VMEM((order, min(4, n // 2) * rows), f32)]
        + [pltpu.SemaphoreType.DMA((4,))] * 2,
        compiler_params=pltpu.CompilerParams(
            collective_id=1, has_side_effects=True, vmem_limit_bytes=60 * 2**20
        ),
        name="sweep_points",
    )(
        all_points.reshape((n // 2, 2) + all_points.shape[1:]),
        all_targets.reshape((n // 2, 2) + all_targets.shape[1:]),
        picked,
        inverse,
    )
    return [wide, tile.reshape(n, rows, rows)] + rest


def cg_kernel(
    n,
    width,
    owners,
    tile_ref,
    rhs_ref,
    wide_ref,
    zed_ref,
    inverse_ref,
    proj_ref,
    image_ref,
    square_ref,
    sol_ref,
    res_ref,
    dirs,
    put,
    got,
    ans,
    kept_proj,
    kept_squares,
    kept_rz,
    all_rz,
    ends,
    narrow,
    wide_split,
    zed_split,
    dir_send,
    dir_recv,
    dir_pair,
    put_send,
    put_recv,
    ans_send,
    ans_recv,
    end_send,
    end_recv,
):
    me = here(width)
    rhs_count, row_count = rhs_ref.shape
    per = rhs_count // owners
    order = wide_ref.shape[1]
    lanes = order // LANES
    first_owner = (n - owners) // 2
    rank = me - first_owner
    owning = (rank >= 0) & (rank < owners)
    own_rows = pl.ds(rank * per, per)
    hello(n, width, me)

    def only_owners(body):
        pl.when(owning)(body)

    def wide_sum(values):
        return jnp.broadcast_to(jnp.sum(values, axis=1, keepdims=True), (values.shape[0], LANES))

    def to_owners(k, proj, sums):
        for q in range(lanes):
            put[k, :, q, :] = proj[:, q * LANES : (q + 1) * LANES]
        for s, value in enumerate(sums):
            put[k, :, lanes + s, :] = value

        def push(i, carry):
            turn = lax.rem(me + i, owners)
            peer = first_owner + turn

            @pl.when(peer != me)
            def _():
                pltpu.make_async_remote_copy(
                    src_ref=put.at[k, pl.ds(turn * per, per)],
                    dst_ref=got.at[k, lax.rem(me - peer + n, n) - 1],
                    send_sem=put_send.at[k],
                    recv_sem=put_recv.at[k],
                    device_id=coords(peer, width),
                    device_id_type=MESH,
                ).start()

            return carry

        lax.fori_loop(0, owners, push, 0)

    def drain_others(ref, sem):
        @pl.when(owning)
        def _():
            drain(ref.at[pl.ds(0, (owners - 1) * per)], sem)

        @pl.when(jnp.logical_not(owning))
        def _():
            drain(ref, sem)

    def finish_put(k):
        drain_others(put.at[k], put_send.at[k])

    def collect(k):
        drain(got.at[k], put_recv.at[k])
        start = put[k, own_rows]
        return lax.fori_loop(0, n - 1, lambda i, acc: acc + got[k, i], start)

    def answer(k, rows):
        for s, value in enumerate(rows):
            ans[k, own_rows, s, :] = value
        spread(
            n,
            width,
            me,
            lambda peer, i: ans.at[k, own_rows],
            lambda peer, i: ans.at[k, own_rows],
            ans_send.at[k],
            ans_recv.at[k],
        )

    def await_answer(k):
        drain_others(ans.at[k], ans_recv.at[k])

    def finish_answer(k):
        def body():
            def one(i, carry):
                drain(ans.at[k, pl.ds(0, per)], ans_send.at[k])
                return carry

            lax.fori_loop(1, n, one, 0)

        only_owners(body)

    def solve(proj):
        def stacked(values):
            if values.shape[0] % 16 == 0:
                return stack(values)
            for t, piece in enumerate(pieces(values)):
                narrow[8 * t : 8 * t + values.shape[0], :] = piece.astype(jnp.float32)
            return narrow[...].astype(jnp.bfloat16)

        count = proj.shape[0]
        half = split_dot(stacked(proj), inverse_ref, 1)[:count]
        coef = split_dot(stacked(half), inverse_ref, 0)[:count]
        return coef, wide_sum(half * half)

    def split(row):
        return [row[:, q * LANES : (q + 1) * LANES] for q in range(lanes)]

    def project(rows):
        return split_dot(stack(rows), wide_split, 0)

    def joined(packed):
        return jnp.concatenate([packed[:, q, :] for q in range(lanes)], axis=1)

    def preconditioned(coef, residual, applied):
        stacked = stack(coef)
        direction = (residual - split_dot(stacked, wide_split, 1)) * (1.0 / noise_level)
        image = (applied - split_dot(stacked, zed_split, 1)) * (1.0 / noise_level)
        return direction, image

    def multiplied(k, image):
        def one(j, acc):
            return acc + dot_t(dirs[k, j], tile_ref[j])

        return lax.fori_loop(0, n, one, noise_level * image, unroll=4)

    narrow[...] = jnp.zeros_like(narrow)
    for split_ref, ref in ((wide_split, wide_ref), (zed_split, zed_ref)):
        for t, piece in enumerate(pieces(ref[...])):
            split_ref[t] = piece
    residual = rhs_ref[...]
    applied = image_ref[...]
    solution = jnp.zeros_like(residual)
    coef, covered = solve(proj_ref[...])
    all_rz[...] = (square_ref[...] - covered) * (1.0 / noise_level)
    direction, image = preconditioned(coef, residual, applied)

    def keep_own():
        for t in range(per):
            row = pl.ds(rank * per + t, 1)
            kept_proj[t : t + 1, :] = proj_ref[row, :]
            kept_squares[t : t + 1, :] = square_ref[row, :]
            kept_rz[t : t + 1, :] = all_rz[row, :]

    only_owners(keep_own)
    all_here(n)

    def later_answer(k):
        total = collect(k)
        size = kept_rz[...] / total[:, lanes, :]
        along, image_squares = total[:, lanes + 1, :], total[:, lanes + 2, :]
        size_row = jnp.concatenate([size] * lanes, axis=1)
        proj = kept_proj[...] - size_row * joined(total)
        squares = kept_squares[...] - 2.0 * size * along + size * size * image_squares
        coef, covered = solve(proj)
        rz = (squares - covered) * (1.0 / noise_level)
        kept_proj[...] = proj
        kept_squares[...] = squares
        kept_rz[...] = rz
        answer(k, split(coef) + [size, rz])

    def last_sums(values):
        ends[me, 0:1, 0:rhs_count] = dot_t(jnp.ones((8, row_count), jnp.float32), values)[0:1]
        spread(
            n,
            width,
            me,
            lambda peer, i: ends.at[me, pl.ds(0, 1)],
            lambda peer, i: ends.at[me, pl.ds(0, 1)],
            end_send,
            end_recv,
        )
        others = ends.at[pl.ds(0, n - 1), pl.ds(0, 1)]
        drain(others, end_recv)
        total = lax.fori_loop(1, n, lambda i, acc: acc + ends[i, 0:1, :], ends[0, 0:1, :])
        lane_at = lax.broadcasted_iota(jnp.int32, (rhs_count, LANES), 1)
        row_at = lax.broadcasted_iota(jnp.int32, (rhs_count, LANES), 0)
        spread_out = jnp.broadcast_to(total, (rhs_count, LANES))
        drain(others, end_send)
        return wide_sum(jnp.where(lane_at == row_at, spread_out, 0.0))

    relays = []
    for k in range(ITERS - 1):
        dirs[k, me] = image
        relay = Relay(
            n,
            width,
            me,
            dirs.at[k],
            dirs.at[k, me],
            dir_send.at[k],
            dir_recv.at[k],
            dir_pair.at[k],
        )
        relays.append(relay)
        relay.start()
        to_owners(
            k,
            project(image),
            [wide_sum(direction * image), wide_sum(residual * image), wide_sum(image * image)],
        )
        relay.relay_lines()
        only_owners(functools.partial(later_answer, k))
        relay.relay_plane()
        relay.finish()
        twice = multiplied(k, image)
        await_answer(k)
        size = ans[k, :, lanes, :]
        rz = ans[k, :, lanes + 1, :]
        ratio = rz / all_rz[...]
        all_rz[...] = rz
        solution = solution + size * direction
        residual = residual - size * image
        applied = applied - size * twice
        fresh, fresh_image = preconditioned(joined(ans[k]), residual, applied)
        direction = fresh + ratio * direction
        image = fresh_image + ratio * image
    size = all_rz[...] / last_sums(direction * image)
    solution = solution + size * direction
    residual = residual - size * image
    sol_ref[...] = solution
    res_ref[...] = residual
    for relay in relays:
        relay.finish_sends()
    for k in range(ITERS - 1):
        finish_put(k)
        finish_answer(k)


def solve_cg(tile, targets_t, wide_factor, zed, inverse, proj, image, squares, n, width):
    rhs_count, row_count = targets_t.shape
    owners = min(n // 2, rhs_count)
    per = rhs_count // owners
    order = wide_factor.shape[1]
    rows = -(-(order // LANES + 3) // 8) * 8
    vmem = pl.BlockSpec(memory_space=pltpu.VMEM)
    f32 = jnp.float32
    return pl.pallas_call(
        functools.partial(cg_kernel, n, width, owners),
        out_shape=[jax.ShapeDtypeStruct((rhs_count, row_count), f32)] * 2,
        in_specs=[vmem] * 8,
        out_specs=[vmem] * 2,
        scratch_shapes=[
            pltpu.VMEM((ITERS - 1, n, rhs_count, row_count), f32),
            pltpu.VMEM((ITERS - 1, rhs_count, rows, LANES), f32),
            pltpu.VMEM((ITERS - 1, n - 1, per, rows, LANES), f32),
            pltpu.VMEM((ITERS - 1, rhs_count, rows, LANES), f32),
            pltpu.VMEM((per, order), f32),
            pltpu.VMEM((per, LANES), f32),
            pltpu.VMEM((per, LANES), f32),
            pltpu.VMEM((rhs_count, LANES), f32),
            pltpu.VMEM((n, 8, LANES), f32),
            pltpu.VMEM((24, order), f32),
            pltpu.VMEM((3,) + wide_factor.shape, jnp.bfloat16),
            pltpu.VMEM((3,) + wide_factor.shape, jnp.bfloat16),
            pltpu.SemaphoreType.DMA((ITERS - 1,)),
            pltpu.SemaphoreType.DMA((ITERS - 1, n // 2)),
            pltpu.SemaphoreType.DMA((ITERS - 1,)),
        ]
        + [pltpu.SemaphoreType.DMA((ITERS - 1,))] * 4
        + [pltpu.SemaphoreType.DMA] * 2,
        compiler_params=pltpu.CompilerParams(
            collective_id=2, has_side_effects=True, vmem_limit_bytes=60 * 2**20
        ),
        name="conjugate_gradients",
    )(tile, targets_t, wide_factor, zed, inverse, proj, image, squares)


def finish_kernel(wide_ref, solution_ref, residual_ref, factor_ref, solution_out, residual_out):
    factor_ref[...] = wide_ref[...].astype(jnp.bfloat16)
    solution_out[...] = solution_ref[...]
    residual_out[...] = residual_ref[...]


def finish(wide, solution_t, residual_t):
    vmem = pl.BlockSpec(memory_space=pltpu.VMEM)
    flat = jax.ShapeDtypeStruct(solution_t.shape, jnp.float32)
    return pl.pallas_call(
        finish_kernel,
        out_shape=[jax.ShapeDtypeStruct(wide.shape, jnp.bfloat16), flat, flat],
        in_specs=[vmem] * 3,
        out_specs=[vmem] * 3,
        name="finish_outputs",
    )(wide, solution_t, residual_t)


def per_device(n, width, points, targets, pivots):
    targets_t = targets.T
    all_points, picked = gather_all(points, pivots, n, width)
    inverse, all_targets = pivot_inverse(picked, targets_t, n, width)
    wide, tile, gram, proj, zed, image, squares = sweep(
        all_points, all_targets, picked, inverse, n, width
    )
    solution_t, residual_t = solve_cg(
        tile, targets_t, wide, zed, gram_inverse(gram), proj, image, squares, n, width
    )
    factor, solution_t, residual_t = finish(wide, solution_t, residual_t)
    return (factor, solution_t.T, residual_t.T)


def solution(mesh):
    n, width = mesh.size, mesh.shape["col"]
    return jax.shard_map(
        functools.partial(per_device, n, width),
        mesh=mesh,
        in_specs=(P(("blk", "col"), None), P(("blk", "col"), None), P()),
        out_specs=(P(("blk", "col"), None), P(("blk", "col"), None), P(("blk", "col"), None)),
        check_vma=False,
    )
```

```python
import functools

import jax
import jax.numpy as jnp
from jax import lax
from jax.experimental import pallas as pl
from jax.experimental.pallas import tpu as pltpu
from jax.sharding import PartitionSpec as P

FEATURES = 128
ITERS = 3
LANES = 128


noise_level = 0.5
jitter_level = 0.05
highest = lax.Precision.HIGHEST
MESH = pl.DeviceIdType.MESH


def dot_t(left, right):
    return lax.dot_general(
        left,
        right,
        (((1,), (1,)), ((), ())),
        precision=highest,
        preferred_element_type=jnp.float32,
    )


def pieces(values):
    high = values.astype(jnp.bfloat16)
    rest = values - high.astype(jnp.float32)
    middle = rest.astype(jnp.bfloat16)
    low = (rest - middle.astype(jnp.float32)).astype(jnp.bfloat16)
    return high, middle, low


def split_dot(stacked, refs, side):
    step = stacked.shape[0] // 3
    parts = [
        lax.dot_general(
            stacked[: (3 - k) * step],
            refs[k],
            (((1,), (side,)), ((), ())),
            preferred_element_type=jnp.float32,
        )
        for k in range(3)
    ]
    total = parts[0][2 * step :] + parts[1][step : 2 * step] + parts[2]
    return parts[0][:step] + (parts[0][step : 2 * step] + parts[1][:step] + total)


def stack(values):
    return jnp.concatenate(pieces(values), axis=0)


def column_norms(point_rows):
    wide_rows = point_rows.astype(jnp.float32)
    return jnp.sum(wide_rows * wide_rows, axis=1, keepdims=True)


def row_norms(point_rows):
    wide_rows = point_rows.astype(jnp.float32)
    return dot_t(jnp.ones((8, wide_rows.shape[1]), jnp.float32), wide_rows * wide_rows)[0:1]


def kernel_block(left_rows, left_norms, right_rows, right_norms):
    inner = lax.dot_general(
        left_rows, right_rows, (((1,), (1,)), ((), ())), preferred_element_type=jnp.float32
    )
    distance = left_norms + right_norms - 2.0 * inner
    return jnp.exp(-2.0 * distance / FEATURES)


def lower_inverse_rows(rows):
    count = len(rows)
    group = max(count // 2, 1)
    lane = lax.broadcasted_iota(jnp.int32, (8, LANES), 1)
    sub = lax.broadcasted_iota(jnp.int32, (8, LANES), 0)

    def full_of(values):
        return jnp.broadcast_to(values, (8, LANES))

    def columns(row, base):
        return [full_of(row[:, base + c : base + c + 1]) for c in range(8)]

    rows = list(rows)
    done = []
    for start in range(0, count, group):
        end = start + group
        whole = []
        ahead = columns(rows[start], 8 * start)
        pivot = full_of(ahead[0][0:1])
        for p in range(start, end):
            base = 8 * p
            inside = (lane >= base) & (lane < base + 8)
            cols = ahead
            forward = jnp.where(inside, jnp.where(lane == sub + base, 1.0, 0.0), rows[p])
            pivots = jnp.ones((8, LANES), jnp.float32)
            recips, spread_rows, coefs = [], [], []
            more = p + 1 < end
            if more:
                own = columns(rows[p + 1], base)
                ahead = columns(rows[p + 1], base + 8)
                following = jnp.where(inside, 0.0, rows[p + 1])
            for j in range(8):
                recip = 1.0 / pivot
                pivots = jnp.where(sub == j, pivot, pivots)
                coef = {c: full_of(cols[c][j : j + 1]) for c in range(j + 1, 8)}
                if j < 7:
                    square = full_of(cols[j][j + 1 : j + 2]) * coef[j + 1]
                    pivot = full_of(cols[j + 1][j + 1 : j + 2]) - square * recip
                elif more:
                    corner = full_of(own[7][0:1])
                    pivot = full_of(ahead[0][0:1]) - corner * corner * recip
                scaled = cols[j] * recip
                below = jnp.where(sub > j, scaled, 0.0)
                spread_row = full_of(forward[j : j + 1])
                forward = forward - below * spread_row
                for c in range(j + 1, 8):
                    cols[c] = cols[c] - scaled * coef[c]
                if more:
                    multiplier = own[j] * recip
                    for c in range(j + 1, 8):
                        own[c] = own[c] - multiplier * coef[c]
                    for c in range(8):
                        ahead[c] = ahead[c] - multiplier * full_of(own[j][c : c + 1])
                    following = following - multiplier * spread_row
                recips.append(recip)
                spread_rows.append(spread_row)
                coefs.append(coef)
            scaled = forward * lax.rsqrt(pivots)
            lower = lane <= sub + base
            done.append(jnp.where(lower, scaled, 0.0))
            whole.append(jnp.where(lower | (lane >= 8 * end), scaled, 0.0))
            if more:
                rows[p + 1] = following
            for v in range(p + 2, end):
                own_v = columns(rows[v], base)
                new = jnp.where(inside, 0.0, rows[v])
                for j in range(8):
                    multiplier = own_v[j] * recips[j]
                    new = new - multiplier * spread_rows[j]
                    for c in range(j + 1, 8):
                        own_v[c] = own_v[c] - multiplier * coefs[j][c]
                rows[v] = new
        if end < count:
            side = jnp.concatenate(whole, axis=0)
            both = lax.dot_general(side, side, (((0,), (0,)), ((), ())), precision=highest, preferred_element_type=jnp.float32)
            inside = (lane >= 8 * start) & (lane < 8 * end)
            for v in range(end, count):
                rows[v] = jnp.where(inside, 0.0, rows[v]) - both[8 * v : 8 * v + 8]
    return done

def invert_lower(work, out_ref, beside=None):
    order = work.shape[0]
    blocks = order // LANES
    row_at = lax.broadcasted_iota(jnp.int32, (LANES, LANES), 0)
    col_at = lax.broadcasted_iota(jnp.int32, (LANES, LANES), 1)

    def one_block(j, carry):
        at = pl.multiple_of(j * LANES, LANES)
        inverse = jnp.concatenate(
            lower_inverse_rows(
                [work[pl.ds(at + 8 * v, 8), pl.ds(at, LANES)] for v in range(LANES // 8)]
            ),
            axis=0,
        )
        work[pl.ds(at, LANES), pl.ds(at, LANES)] = jnp.where(row_at == col_at, 1.0, 0.0)

        def combine(k):
            low, high = k * LANES, (k + 1) * LANES
            side = jnp.dot(inverse, work[low:high, :], precision=highest, preferred_element_type=jnp.float32)
            out_ref[low:high, :high] = side[:, :high]
            if high < order:
                out_ref[low:high, high:] = jnp.zeros((LANES, order - high), jnp.float32)
                change = lax.dot_general(side[:, high:], side, (((0,), (0,)), ((), ())), precision=highest, preferred_element_type=jnp.float32)
                if low: work[high:, :low] -= change[:, :low]
                work[high:, low:high] = -change[:, low:high]
                work[high:, high:] -= change[:, high:]

        for k in range(blocks):
            pl.when(j == k)(functools.partial(combine, k))
        if beside is not None:
            beside(j)
        return carry

    lax.fori_loop(0, blocks, one_block, 0)


def shifted(matrix, level):
    row_at = lax.broadcasted_iota(jnp.int32, matrix.shape, 0)
    col_at = lax.broadcasted_iota(jnp.int32, matrix.shape, 1)
    return matrix + jnp.where(row_at == col_at, level, 0.0)


def pivot_kernel(
    n, width, picked_ref, targets_ref, out_ref, all_targets, work, send_sem, recv_sems, pair_sem
):
    me = here(width)
    all_targets[me] = targets_ref[...]
    relay = Relay(
        n, width, me, all_targets, all_targets.at[me], send_sem, recv_sems, pair_sem
    )
    relay.hello()
    picked = picked_ref[...].astype(jnp.bfloat16)
    work[...] = shifted(
        kernel_block(picked, column_norms(picked), picked, row_norms(picked)), jitter_level
    )

    def begin():
        relay.all_here()
        relay.start()

    def beside(j):
        pl.when(j == 0)(begin)
        pl.when(j == 1)(relay.relay_lines)
        pl.when(j == 2)(relay.relay_plane)

    invert_lower(work, out_ref, beside)
    relay.finish()
    relay.finish_sends()


def pivot_inverse(picked, targets_t, n, width):
    order = picked.shape[0]
    vmem = pl.BlockSpec(memory_space=pltpu.VMEM)
    f32 = jnp.float32
    return pl.pallas_call(
        functools.partial(pivot_kernel, n, width),
        out_shape=[
            jax.ShapeDtypeStruct((order, order), f32),
            jax.ShapeDtypeStruct((n,) + targets_t.shape, f32),
        ],
        in_specs=[vmem] * 2,
        out_specs=[vmem] * 2,
        scratch_shapes=[
            pltpu.VMEM((order, order), f32),
            pltpu.SemaphoreType.DMA,
            pltpu.SemaphoreType.DMA((n // 2,)),
            pltpu.SemaphoreType.DMA((width,)),
        ],
        compiler_params=pltpu.CompilerParams(collective_id=3, has_side_effects=True),
        name="pivot_inverse",
    )(picked, targets_t)


def gram_kernel(gram_ref, split_ref, work, out_ref):
    work[...] = shifted(gram_ref[...], noise_level)
    invert_lower(work, out_ref)
    for k, piece in enumerate(pieces(out_ref[...])):
        split_ref[k] = piece


def gram_inverse(gram):
    vmem = pl.BlockSpec(memory_space=pltpu.VMEM)
    return pl.pallas_call(
        gram_kernel,
        out_shape=jax.ShapeDtypeStruct((3,) + gram.shape, jnp.bfloat16),
        in_specs=[vmem],
        out_specs=vmem,
        scratch_shapes=[pltpu.VMEM(gram.shape, jnp.float32)] * 2,
        name="gram_inverse",
    )(gram)


def here(width):
    return lax.axis_index("blk") * width + lax.axis_index("col")


def coords(index, width):
    return (lax.div(index, width), lax.rem(index, width))


def hello(n, width, me):
    barrier = pltpu.get_barrier_semaphore()

    def one(i, carry):
        peer = lax.rem(me + i, n)
        pl.semaphore_signal(
            barrier, inc=1, device_id=coords(peer, width), device_id_type=MESH
        )
        return carry

    lax.fori_loop(1, n, one, 0)


def all_here(n):
    pl.semaphore_wait(pltpu.get_barrier_semaphore(), n - 1)


def spread(n, width, me, src, dst, send_sem, recv_sem):
    def push(i, carry):
        peer = lax.rem(me + i, n)
        pltpu.make_async_remote_copy(
            src_ref=src(peer, i),
            dst_ref=dst(peer, i),
            send_sem=send_sem,
            recv_sem=recv_sem,
            device_id=coords(peer, width),
            device_id_type=MESH,
        ).start()
        return carry

    lax.fori_loop(1, n, push, 0)


def drain(ref, sem):
    pltpu.make_async_copy(ref, ref, sem).wait()


def flip(index, bits):
    moved = index
    weight = 1
    while weight <= bits:
        if bits & weight:
            moved = moved + weight * (1 - 2 * lax.rem(lax.div(index, weight), 2))
        weight *= 2
    return moved


class Relay:
    def __init__(self, n, width, me, blocks, own, send_sem, recv_sems, pair_sems):
        self.n, self.width, self.me = n, width, me
        self.blocks, self.own = blocks, own
        self.send_sem, self.recv_sems, self.pair_sems = send_sem, recv_sems, pair_sems
        self.plane = 2 * width
        self.lines = n // self.plane

    def hello(self):
        barrier = pltpu.get_barrier_semaphore()

        def signal(peer):
            pl.semaphore_signal(
                barrier, inc=1, device_id=coords(peer, self.width), device_id_type=MESH
            )

        def along(i, carry):
            signal(lax.rem(self.me + self.plane * i, self.n))
            return carry

        lax.fori_loop(1, self.lines, along, 0)
        for q in range(2, self.plane, 2):
            signal(flip(self.me, q))
        signal(flip(self.me, 1))

    def all_here(self):
        pl.semaphore_wait(
            pltpu.get_barrier_semaphore(), self.lines - 1 + self.plane // 2
        )

    def send(self, src_ref, source, peer, recv_sem):
        pltpu.make_async_remote_copy(
            src_ref=src_ref,
            dst_ref=self.blocks.at[source],
            send_sem=self.send_sem,
            recv_sem=recv_sem,
            device_id=coords(peer, self.width),
            device_id_type=MESH,
        ).start()

    def fan(self, src_ref, source, i):
        for q in range(2, self.plane, 2):
            sem = self.recv_sems.at[self.lines * (q // 2) + i]
            self.send(src_ref, source, flip(self.me, q), sem)
        self.send(src_ref, source, flip(self.me, 1), self.pair_sems.at[0])

    def start(self):
        def along(i, carry):
            peer = lax.rem(self.me + self.plane * i, self.n)
            self.send(self.own, self.me, peer, self.recv_sems.at[i])
            return carry

        lax.fori_loop(1, self.lines, along, 0)
        self.fan(self.own, self.me, 0)

    def relay_lines(self):
        def one(i, carry):
            source = lax.rem(self.me - self.plane * i + self.n, self.n)
            drain(self.blocks.at[source], self.recv_sems.at[i])
            self.fan(self.blocks.at[source], source, i)
            return carry

        lax.fori_loop(1, self.lines, one, 0)

    def relay_plane(self, *offsets):
        for q in offsets or range(2, self.plane, 2):

            def one(i, carry, q=q):
                source = lax.rem(flip(self.me, q) - self.plane * i + self.n, self.n)
                ref = self.blocks.at[source]
                drain(ref, self.recv_sems.at[self.lines * (q // 2) + i])
                self.send(ref, source, flip(self.me, 1), self.pair_sems.at[q // 2])
                return carry

            lax.fori_loop(0, self.lines, one, 0)

    def finish(self, *offsets):
        for q in offsets or range(0, self.plane, 2):
            drain(self.blocks.at[pl.ds(0, self.lines)], self.pair_sems.at[q // 2])

    def finish_sends(self):
        drain(self.blocks.at[pl.ds(0, self.n - 1)], self.send_sem)


def gather_kernel(
    n,
    width,
    points_ref,
    pivots_ref,
    all_points,
    picked_ref,
    send_sem,
    recv_sems,
    pair_sem,
    own_sem,
):
    me = here(width)
    relay = Relay(n, width, me, all_points, points_ref, send_sem, recv_sems, pair_sem)
    relay.hello()
    keep = pltpu.make_async_copy(points_ref, all_points.at[me], own_sem)
    keep.start()
    rows = points_ref.shape[0]
    order = picked_ref.shape[0]
    pivots = pivots_ref[...].astype(jnp.float32)
    in_row = jnp.concatenate([pivots[k : k + 1] for k in range(pivots.shape[0])], axis=1)
    in_column = jnp.broadcast_to(in_row, (8, order)).T
    chosen = jnp.broadcast_to(in_column[:, 0:1], (order, rows))
    row_at = lax.broadcasted_iota(jnp.int32, (order, rows), 1).astype(jnp.float32)
    together = min(4, relay.lines)
    picked_ref[...] = jnp.zeros_like(picked_ref)
    relay.all_here()
    relay.start()

    def pick(group):
        def one(i, carry):
            sources = [group + relay.plane * (together * i + t) for t in range(together)]
            hits = [
                jnp.where(chosen - (rows * source).astype(jnp.float32) == row_at, 1.0, 0.0).astype(jnp.bfloat16)
                for source in sources
            ]
            found = jnp.concatenate([all_points[source] for source in sources], axis=0)
            picked_ref[...] += jnp.dot(
                jnp.concatenate(hits, axis=1), found, preferred_element_type=jnp.float32
            )
            return carry

        lax.fori_loop(0, relay.lines // together, one, 0)

    def low(bits):
        return lax.rem(flip(me, bits), relay.plane)

    relay.relay_lines()
    keep.wait()
    pick(low(0))
    for q in range(2, relay.plane, 2):
        relay.relay_plane(q)
        pick(low(q))
    for q in range(0, relay.plane, 2):
        relay.finish(q)
        pick(low(q + 1))
    relay.finish_sends()


def gather_all(points, pivots, n, width):
    vmem = pl.BlockSpec(memory_space=pltpu.VMEM)
    order = pivots.shape[0] * pivots.shape[1]
    return pl.pallas_call(
        functools.partial(gather_kernel, n, width),
        out_shape=[
            jax.ShapeDtypeStruct((n,) + points.shape, points.dtype),
            jax.ShapeDtypeStruct((order, points.shape[1]), jnp.float32),
        ],
        in_specs=[vmem] * 2,
        out_specs=[vmem] * 2,
        scratch_shapes=[
            pltpu.SemaphoreType.DMA,
            pltpu.SemaphoreType.DMA((n // 2,)),
            pltpu.SemaphoreType.DMA((width,)),
            pltpu.SemaphoreType.DMA,
        ],
        compiler_params=pltpu.CompilerParams(collective_id=0, has_side_effects=True),
        name="gather_points",
    )(points, pivots)


def sweep_kernel(
    n,
    width,
    points_ref,
    targets_ref,
    picked_ref,
    inverse_ref,
    wide_ref,
    tile_ref,
    gram_ref,
    proj_ref,
    zed_ref,
    image_ref,
    square_ref,
    left_part,
    right_part,
    left_got,
    right_got,
    crossed,
    send_sem,
    recv_sem,
):
    me = here(width)
    core, pair = lax.rem(me, 2), lax.div(me, 2)
    other = 1 - core
    partner = flip(me, 1)
    barrier = pltpu.get_barrier_semaphore()
    pl.semaphore_signal(barrier, inc=1, device_id=coords(partner, width), device_id_type=MESH)
    order = inverse_ref.shape[0]
    half = order // 2
    chunk = min(4, n // 2)
    picked = picked_ref[...].astype(jnp.bfloat16)
    picked_column = column_norms(picked)
    own = points_ref[pair, core]
    beside = points_ref[pair, other]
    own_column, beside_column = column_norms(own), column_norms(beside)
    own_targets = targets_ref[pair, core]
    image_ref[...] = noise_level * own_targets
    square_ref[...] = jnp.zeros_like(square_ref)
    for ref in (left_part, right_part):
        ref[...] = jnp.zeros_like(ref)

    steps = n // 2 // chunk

    def cross_of(i):
        at = i * chunk
        near = jnp.concatenate([points_ref[at + t, core] for t in range(chunk)], axis=0)
        return kernel_block(picked, picked_column, near, row_norms(near))

    crossed[...] = cross_of(0)

    def step(i, carry):
        at = i * chunk
        cross = crossed[...]
        near = jnp.concatenate([points_ref[at + t, core] for t in range(chunk)], axis=0)
        far = jnp.concatenate([points_ref[at + t, other] for t in range(chunk)], axis=0)
        near_targets = jnp.concatenate([targets_ref[at + t, core] for t in range(chunk)], axis=1)
        far_targets = jnp.concatenate([targets_ref[at + t, other] for t in range(chunk)], axis=1)
        near_row, far_row = row_norms(near), row_norms(far)
        own_near = kernel_block(own, own_column, near, near_row)
        own_far = kernel_block(own, own_column, far, far_row)
        beside_near = kernel_block(beside, beside_column, near, near_row)
        size = own.shape[0]
        for t in range(chunk):
            tile_ref[at + t, core] = own_near[:, t * size : (t + 1) * size]
            tile_ref[at + t, other] = own_far[:, t * size : (t + 1) * size]
        first = jnp.dot(
            inverse_ref[:, :half],
            cross[:half],
            precision=highest,
            preferred_element_type=jnp.float32,
        )
        top = first[:half]
        low = first[half:] + jnp.dot(
            inverse_ref[half:, half:],
            cross[half:],
            precision=highest,
            preferred_element_type=jnp.float32,
        )
        crossed[...] = cross_of(jnp.minimum(i + 1, steps - 1))
        extra = [own_near, beside_near, near_targets]
        left_part[...] += dot_t(jnp.concatenate([top] + extra, axis=0), top)
        right_part[...] += dot_t(jnp.concatenate([top, low] + extra, axis=0), low)
        image_ref[...] += split_dot(
            stack(jnp.concatenate([near_targets, far_targets], axis=1)),
            pieces(jnp.concatenate([own_near, own_far], axis=1)),
            1,
        )
        squares = near_targets * near_targets + far_targets * far_targets
        for t in range(chunk):
            square_ref[...] += squares[:, t * size : (t + 1) * size]

        @pl.when(i == lax.div(pair, chunk))
        def _():
            for t in range(chunk):

                @pl.when(lax.rem(pair, chunk) == t)
                def _(t=t):
                    for rows, value in ((slice(0, half), top), (slice(half, order), low)):
                        wide_ref[:, rows] = value[:, t * size : (t + 1) * size].T

        return carry

    lax.fori_loop(0, steps, step, 0)
    pl.semaphore_wait(barrier, 1)
    size = own.shape[0]
    sides = [(left_part, left_got, half, 0), (right_part, right_got, order, half)]
    copies = []
    for part, got, tall, _ in sides:
        for rows in (pl.ds(0, tall), pl.ds(tall + size, part.shape[0] - tall - size)):
            copy = pltpu.make_async_remote_copy(
                src_ref=part.at[rows],
                dst_ref=got.at[rows],
                send_sem=send_sem.at[len(copies)],
                recv_sem=recv_sem.at[len(copies)],
                device_id=coords(partner, width),
                device_id_type=MESH,
            )
            copy.start()
            copies.append(copy)
    square_ref[...] = jnp.broadcast_to(
        jnp.sum(square_ref[...], axis=1, keepdims=True), square_ref.shape
    )
    gram_ref[half:, :half] = jnp.zeros((order - half, half), jnp.float32)
    for copy in copies:
        copy.wait_recv()
    for part, got, tall, at in sides:
        lanes = slice(at, at + part.shape[1])
        gram_ref[:tall, lanes] = part[:tall] + got[:tall]
        zed_ref[:, lanes] = (
            noise_level * wide_ref[:, lanes]
            + part[tall : tall + size]
            + got[tall + size : tall + 2 * size]
        )
        proj_ref[:, lanes] = part[tall + 2 * size :] + got[tall + 2 * size :]
    for copy in copies:
        copy.wait_send()


def sweep(all_points, all_targets, picked, inverse, n, width):
    rows, rhs_count, order = all_points.shape[1], all_targets.shape[1], picked.shape[0]
    vmem = pl.BlockSpec(memory_space=pltpu.VMEM)
    f32 = jnp.float32
    half = order // 2
    extra = 2 * rows + rhs_count
    partial = [
        pltpu.VMEM((half + extra, half), f32),
        pltpu.VMEM((order + extra, order - half), f32),
    ]
    wide, tile, *rest = pl.pallas_call(
        functools.partial(sweep_kernel, n, width),
        out_shape=[
            jax.ShapeDtypeStruct(shape, dtype)
            for shape, dtype in [
                ((rows, order), f32),
                ((n // 2, 2, rows, rows), f32),
                ((order, order), f32),
                ((rhs_count, order), f32),
                ((rows, order), f32),
                ((rhs_count, rows), f32),
                ((rhs_count, rows), f32),
            ]
        ],
        in_specs=[vmem] * 4,
        out_specs=[vmem] * 7,
        scratch_shapes=partial * 2
        + [pltpu.VMEM((order, min(4, n // 2) * rows), f32)]
        + [pltpu.SemaphoreType.DMA((4,))] * 2,
        compiler_params=pltpu.CompilerParams(
            collective_id=1, has_side_effects=True, vmem_limit_bytes=60 * 2**20
        ),
        name="sweep_points",
    )(
        all_points.reshape((n // 2, 2) + all_points.shape[1:]),
        all_targets.reshape((n // 2, 2) + all_targets.shape[1:]),
        picked,
        inverse,
    )
    return [wide, tile.reshape(n, rows, rows)] + rest


def cg_kernel(
    n,
    width,
    owners,
    tile_ref,
    rhs_ref,
    wide_ref,
    zed_ref,
    inverse_ref,
    proj_ref,
    image_ref,
    square_ref,
    sol_ref,
    res_ref,
    dirs,
    put,
    got,
    ans,
    kept_proj,
    kept_squares,
    kept_rz,
    all_rz,
    ends,
    narrow,
    wide_split,
    zed_split,
    dir_send,
    dir_recv,
    dir_pair,
    put_send,
    put_recv,
    ans_send,
    ans_recv,
    end_send,
    end_recv,
):
    me = here(width)
    rhs_count, row_count = rhs_ref.shape
    per = rhs_count // owners
    order = wide_ref.shape[1]
    lanes = order // LANES
    first_owner = (n - owners) // 2
    rank = me - first_owner
    owning = (rank >= 0) & (rank < owners)
    own_rows = pl.ds(rank * per, per)
    hello(n, width, me)

    def only_owners(body):
        pl.when(owning)(body)

    def wide_sum(values):
        return jnp.broadcast_to(jnp.sum(values, axis=1, keepdims=True), (values.shape[0], LANES))

    def to_owners(k, proj, sums):
        for q in range(lanes):
            put[k, :, q, :] = proj[:, q * LANES : (q + 1) * LANES]
        for s, value in enumerate(sums):
            put[k, :, lanes + s, :] = value

        def push(i, carry):
            turn = lax.rem(me + i, owners)
            peer = first_owner + turn

            @pl.when(peer != me)
            def _():
                pltpu.make_async_remote_copy(
                    src_ref=put.at[k, pl.ds(turn * per, per)],
                    dst_ref=got.at[k, lax.rem(me - peer + n, n) - 1],
                    send_sem=put_send.at[k],
                    recv_sem=put_recv.at[k],
                    device_id=coords(peer, width),
                    device_id_type=MESH,
                ).start()

            return carry

        lax.fori_loop(0, owners, push, 0)

    def drain_others(ref, sem):
        @pl.when(owning)
        def _():
            drain(ref.at[pl.ds(0, (owners - 1) * per)], sem)

        @pl.when(jnp.logical_not(owning))
        def _():
            drain(ref, sem)

    def finish_put(k):
        drain_others(put.at[k], put_send.at[k])

    def collect(k):
        drain(got.at[k], put_recv.at[k])
        start = put[k, own_rows]
        return lax.fori_loop(0, n - 1, lambda i, acc: acc + got[k, i], start)

    def answer(k, rows):
        for s, value in enumerate(rows):
            ans[k, own_rows, s, :] = value
        spread(
            n,
            width,
            me,
            lambda peer, i: ans.at[k, own_rows],
            lambda peer, i: ans.at[k, own_rows],
            ans_send.at[k],
            ans_recv.at[k],
        )

    def await_answer(k):
        drain_others(ans.at[k], ans_recv.at[k])

    def finish_answer(k):
        def body():
            def one(i, carry):
                drain(ans.at[k, pl.ds(0, per)], ans_send.at[k])
                return carry

            lax.fori_loop(1, n, one, 0)

        only_owners(body)

    def solve(proj):
        def stacked(values):
            if values.shape[0] % 16 == 0:
                return stack(values)
            for t, piece in enumerate(pieces(values)):
                narrow[8 * t : 8 * t + values.shape[0], :] = piece.astype(jnp.float32)
            return narrow[...].astype(jnp.bfloat16)

        count = proj.shape[0]
        half = split_dot(stacked(proj), inverse_ref, 1)[:count]
        coef = split_dot(stacked(half), inverse_ref, 0)[:count]
        return coef, wide_sum(half * half)

    def split(row):
        return [row[:, q * LANES : (q + 1) * LANES] for q in range(lanes)]

    def project(rows):
        return split_dot(stack(rows), wide_split, 0)

    def joined(packed):
        return jnp.concatenate([packed[:, q, :] for q in range(lanes)], axis=1)

    def preconditioned(coef, residual, applied):
        stacked = stack(coef)
        direction = (residual - split_dot(stacked, wide_split, 1)) * (1.0 / noise_level)
        image = (applied - split_dot(stacked, zed_split, 1)) * (1.0 / noise_level)
        return direction, image

    def multiplied(k, image):
        def one(j, acc):
            return acc + dot_t(dirs[k, j], tile_ref[j])

        return lax.fori_loop(0, n, one, noise_level * image, unroll=4)

    narrow[...] = jnp.zeros_like(narrow)
    for split_ref, ref in ((wide_split, wide_ref), (zed_split, zed_ref)):
        for t, piece in enumerate(pieces(ref[...])):
            split_ref[t] = piece
    residual = rhs_ref[...]
    applied = image_ref[...]
    solution = jnp.zeros_like(residual)
    coef, covered = solve(proj_ref[...])
    all_rz[...] = (square_ref[...] - covered) * (1.0 / noise_level)
    direction, image = preconditioned(coef, residual, applied)

    def keep_own():
        for t in range(per):
            row = pl.ds(rank * per + t, 1)
            kept_proj[t : t + 1, :] = proj_ref[row, :]
            kept_squares[t : t + 1, :] = square_ref[row, :]
            kept_rz[t : t + 1, :] = all_rz[row, :]

    only_owners(keep_own)
    all_here(n)

    def later_answer(k):
        total = collect(k)
        size = kept_rz[...] / total[:, lanes, :]
        along, image_squares = total[:, lanes + 1, :], total[:, lanes + 2, :]
        size_row = jnp.concatenate([size] * lanes, axis=1)
        proj = kept_proj[...] - size_row * joined(total)
        squares = kept_squares[...] - 2.0 * size * along + size * size * image_squares
        coef, covered = solve(proj)
        rz = (squares - covered) * (1.0 / noise_level)
        kept_proj[...] = proj
        kept_squares[...] = squares
        kept_rz[...] = rz
        answer(k, split(coef) + [size, rz])

    def last_sums(values):
        ends[me, 0:1, 0:rhs_count] = dot_t(jnp.ones((8, row_count), jnp.float32), values)[0:1]
        spread(
            n,
            width,
            me,
            lambda peer, i: ends.at[me, pl.ds(0, 1)],
            lambda peer, i: ends.at[me, pl.ds(0, 1)],
            end_send,
            end_recv,
        )
        others = ends.at[pl.ds(0, n - 1), pl.ds(0, 1)]
        drain(others, end_recv)
        total = lax.fori_loop(1, n, lambda i, acc: acc + ends[i, 0:1, :], ends[0, 0:1, :])
        lane_at = lax.broadcasted_iota(jnp.int32, (rhs_count, LANES), 1)
        row_at = lax.broadcasted_iota(jnp.int32, (rhs_count, LANES), 0)
        spread_out = jnp.broadcast_to(total, (rhs_count, LANES))
        drain(others, end_send)
        return wide_sum(jnp.where(lane_at == row_at, spread_out, 0.0))

    relays = []
    for k in range(ITERS - 1):
        dirs[k, me] = image
        relay = Relay(
            n,
            width,
            me,
            dirs.at[k],
            dirs.at[k, me],
            dir_send.at[k],
            dir_recv.at[k],
            dir_pair.at[k],
        )
        relays.append(relay)
        relay.start()
        to_owners(
            k,
            project(image),
            [wide_sum(direction * image), wide_sum(residual * image), wide_sum(image * image)],
        )
        relay.relay_lines()
        only_owners(functools.partial(later_answer, k))
        relay.relay_plane()
        relay.finish()
        twice = multiplied(k, image)
        await_answer(k)
        size = ans[k, :, lanes, :]
        rz = ans[k, :, lanes + 1, :]
        ratio = rz / all_rz[...]
        all_rz[...] = rz
        solution = solution + size * direction
        residual = residual - size * image
        applied = applied - size * twice
        fresh, fresh_image = preconditioned(joined(ans[k]), residual, applied)
        direction = fresh + ratio * direction
        image = fresh_image + ratio * image
    size = all_rz[...] / last_sums(direction * image)
    solution = solution + size * direction
    residual = residual - size * image
    sol_ref[...] = solution
    res_ref[...] = residual
    for relay in relays:
        relay.finish_sends()
    for k in range(ITERS - 1):
        finish_put(k)
        finish_answer(k)


def solve_cg(tile, targets_t, wide_factor, zed, inverse, proj, image, squares, n, width):
    rhs_count, row_count = targets_t.shape
    owners = min(n // 2, rhs_count)
    per = rhs_count // owners
    order = wide_factor.shape[1]
    rows = -(-(order // LANES + 3) // 8) * 8
    vmem = pl.BlockSpec(memory_space=pltpu.VMEM)
    f32 = jnp.float32
    return pl.pallas_call(
        functools.partial(cg_kernel, n, width, owners),
        out_shape=[jax.ShapeDtypeStruct((rhs_count, row_count), f32)] * 2,
        in_specs=[vmem] * 8,
        out_specs=[vmem] * 2,
        scratch_shapes=[
            pltpu.VMEM((ITERS - 1, n, rhs_count, row_count), f32),
            pltpu.VMEM((ITERS - 1, rhs_count, rows, LANES), f32),
            pltpu.VMEM((ITERS - 1, n - 1, per, rows, LANES), f32),
            pltpu.VMEM((ITERS - 1, rhs_count, rows, LANES), f32),
            pltpu.VMEM((per, order), f32),
            pltpu.VMEM((per, LANES), f32),
            pltpu.VMEM((per, LANES), f32),
            pltpu.VMEM((rhs_count, LANES), f32),
            pltpu.VMEM((n, 8, LANES), f32),
            pltpu.VMEM((24, order), f32),
            pltpu.VMEM((3,) + wide_factor.shape, jnp.bfloat16),
            pltpu.VMEM((3,) + wide_factor.shape, jnp.bfloat16),
            pltpu.SemaphoreType.DMA((ITERS - 1,)),
            pltpu.SemaphoreType.DMA((ITERS - 1, n // 2)),
            pltpu.SemaphoreType.DMA((ITERS - 1, width)),
        ]
        + [pltpu.SemaphoreType.DMA((ITERS - 1,))] * 4
        + [pltpu.SemaphoreType.DMA] * 2,
        compiler_params=pltpu.CompilerParams(
            collective_id=2, has_side_effects=True, vmem_limit_bytes=60 * 2**20
        ),
        name="conjugate_gradients",
    )(tile, targets_t, wide_factor, zed, inverse, proj, image, squares)


def finish_kernel(wide_ref, solution_ref, residual_ref, factor_ref, solution_out, residual_out):
    factor_ref[...] = wide_ref[...].astype(jnp.bfloat16)
    solution_out[...] = solution_ref[...]
    residual_out[...] = residual_ref[...]


def finish(wide, solution_t, residual_t):
    vmem = pl.BlockSpec(memory_space=pltpu.VMEM)
    flat = jax.ShapeDtypeStruct(solution_t.shape, jnp.float32)
    return pl.pallas_call(
        finish_kernel,
        out_shape=[jax.ShapeDtypeStruct(wide.shape, jnp.bfloat16), flat, flat],
        in_specs=[vmem] * 3,
        out_specs=[vmem] * 3,
        name="finish_outputs",
    )(wide, solution_t, residual_t)


def per_device(n, width, points, targets, pivots):
    targets_t = targets.T
    all_points, picked = gather_all(points, pivots, n, width)
    inverse, all_targets = pivot_inverse(picked, targets_t, n, width)
    wide, tile, gram, proj, zed, image, squares = sweep(
        all_points, all_targets, picked, inverse, n, width
    )
    solution_t, residual_t = solve_cg(
        tile, targets_t, wide, zed, gram_inverse(gram), proj, image, squares, n, width
    )
    factor, solution_t, residual_t = finish(wide, solution_t, residual_t)
    return (factor, solution_t.T, residual_t.T)


def solution(mesh):
    n, width = mesh.size, mesh.shape["col"]
    return jax.shard_map(
        functools.partial(per_device, n, width),
        mesh=mesh,
        in_specs=(P(("blk", "col"), None), P(("blk", "col"), None), P()),
        out_specs=(P(("blk", "col"), None), P(("blk", "col"), None), P(("blk", "col"), None)),
        check_vma=False,
    )
```

```python
import functools

import jax
import jax.numpy as jnp
from jax import lax
from jax.experimental import pallas as pl
from jax.experimental.pallas import tpu as pltpu
from jax.sharding import PartitionSpec as P

FEATURES = 128
ITERS = 3
LANES = 128


noise_level = 0.5
jitter_level = 0.05
highest = lax.Precision.HIGHEST
MESH = pl.DeviceIdType.MESH


def dot_t(left, right):
    return lax.dot_general(
        left,
        right,
        (((1,), (1,)), ((), ())),
        precision=highest,
        preferred_element_type=jnp.float32,
    )


def pieces(values):
    high = values.astype(jnp.bfloat16)
    rest = values - high.astype(jnp.float32)
    middle = rest.astype(jnp.bfloat16)
    low = (rest - middle.astype(jnp.float32)).astype(jnp.bfloat16)
    return high, middle, low


def split_dot(stacked, refs, side):
    step = stacked.shape[0] // 3
    parts = [
        lax.dot_general(
            stacked[: (3 - k) * step],
            refs[k],
            (((1,), (side,)), ((), ())),
            preferred_element_type=jnp.float32,
        )
        for k in range(3)
    ]
    total = parts[0][2 * step :] + parts[1][step : 2 * step] + parts[2]
    return parts[0][:step] + (parts[0][step : 2 * step] + parts[1][:step] + total)


def stack(values):
    return jnp.concatenate(pieces(values), axis=0)


def column_norms(point_rows):
    wide_rows = point_rows.astype(jnp.float32)
    return jnp.sum(wide_rows * wide_rows, axis=1, keepdims=True)


def row_norms(point_rows):
    wide_rows = point_rows.astype(jnp.float32)
    return dot_t(jnp.ones((8, wide_rows.shape[1]), jnp.float32), wide_rows * wide_rows)[0:1]


def kernel_block(left_rows, left_norms, right_rows, right_norms):
    inner = lax.dot_general(
        left_rows, right_rows, (((1,), (1,)), ((), ())), preferred_element_type=jnp.float32
    )
    distance = left_norms + right_norms - 2.0 * inner
    return jnp.exp(-2.0 * distance / FEATURES)


def lower_inverse_rows(rows):
    count = len(rows)
    group = max(count // 2, 1)
    lane = lax.broadcasted_iota(jnp.int32, (8, LANES), 1)
    sub = lax.broadcasted_iota(jnp.int32, (8, LANES), 0)

    def full_of(values):
        return jnp.broadcast_to(values, (8, LANES))

    def columns(row, base):
        return [full_of(row[:, base + c : base + c + 1]) for c in range(8)]

    rows = list(rows)
    done = []
    for start in range(0, count, group):
        end = start + group
        whole = []
        ahead = columns(rows[start], 8 * start)
        pivot = full_of(ahead[0][0:1])
        for p in range(start, end):
            base = 8 * p
            inside = (lane >= base) & (lane < base + 8)
            cols = ahead
            forward = jnp.where(inside, jnp.where(lane == sub + base, 1.0, 0.0), rows[p])
            pivots = jnp.ones((8, LANES), jnp.float32)
            recips, spread_rows, coefs = [], [], []
            more = p + 1 < end
            if more:
                own = columns(rows[p + 1], base)
                ahead = columns(rows[p + 1], base + 8)
                following = jnp.where(inside, 0.0, rows[p + 1])
            for j in range(8):
                recip = 1.0 / pivot
                pivots = jnp.where(sub == j, pivot, pivots)
                coef = {c: full_of(cols[c][j : j + 1]) for c in range(j + 1, 8)}
                if j < 7:
                    square = full_of(cols[j][j + 1 : j + 2]) * coef[j + 1]
                    pivot = full_of(cols[j + 1][j + 1 : j + 2]) - square * recip
                elif more:
                    corner = full_of(own[7][0:1])
                    pivot = full_of(ahead[0][0:1]) - corner * corner * recip
                scaled = cols[j] * recip
                below = jnp.where(sub > j, scaled, 0.0)
                spread_row = full_of(forward[j : j + 1])
                forward = forward - below * spread_row
                for c in range(j + 1, 8):
                    cols[c] = cols[c] - scaled * coef[c]
                if more:
                    multiplier = own[j] * recip
                    for c in range(j + 1, 8):
                        own[c] = own[c] - multiplier * coef[c]
                    for c in range(8):
                        ahead[c] = ahead[c] - multiplier * full_of(own[j][c : c + 1])
                    following = following - multiplier * spread_row
                recips.append(recip)
                spread_rows.append(spread_row)
                coefs.append(coef)
            scaled = forward * lax.rsqrt(pivots)
            lower = lane <= sub + base
            done.append(jnp.where(lower, scaled, 0.0))
            whole.append(jnp.where(lower | (lane >= 8 * end), scaled, 0.0))
            if more:
                rows[p + 1] = following
            for v in range(p + 2, end):
                own_v = columns(rows[v], base)
                new = jnp.where(inside, 0.0, rows[v])
                for j in range(8):
                    multiplier = own_v[j] * recips[j]
                    new = new - multiplier * spread_rows[j]
                    for c in range(j + 1, 8):
                        own_v[c] = own_v[c] - multiplier * coefs[j][c]
                rows[v] = new
        if end < count:
            side = jnp.concatenate(whole, axis=0)
            both = lax.dot_general(side, side, (((0,), (0,)), ((), ())), precision=highest, preferred_element_type=jnp.float32)
            inside = (lane >= 8 * start) & (lane < 8 * end)
            for v in range(end, count):
                rows[v] = jnp.where(inside, 0.0, rows[v]) - both[8 * v : 8 * v + 8]
    return done

def invert_lower(work, out_ref, beside=None):
    order = work.shape[0]
    blocks = order // LANES
    row_at = lax.broadcasted_iota(jnp.int32, (LANES, LANES), 0)
    col_at = lax.broadcasted_iota(jnp.int32, (LANES, LANES), 1)

    def one_block(j, carry):
        at = pl.multiple_of(j * LANES, LANES)
        inverse = jnp.concatenate(
            lower_inverse_rows(
                [work[pl.ds(at + 8 * v, 8), pl.ds(at, LANES)] for v in range(LANES // 8)]
            ),
            axis=0,
        )
        work[pl.ds(at, LANES), pl.ds(at, LANES)] = jnp.where(row_at == col_at, 1.0, 0.0)

        def combine(k):
            low, high = k * LANES, (k + 1) * LANES
            side = jnp.dot(inverse, work[low:high, :], precision=highest, preferred_element_type=jnp.float32)
            out_ref[low:high, :high] = side[:, :high]
            if high < order:
                out_ref[low:high, high:] = jnp.zeros((LANES, order - high), jnp.float32)
                change = lax.dot_general(side[:, high:], side, (((0,), (0,)), ((), ())), precision=highest, preferred_element_type=jnp.float32)
                if low: work[high:, :low] -= change[:, :low]
                work[high:, low:high] = -change[:, low:high]
                work[high:, high:] -= change[:, high:]

        for k in range(blocks):
            pl.when(j == k)(functools.partial(combine, k))
        if beside is not None:
            beside(j)
        return carry

    lax.fori_loop(0, blocks, one_block, 0)


def shifted(matrix, level):
    row_at = lax.broadcasted_iota(jnp.int32, matrix.shape, 0)
    col_at = lax.broadcasted_iota(jnp.int32, matrix.shape, 1)
    return matrix + jnp.where(row_at == col_at, level, 0.0)


def pivot_kernel(
    n, width, picked_ref, targets_ref, out_ref, all_targets, work, send_sem, recv_sems, pair_sem
):
    me = here(width)
    all_targets[me] = targets_ref[...]
    relay = Relay(
        n, width, me, all_targets, all_targets.at[me], send_sem, recv_sems, pair_sem
    )
    relay.hello()
    picked = picked_ref[...].astype(jnp.bfloat16)
    work[...] = shifted(
        kernel_block(picked, column_norms(picked), picked, row_norms(picked)), jitter_level
    )

    def begin():
        relay.all_here()
        relay.start()

    def beside(j):
        pl.when(j == 0)(begin)
        pl.when(j == 1)(relay.relay_lines)
        pl.when(j == 2)(relay.relay_plane)

    invert_lower(work, out_ref, beside)
    relay.finish()
    relay.finish_sends()


def pivot_inverse(picked, targets_t, n, width):
    order = picked.shape[0]
    vmem = pl.BlockSpec(memory_space=pltpu.VMEM)
    f32 = jnp.float32
    return pl.pallas_call(
        functools.partial(pivot_kernel, n, width),
        out_shape=[
            jax.ShapeDtypeStruct((order, order), f32),
            jax.ShapeDtypeStruct((n,) + targets_t.shape, f32),
        ],
        in_specs=[vmem] * 2,
        out_specs=[vmem] * 2,
        scratch_shapes=[
            pltpu.VMEM((order, order), f32),
            pltpu.SemaphoreType.DMA,
            pltpu.SemaphoreType.DMA((n // 2,)),
            pltpu.SemaphoreType.DMA((width,)),
        ],
        compiler_params=pltpu.CompilerParams(collective_id=3, has_side_effects=True),
        name="pivot_inverse",
    )(picked, targets_t)


def gram_kernel(gram_ref, split_ref, work, out_ref):
    work[...] = shifted(gram_ref[...], noise_level)
    invert_lower(work, out_ref)
    for k, piece in enumerate(pieces(out_ref[...])):
        split_ref[k] = piece


def gram_inverse(gram):
    vmem = pl.BlockSpec(memory_space=pltpu.VMEM)
    return pl.pallas_call(
        gram_kernel,
        out_shape=jax.ShapeDtypeStruct((3,) + gram.shape, jnp.bfloat16),
        in_specs=[vmem],
        out_specs=vmem,
        scratch_shapes=[pltpu.VMEM(gram.shape, jnp.float32)] * 2,
        name="gram_inverse",
    )(gram)


def here(width):
    return lax.axis_index("blk") * width + lax.axis_index("col")


def coords(index, width):
    return (lax.div(index, width), lax.rem(index, width))


def hello(n, width, me):
    barrier = pltpu.get_barrier_semaphore()

    def one(i, carry):
        peer = lax.rem(me + i, n)
        pl.semaphore_signal(
            barrier, inc=1, device_id=coords(peer, width), device_id_type=MESH
        )
        return carry

    lax.fori_loop(1, n, one, 0)


def all_here(n):
    pl.semaphore_wait(pltpu.get_barrier_semaphore(), n - 1)


def spread(n, width, me, src, dst, send_sem, recv_sem):
    def push(i, carry):
        peer = lax.rem(me + i, n)
        pltpu.make_async_remote_copy(
            src_ref=src(peer, i),
            dst_ref=dst(peer, i),
            send_sem=send_sem,
            recv_sem=recv_sem,
            device_id=coords(peer, width),
            device_id_type=MESH,
        ).start()
        return carry

    lax.fori_loop(1, n, push, 0)


def drain(ref, sem):
    pltpu.make_async_copy(ref, ref, sem).wait()


def flip(index, bits):
    moved = index
    weight = 1
    while weight <= bits:
        if bits & weight:
            moved = moved + weight * (1 - 2 * lax.rem(lax.div(index, weight), 2))
        weight *= 2
    return moved


class Relay:
    def __init__(self, n, width, me, blocks, own, send_sem, recv_sems, pair_sems):
        self.n, self.width, self.me = n, width, me
        self.blocks, self.own = blocks, own
        self.send_sem, self.recv_sems, self.pair_sems = send_sem, recv_sems, pair_sems
        self.plane = 2 * width
        self.lines = n // self.plane

    def hello(self):
        barrier = pltpu.get_barrier_semaphore()

        def signal(peer):
            pl.semaphore_signal(
                barrier, inc=1, device_id=coords(peer, self.width), device_id_type=MESH
            )

        def along(i, carry):
            signal(lax.rem(self.me + self.plane * i, self.n))
            return carry

        lax.fori_loop(1, self.lines, along, 0)
        for q in range(2, self.plane, 2):
            signal(flip(self.me, q))
        signal(flip(self.me, 1))

    def all_here(self):
        pl.semaphore_wait(
            pltpu.get_barrier_semaphore(), self.lines - 1 + self.plane // 2
        )

    def send(self, src_ref, source, peer, recv_sem):
        pltpu.make_async_remote_copy(
            src_ref=src_ref,
            dst_ref=self.blocks.at[source],
            send_sem=self.send_sem,
            recv_sem=recv_sem,
            device_id=coords(peer, self.width),
            device_id_type=MESH,
        ).start()

    def fan(self, src_ref, source, i):
        for q in range(2, self.plane, 2):
            sem = self.recv_sems.at[self.lines * (q // 2) + i]
            self.send(src_ref, source, flip(self.me, q), sem)
        self.send(src_ref, source, flip(self.me, 1), self.pair_sems.at[0])

    def start(self):
        def along(i, carry):
            peer = lax.rem(self.me + self.plane * i, self.n)
            self.send(self.own, self.me, peer, self.recv_sems.at[i])
            return carry

        lax.fori_loop(1, self.lines, along, 0)
        self.fan(self.own, self.me, 0)

    def relay_lines(self):
        def one(i, carry):
            source = lax.rem(self.me - self.plane * i + self.n, self.n)
            drain(self.blocks.at[source], self.recv_sems.at[i])
            self.fan(self.blocks.at[source], source, i)
            return carry

        lax.fori_loop(1, self.lines, one, 0)

    def relay_plane(self, *offsets):
        for q in offsets or range(2, self.plane, 2):

            def one(i, carry, q=q):
                source = lax.rem(flip(self.me, q) - self.plane * i + self.n, self.n)
                ref = self.blocks.at[source]
                drain(ref, self.recv_sems.at[self.lines * (q // 2) + i])
                self.send(ref, source, flip(self.me, 1), self.pair_sems.at[q // 2])
                return carry

            lax.fori_loop(0, self.lines, one, 0)

    def finish(self, *offsets):
        for q in offsets or range(0, self.plane, 2):
            drain(self.blocks.at[pl.ds(0, self.lines)], self.pair_sems.at[q // 2])

    def finish_sends(self):
        drain(self.blocks.at[pl.ds(0, self.n - 1)], self.send_sem)


def gather_kernel(
    n,
    width,
    points_ref,
    pivots_ref,
    all_points,
    picked_ref,
    send_sem,
    recv_sems,
    pair_sem,
    own_sem,
):
    me = here(width)
    relay = Relay(n, width, me, all_points, points_ref, send_sem, recv_sems, pair_sem)
    relay.hello()
    keep = pltpu.make_async_copy(points_ref, all_points.at[me], own_sem)
    keep.start()
    rows = points_ref.shape[0]
    order = picked_ref.shape[0]
    pivots = pivots_ref[...].astype(jnp.float32)
    in_row = jnp.concatenate([pivots[k : k + 1] for k in range(pivots.shape[0])], axis=1)
    in_column = jnp.broadcast_to(in_row, (8, order)).T
    chosen = jnp.broadcast_to(in_column[:, 0:1], (order, rows))
    row_at = lax.broadcasted_iota(jnp.int32, (order, rows), 1).astype(jnp.float32)
    together = min(4, relay.lines)
    picked_ref[...] = jnp.zeros_like(picked_ref)
    relay.all_here()
    relay.start()

    def pick(group):
        def one(i, carry):
            sources = [group + relay.plane * (together * i + t) for t in range(together)]
            hits = [
                jnp.where(chosen - (rows * source).astype(jnp.float32) == row_at, 1.0, 0.0).astype(jnp.bfloat16)
                for source in sources
            ]
            found = jnp.concatenate([all_points[source] for source in sources], axis=0)
            picked_ref[...] += jnp.dot(
                jnp.concatenate(hits, axis=1), found, preferred_element_type=jnp.float32
            )
            return carry

        lax.fori_loop(0, relay.lines // together, one, 0)

    def low(bits):
        return lax.rem(flip(me, bits), relay.plane)

    relay.relay_lines()
    keep.wait()
    pick(low(0))
    for q in range(2, relay.plane, 2):
        relay.relay_plane(q)
        pick(low(q))
    for q in range(0, relay.plane, 2):
        relay.finish(q)
        pick(low(q + 1))
    relay.finish_sends()


def gather_all(points, pivots, n, width):
    vmem = pl.BlockSpec(memory_space=pltpu.VMEM)
    order = pivots.shape[0] * pivots.shape[1]
    return pl.pallas_call(
        functools.partial(gather_kernel, n, width),
        out_shape=[
            jax.ShapeDtypeStruct((n,) + points.shape, points.dtype),
            jax.ShapeDtypeStruct((order, points.shape[1]), jnp.float32),
        ],
        in_specs=[vmem] * 2,
        out_specs=[vmem] * 2,
        scratch_shapes=[
            pltpu.SemaphoreType.DMA,
            pltpu.SemaphoreType.DMA((n // 2,)),
            pltpu.SemaphoreType.DMA((width,)),
            pltpu.SemaphoreType.DMA,
        ],
        compiler_params=pltpu.CompilerParams(collective_id=0, has_side_effects=True),
        name="gather_points",
    )(points, pivots)


def sweep_kernel(
    n,
    width,
    points_ref,
    targets_ref,
    picked_ref,
    inverse_ref,
    wide_ref,
    tile_ref,
    gram_ref,
    proj_ref,
    zed_ref,
    image_ref,
    square_ref,
    left_part,
    right_part,
    left_got,
    right_got,
    crossed,
    send_sem,
    recv_sem,
):
    me = here(width)
    core, pair = lax.rem(me, 2), lax.div(me, 2)
    other = 1 - core
    partner = flip(me, 1)
    barrier = pltpu.get_barrier_semaphore()
    pl.semaphore_signal(barrier, inc=1, device_id=coords(partner, width), device_id_type=MESH)
    order = inverse_ref.shape[0]
    half = order // 2
    chunk = min(4, n // 2)
    picked = picked_ref[...].astype(jnp.bfloat16)
    picked_column = column_norms(picked)
    own = points_ref[pair, core]
    beside = points_ref[pair, other]
    own_column, beside_column = column_norms(own), column_norms(beside)
    own_targets = targets_ref[pair, core]
    image_ref[...] = noise_level * own_targets
    square_ref[...] = jnp.zeros_like(square_ref)
    for ref in (left_part, right_part):
        ref[...] = jnp.zeros_like(ref)

    steps = n // 2 // chunk

    def cross_of(i):
        at = i * chunk
        near = jnp.concatenate([points_ref[at + t, core] for t in range(chunk)], axis=0)
        return kernel_block(picked, picked_column, near, row_norms(near))

    crossed[...] = cross_of(0)

    def step(i, carry):
        at = i * chunk
        cross = crossed[...]
        near = jnp.concatenate([points_ref[at + t, core] for t in range(chunk)], axis=0)
        far = jnp.concatenate([points_ref[at + t, other] for t in range(chunk)], axis=0)
        near_targets = jnp.concatenate([targets_ref[at + t, core] for t in range(chunk)], axis=1)
        far_targets = jnp.concatenate([targets_ref[at + t, other] for t in range(chunk)], axis=1)
        near_row, far_row = row_norms(near), row_norms(far)
        own_near = kernel_block(own, own_column, near, near_row)
        own_far = kernel_block(own, own_column, far, far_row)
        beside_near = kernel_block(beside, beside_column, near, near_row)
        size = own.shape[0]
        for t in range(chunk):
            tile_ref[at + t, core] = own_near[:, t * size : (t + 1) * size]
            tile_ref[at + t, other] = own_far[:, t * size : (t + 1) * size]
        first = jnp.dot(
            inverse_ref[:, :half],
            cross[:half],
            precision=highest,
            preferred_element_type=jnp.float32,
        )
        top = first[:half]
        low = first[half:] + jnp.dot(
            inverse_ref[half:, half:],
            cross[half:],
            precision=highest,
            preferred_element_type=jnp.float32,
        )
        crossed[...] = cross_of(jnp.minimum(i + 1, steps - 1))
        extra = [own_near, beside_near, near_targets]
        left_part[...] += dot_t(jnp.concatenate([top] + extra, axis=0), top)
        right_part[...] += dot_t(jnp.concatenate([top, low] + extra, axis=0), low)
        image_ref[...] += split_dot(
            stack(jnp.concatenate([near_targets, far_targets], axis=1)),
            pieces(jnp.concatenate([own_near, own_far], axis=1)),
            1,
        )
        squares = near_targets * near_targets + far_targets * far_targets
        for t in range(chunk):
            square_ref[...] += squares[:, t * size : (t + 1) * size]

        @pl.when(i == lax.div(pair, chunk))
        def _():
            for t in range(chunk):

                @pl.when(lax.rem(pair, chunk) == t)
                def _(t=t):
                    for rows, value in ((slice(0, half), top), (slice(half, order), low)):
                        wide_ref[:, rows] = value[:, t * size : (t + 1) * size].T

        return carry

    lax.fori_loop(0, steps, step, 0)
    pl.semaphore_wait(barrier, 1)
    size = own.shape[0]
    sides = [(left_part, left_got, half, 0), (right_part, right_got, order, half)]
    copies = []
    for part, got, tall, _ in sides:
        for rows in (pl.ds(0, tall), pl.ds(tall + size, part.shape[0] - tall - size)):
            copy = pltpu.make_async_remote_copy(
                src_ref=part.at[rows],
                dst_ref=got.at[rows],
                send_sem=send_sem.at[len(copies)],
                recv_sem=recv_sem.at[len(copies)],
                device_id=coords(partner, width),
                device_id_type=MESH,
            )
            copy.start()
            copies.append(copy)
    square_ref[...] = jnp.broadcast_to(
        jnp.sum(square_ref[...], axis=1, keepdims=True), square_ref.shape
    )
    gram_ref[half:, :half] = jnp.zeros((order - half, half), jnp.float32)
    for copy in copies:
        copy.wait_recv()
    for part, got, tall, at in sides:
        lanes = slice(at, at + part.shape[1])
        gram_ref[:tall, lanes] = part[:tall] + got[:tall]
        zed_ref[:, lanes] = (
            noise_level * wide_ref[:, lanes]
            + part[tall : tall + size]
            + got[tall + size : tall + 2 * size]
        )
        proj_ref[:, lanes] = part[tall + 2 * size :] + got[tall + 2 * size :]
    for copy in copies:
        copy.wait_send()


def sweep(all_points, all_targets, picked, inverse, n, width):
    rows, rhs_count, order = all_points.shape[1], all_targets.shape[1], picked.shape[0]
    vmem = pl.BlockSpec(memory_space=pltpu.VMEM)
    f32 = jnp.float32
    half = order // 2
    extra = 2 * rows + rhs_count
    partial = [
        pltpu.VMEM((half + extra, half), f32),
        pltpu.VMEM((order + extra, order - half), f32),
    ]
    wide, tile, *rest = pl.pallas_call(
        functools.partial(sweep_kernel, n, width),
        out_shape=[
            jax.ShapeDtypeStruct(shape, dtype)
            for shape, dtype in [
                ((rows, order), f32),
                ((n // 2, 2, rows, rows), f32),
                ((order, order), f32),
                ((rhs_count, order), f32),
                ((rows, order), f32),
                ((rhs_count, rows), f32),
                ((rhs_count, rows), f32),
            ]
        ],
        in_specs=[vmem] * 4,
        out_specs=[vmem] * 7,
        scratch_shapes=partial * 2
        + [pltpu.VMEM((order, min(4, n // 2) * rows), f32)]
        + [pltpu.SemaphoreType.DMA((4,))] * 2,
        compiler_params=pltpu.CompilerParams(
            collective_id=1, has_side_effects=True, vmem_limit_bytes=60 * 2**20
        ),
        name="sweep_points",
    )(
        all_points.reshape((n // 2, 2) + all_points.shape[1:]),
        all_targets.reshape((n // 2, 2) + all_targets.shape[1:]),
        picked,
        inverse,
    )
    return [wide, tile.reshape(n, rows, rows)] + rest


def cg_kernel(
    n,
    width,
    owners,
    tile_ref,
    rhs_ref,
    wide_ref,
    zed_ref,
    inverse_ref,
    proj_ref,
    image_ref,
    square_ref,
    sol_ref,
    res_ref,
    dirs,
    put,
    got,
    ans,
    kept_proj,
    kept_squares,
    kept_rz,
    all_rz,
    ends,
    narrow,
    wide_split,
    zed_split,
    dir_send,
    dir_recv,
    dir_pair,
    put_send,
    put_recv,
    ans_send,
    ans_recv,
    end_send,
    end_recv,
):
    me = here(width)
    rhs_count, row_count = rhs_ref.shape
    per = rhs_count // owners
    order = wide_ref.shape[1]
    lanes = order // LANES
    first_owner = (n - owners) // 2
    rank = me - first_owner
    owning = (rank >= 0) & (rank < owners)
    own_rows = pl.ds(rank * per, per)
    sent = pl.ds(0, lanes + 1)
    hello(n, width, me)

    def packed_row(values):
        lane_at = lax.broadcasted_iota(jnp.int32, values[0].shape, 1)
        row = values[-1]
        for s in range(len(values) - 1):
            row = jnp.where(lane_at == s, values[s], row)
        return row

    def unpacked(row, s):
        return jnp.broadcast_to(row[:, s : s + 1], row.shape)

    def only_owners(body):
        pl.when(owning)(body)

    def wide_sum(values):
        return jnp.broadcast_to(jnp.sum(values, axis=1, keepdims=True), (values.shape[0], LANES))

    def to_owners(k, proj, sums):
        for q in range(lanes):
            put[k, :, q, :] = proj[:, q * LANES : (q + 1) * LANES]
        put[k, :, lanes, :] = packed_row(sums)

        def push(i, carry):
            turn = lax.rem(me + i, owners)
            peer = first_owner + turn

            @pl.when(peer != me)
            def _():
                pltpu.make_async_remote_copy(
                    src_ref=put.at[k, pl.ds(turn * per, per), sent],
                    dst_ref=got.at[k, lax.rem(me - peer + n, n) - 1, :, sent],
                    send_sem=put_send.at[k],
                    recv_sem=put_recv.at[k],
                    device_id=coords(peer, width),
                    device_id_type=MESH,
                ).start()

            return carry

        lax.fori_loop(0, owners, push, 0)

    def drain_others(ref, sem):
        @pl.when(owning)
        def _():
            drain(ref.at[pl.ds(0, (owners - 1) * per)], sem)

        @pl.when(jnp.logical_not(owning))
        def _():
            drain(ref, sem)

    def finish_put(k):
        drain_others(put.at[k, :, sent], put_send.at[k])

    def collect(k):
        drain(got.at[k, :, :, sent], put_recv.at[k])
        start = put[k, own_rows, : lanes + 1]
        return lax.fori_loop(0, n - 1, lambda i, acc: acc + got[k, i, :, : lanes + 1], start)

    def answer(k, rows):
        for s, value in enumerate(rows):
            ans[k, own_rows, s, :] = value
        spread(
            n,
            width,
            me,
            lambda peer, i: ans.at[k, own_rows, sent],
            lambda peer, i: ans.at[k, own_rows, sent],
            ans_send.at[k],
            ans_recv.at[k],
        )

    def await_answer(k):
        drain_others(ans.at[k, :, sent], ans_recv.at[k])

    def finish_answer(k):
        def body():
            def one(i, carry):
                drain(ans.at[k, pl.ds(0, per), sent], ans_send.at[k])
                return carry

            lax.fori_loop(1, n, one, 0)

        only_owners(body)

    def solve(proj):
        def stacked(values):
            if values.shape[0] % 16 == 0:
                return stack(values)
            for t, piece in enumerate(pieces(values)):
                narrow[8 * t : 8 * t + values.shape[0], :] = piece.astype(jnp.float32)
            return narrow[...].astype(jnp.bfloat16)

        count = proj.shape[0]
        half = split_dot(stacked(proj), inverse_ref, 1)[:count]
        coef = split_dot(stacked(half), inverse_ref, 0)[:count]
        return coef, wide_sum(half * half)

    def split(row):
        return [row[:, q * LANES : (q + 1) * LANES] for q in range(lanes)]

    def project(rows):
        return split_dot(stack(rows), wide_split, 0)

    def joined(packed):
        return jnp.concatenate([packed[:, q, :] for q in range(lanes)], axis=1)

    def preconditioned(coef, residual, applied):
        stacked = stack(coef)
        direction = (residual - split_dot(stacked, wide_split, 1)) * (1.0 / noise_level)
        image = (applied - split_dot(stacked, zed_split, 1)) * (1.0 / noise_level)
        return direction, image

    def multiplied(k, image):
        def one(j, acc):
            return acc + dot_t(dirs[k, j], tile_ref[j])

        return lax.fori_loop(0, n, one, noise_level * image, unroll=4)

    narrow[...] = jnp.zeros_like(narrow)
    for split_ref, ref in ((wide_split, wide_ref), (zed_split, zed_ref)):
        for t, piece in enumerate(pieces(ref[...])):
            split_ref[t] = piece
    residual = rhs_ref[...]
    applied = image_ref[...]
    solution = jnp.zeros_like(residual)
    coef, covered = solve(proj_ref[...])
    all_rz[...] = (square_ref[...] - covered) * (1.0 / noise_level)
    direction, image = preconditioned(coef, residual, applied)

    def keep_own():
        for t in range(per):
            row = pl.ds(rank * per + t, 1)
            kept_proj[t : t + 1, :] = proj_ref[row, :]
            kept_squares[t : t + 1, :] = square_ref[row, :]
            kept_rz[t : t + 1, :] = all_rz[row, :]

    only_owners(keep_own)
    all_here(n)

    def later_answer(k):
        total = collect(k)
        sums = total[:, lanes, :]
        size = kept_rz[...] / unpacked(sums, 0)
        along, image_squares = unpacked(sums, 1), unpacked(sums, 2)
        size_row = jnp.concatenate([size] * lanes, axis=1)
        proj = kept_proj[...] - size_row * joined(total)
        squares = kept_squares[...] - 2.0 * size * along + size * size * image_squares
        coef, covered = solve(proj)
        rz = (squares - covered) * (1.0 / noise_level)
        kept_proj[...] = proj
        kept_squares[...] = squares
        kept_rz[...] = rz
        answer(k, split(coef) + [packed_row([size, rz])])

    def last_sums(values):
        ends[me, 0:1, 0:rhs_count] = dot_t(jnp.ones((8, row_count), jnp.float32), values)[0:1]
        spread(
            n,
            width,
            me,
            lambda peer, i: ends.at[me, pl.ds(0, 1)],
            lambda peer, i: ends.at[me, pl.ds(0, 1)],
            end_send,
            end_recv,
        )
        others = ends.at[pl.ds(0, n - 1), pl.ds(0, 1)]
        drain(others, end_recv)
        total = lax.fori_loop(1, n, lambda i, acc: acc + ends[i, 0:1, :], ends[0, 0:1, :])
        lane_at = lax.broadcasted_iota(jnp.int32, (rhs_count, LANES), 1)
        row_at = lax.broadcasted_iota(jnp.int32, (rhs_count, LANES), 0)
        spread_out = jnp.broadcast_to(total, (rhs_count, LANES))
        drain(others, end_send)
        return wide_sum(jnp.where(lane_at == row_at, spread_out, 0.0))

    relays = []
    for k in range(ITERS - 1):
        dirs[k, me] = image
        relay = Relay(
            n,
            width,
            me,
            dirs.at[k],
            dirs.at[k, me],
            dir_send.at[k],
            dir_recv.at[k],
            dir_pair.at[k],
        )
        relays.append(relay)
        relay.start()
        to_owners(
            k,
            project(image),
            [wide_sum(direction * image), wide_sum(residual * image), wide_sum(image * image)],
        )
        relay.relay_lines()
        only_owners(functools.partial(later_answer, k))
        relay.relay_plane()
        relay.finish()
        twice = multiplied(k, image)
        await_answer(k)
        scalars = ans[k, :, lanes, :]
        size, rz = unpacked(scalars, 0), unpacked(scalars, 1)
        ratio = rz / all_rz[...]
        all_rz[...] = rz
        solution = solution + size * direction
        residual = residual - size * image
        applied = applied - size * twice
        fresh, fresh_image = preconditioned(joined(ans[k]), residual, applied)
        direction = fresh + ratio * direction
        image = fresh_image + ratio * image
    size = all_rz[...] / last_sums(direction * image)
    solution = solution + size * direction
    residual = residual - size * image
    sol_ref[...] = solution
    res_ref[...] = residual
    for relay in relays:
        relay.finish_sends()
    for k in range(ITERS - 1):
        finish_put(k)
        finish_answer(k)


def solve_cg(tile, targets_t, wide_factor, zed, inverse, proj, image, squares, n, width):
    rhs_count, row_count = targets_t.shape
    owners = min(n // 2, rhs_count)
    per = rhs_count // owners
    order = wide_factor.shape[1]
    rows = -(-(order // LANES + 3) // 8) * 8
    vmem = pl.BlockSpec(memory_space=pltpu.VMEM)
    f32 = jnp.float32
    return pl.pallas_call(
        functools.partial(cg_kernel, n, width, owners),
        out_shape=[jax.ShapeDtypeStruct((rhs_count, row_count), f32)] * 2,
        in_specs=[vmem] * 8,
        out_specs=[vmem] * 2,
        scratch_shapes=[
            pltpu.VMEM((ITERS - 1, n, rhs_count, row_count), f32),
            pltpu.VMEM((ITERS - 1, rhs_count, rows, LANES), f32),
            pltpu.VMEM((ITERS - 1, n - 1, per, rows, LANES), f32),
            pltpu.VMEM((ITERS - 1, rhs_count, rows, LANES), f32),
            pltpu.VMEM((per, order), f32),
            pltpu.VMEM((per, LANES), f32),
            pltpu.VMEM((per, LANES), f32),
            pltpu.VMEM((rhs_count, LANES), f32),
            pltpu.VMEM((n, 8, LANES), f32),
            pltpu.VMEM((24, order), f32),
            pltpu.VMEM((3,) + wide_factor.shape, jnp.bfloat16),
            pltpu.VMEM((3,) + wide_factor.shape, jnp.bfloat16),
            pltpu.SemaphoreType.DMA((ITERS - 1,)),
            pltpu.SemaphoreType.DMA((ITERS - 1, n // 2)),
            pltpu.SemaphoreType.DMA((ITERS - 1, width)),
        ]
        + [pltpu.SemaphoreType.DMA((ITERS - 1,))] * 4
        + [pltpu.SemaphoreType.DMA] * 2,
        compiler_params=pltpu.CompilerParams(
            collective_id=2, has_side_effects=True, vmem_limit_bytes=60 * 2**20
        ),
        name="conjugate_gradients",
    )(tile, targets_t, wide_factor, zed, inverse, proj, image, squares)


def finish_kernel(wide_ref, solution_ref, residual_ref, factor_ref, solution_out, residual_out):
    factor_ref[...] = wide_ref[...].astype(jnp.bfloat16)
    solution_out[...] = solution_ref[...]
    residual_out[...] = residual_ref[...]


def finish(wide, solution_t, residual_t):
    vmem = pl.BlockSpec(memory_space=pltpu.VMEM)
    flat = jax.ShapeDtypeStruct(solution_t.shape, jnp.float32)
    return pl.pallas_call(
        finish_kernel,
        out_shape=[jax.ShapeDtypeStruct(wide.shape, jnp.bfloat16), flat, flat],
        in_specs=[vmem] * 3,
        out_specs=[vmem] * 3,
        name="finish_outputs",
    )(wide, solution_t, residual_t)


def per_device(n, width, points, targets, pivots):
    targets_t = targets.T
    all_points, picked = gather_all(points, pivots, n, width)
    inverse, all_targets = pivot_inverse(picked, targets_t, n, width)
    wide, tile, gram, proj, zed, image, squares = sweep(
        all_points, all_targets, picked, inverse, n, width
    )
    solution_t, residual_t = solve_cg(
        tile, targets_t, wide, zed, gram_inverse(gram), proj, image, squares, n, width
    )
    factor, solution_t, residual_t = finish(wide, solution_t, residual_t)
    return (factor, solution_t.T, residual_t.T)


def solution(mesh):
    n, width = mesh.size, mesh.shape["col"]
    return jax.shard_map(
        functools.partial(per_device, n, width),
        mesh=mesh,
        in_specs=(P(("blk", "col"), None), P(("blk", "col"), None), P()),
        out_specs=(P(("blk", "col"), None), P(("blk", "col"), None), P(("blk", "col"), None)),
        check_vma=False,
    )
```

```python
import functools

import jax
import jax.numpy as jnp
from jax import lax
from jax.experimental import pallas as pl
from jax.experimental.pallas import tpu as pltpu
from jax.sharding import PartitionSpec as P

FEATURES = 128
ITERS = 3
LANES = 128


noise_level = 0.5
jitter_level = 0.05
highest = lax.Precision.HIGHEST
MESH = pl.DeviceIdType.MESH


def dot_t(left, right):
    return lax.dot_general(
        left,
        right,
        (((1,), (1,)), ((), ())),
        precision=highest,
        preferred_element_type=jnp.float32,
    )


def pieces(values):
    high = values.astype(jnp.bfloat16)
    rest = values - high.astype(jnp.float32)
    middle = rest.astype(jnp.bfloat16)
    low = (rest - middle.astype(jnp.float32)).astype(jnp.bfloat16)
    return high, middle, low


def split_dot(stacked, refs, side):
    step = stacked.shape[0] // 3
    parts = [
        lax.dot_general(
            stacked[: (3 - k) * step],
            refs[k],
            (((1,), (side,)), ((), ())),
            preferred_element_type=jnp.float32,
        )
        for k in range(3)
    ]
    total = parts[0][2 * step :] + parts[1][step : 2 * step] + parts[2]
    return parts[0][:step] + (parts[0][step : 2 * step] + parts[1][:step] + total)


def stack(values):
    return jnp.concatenate(pieces(values), axis=0)


def column_norms(point_rows):
    wide_rows = point_rows.astype(jnp.float32)
    return jnp.sum(wide_rows * wide_rows, axis=1, keepdims=True)


def row_norms(point_rows):
    wide_rows = point_rows.astype(jnp.float32)
    return dot_t(jnp.ones((8, wide_rows.shape[1]), jnp.float32), wide_rows * wide_rows)[0:1]


def kernel_block(left_rows, left_norms, right_rows, right_norms):
    inner = lax.dot_general(
        left_rows, right_rows, (((1,), (1,)), ((), ())), preferred_element_type=jnp.float32
    )
    distance = left_norms + right_norms - 2.0 * inner
    return jnp.exp(-2.0 * distance / FEATURES)


def lower_inverse_rows(rows):
    count = len(rows)
    group = max(count // 2, 1)
    lane = lax.broadcasted_iota(jnp.int32, (8, LANES), 1)
    sub = lax.broadcasted_iota(jnp.int32, (8, LANES), 0)

    def full_of(values):
        return jnp.broadcast_to(values, (8, LANES))

    def columns(row, base):
        return [full_of(row[:, base + c : base + c + 1]) for c in range(8)]

    rows = list(rows)
    done = []
    for start in range(0, count, group):
        end = start + group
        whole = []
        ahead = columns(rows[start], 8 * start)
        pivot = full_of(ahead[0][0:1])
        for p in range(start, end):
            base = 8 * p
            inside = (lane >= base) & (lane < base + 8)
            cols = ahead
            forward = jnp.where(inside, jnp.where(lane == sub + base, 1.0, 0.0), rows[p])
            pivots = jnp.ones((8, LANES), jnp.float32)
            recips, spread_rows, coefs = [], [], []
            more = p + 1 < end
            if more:
                own = columns(rows[p + 1], base)
                ahead = columns(rows[p + 1], base + 8)
                following = jnp.where(inside, 0.0, rows[p + 1])
            for j in range(8):
                recip = 1.0 / pivot
                pivots = jnp.where(sub == j, pivot, pivots)
                coef = {c: full_of(cols[c][j : j + 1]) for c in range(j + 1, 8)}
                if j < 7:
                    square = full_of(cols[j][j + 1 : j + 2]) * coef[j + 1]
                    pivot = full_of(cols[j + 1][j + 1 : j + 2]) - square * recip
                elif more:
                    corner = full_of(own[7][0:1])
                    pivot = full_of(ahead[0][0:1]) - corner * corner * recip
                scaled = cols[j] * recip
                below = jnp.where(sub > j, scaled, 0.0)
                spread_row = full_of(forward[j : j + 1])
                forward = forward - below * spread_row
                for c in range(j + 1, 8):
                    cols[c] = cols[c] - scaled * coef[c]
                if more:
                    multiplier = own[j] * recip
                    for c in range(j + 1, 8):
                        own[c] = own[c] - multiplier * coef[c]
                    for c in range(8):
                        ahead[c] = ahead[c] - multiplier * full_of(own[j][c : c + 1])
                    following = following - multiplier * spread_row
                recips.append(recip)
                spread_rows.append(spread_row)
                coefs.append(coef)
            scaled = forward * lax.rsqrt(pivots)
            lower = lane <= sub + base
            done.append(jnp.where(lower, scaled, 0.0))
            whole.append(jnp.where(lower | (lane >= 8 * end), scaled, 0.0))
            if more:
                rows[p + 1] = following
            for v in range(p + 2, end):
                own_v = columns(rows[v], base)
                new = jnp.where(inside, 0.0, rows[v])
                for j in range(8):
                    multiplier = own_v[j] * recips[j]
                    new = new - multiplier * spread_rows[j]
                    for c in range(j + 1, 8):
                        own_v[c] = own_v[c] - multiplier * coefs[j][c]
                rows[v] = new
        if end < count:
            side = jnp.concatenate(whole, axis=0)
            both = lax.dot_general(side, side, (((0,), (0,)), ((), ())), precision=highest, preferred_element_type=jnp.float32)
            inside = (lane >= 8 * start) & (lane < 8 * end)
            for v in range(end, count):
                rows[v] = jnp.where(inside, 0.0, rows[v]) - both[8 * v : 8 * v + 8]
    return done

def invert_lower(work, out_ref, beside=None):
    order = work.shape[0]
    blocks = order // LANES
    row_at = lax.broadcasted_iota(jnp.int32, (LANES, LANES), 0)
    col_at = lax.broadcasted_iota(jnp.int32, (LANES, LANES), 1)

    def one_block(j, carry):
        at = pl.multiple_of(j * LANES, LANES)
        inverse = jnp.concatenate(
            lower_inverse_rows(
                [work[pl.ds(at + 8 * v, 8), pl.ds(at, LANES)] for v in range(LANES // 8)]
            ),
            axis=0,
        )
        work[pl.ds(at, LANES), pl.ds(at, LANES)] = jnp.where(row_at == col_at, 1.0, 0.0)

        def combine(k):
            low, high = k * LANES, (k + 1) * LANES
            side = jnp.dot(inverse, work[low:high, :], precision=highest, preferred_element_type=jnp.float32)
            out_ref[low:high, :high] = side[:, :high]
            if high < order:
                out_ref[low:high, high:] = jnp.zeros((LANES, order - high), jnp.float32)
                change = lax.dot_general(side[:, high:], side, (((0,), (0,)), ((), ())), precision=highest, preferred_element_type=jnp.float32)
                if low: work[high:, :low] -= change[:, :low]
                work[high:, low:high] = -change[:, low:high]
                work[high:, high:] -= change[:, high:]

        for k in range(blocks):
            pl.when(j == k)(functools.partial(combine, k))
        if beside is not None:
            beside(j)
        return carry

    lax.fori_loop(0, blocks, one_block, 0)


def shifted(matrix, level):
    row_at = lax.broadcasted_iota(jnp.int32, matrix.shape, 0)
    col_at = lax.broadcasted_iota(jnp.int32, matrix.shape, 1)
    return matrix + jnp.where(row_at == col_at, level, 0.0)


def pivot_kernel(
    n, width, picked_ref, targets_ref, out_ref, all_targets, work, send_sem, recv_sems, pair_sem
):
    me = here(width)
    all_targets[me] = targets_ref[...]
    relay = Relay(
        n, width, me, all_targets, all_targets.at[me], send_sem, recv_sems, pair_sem
    )
    relay.hello()
    picked = picked_ref[...].astype(jnp.bfloat16)
    work[...] = shifted(
        kernel_block(picked, column_norms(picked), picked, row_norms(picked)), jitter_level
    )

    def begin():
        relay.all_here()
        relay.start()

    def beside(j):
        pl.when(j == 0)(begin)
        pl.when(j == 1)(relay.relay_lines)
        pl.when(j == 2)(relay.relay_plane)

    invert_lower(work, out_ref, beside)
    relay.finish()
    relay.finish_sends()


def pivot_inverse(picked, targets_t, n, width):
    order = picked.shape[0]
    vmem = pl.BlockSpec(memory_space=pltpu.VMEM)
    f32 = jnp.float32
    return pl.pallas_call(
        functools.partial(pivot_kernel, n, width),
        out_shape=[
            jax.ShapeDtypeStruct((order, order), f32),
            jax.ShapeDtypeStruct((n,) + targets_t.shape, f32),
        ],
        in_specs=[vmem] * 2,
        out_specs=[vmem] * 2,
        scratch_shapes=[
            pltpu.VMEM((order, order), f32),
            pltpu.SemaphoreType.DMA,
            pltpu.SemaphoreType.DMA((n // 2,)),
            pltpu.SemaphoreType.DMA((width,)),
        ],
        compiler_params=pltpu.CompilerParams(collective_id=3, has_side_effects=True),
        name="pivot_inverse",
    )(picked, targets_t)


def gram_kernel(gram_ref, split_ref, work, out_ref):
    work[...] = shifted(gram_ref[...], noise_level)
    invert_lower(work, out_ref)
    for k, piece in enumerate(pieces(out_ref[...])):
        split_ref[k] = piece


def gram_inverse(gram):
    vmem = pl.BlockSpec(memory_space=pltpu.VMEM)
    return pl.pallas_call(
        gram_kernel,
        out_shape=jax.ShapeDtypeStruct((3,) + gram.shape, jnp.bfloat16),
        in_specs=[vmem],
        out_specs=vmem,
        scratch_shapes=[pltpu.VMEM(gram.shape, jnp.float32)] * 2,
        name="gram_inverse",
    )(gram)


def here(width):
    return lax.axis_index("blk") * width + lax.axis_index("col")


def coords(index, width):
    return (lax.div(index, width), lax.rem(index, width))


def hello(n, width, me):
    barrier = pltpu.get_barrier_semaphore()

    def one(i, carry):
        peer = lax.rem(me + i, n)
        pl.semaphore_signal(
            barrier, inc=1, device_id=coords(peer, width), device_id_type=MESH
        )
        return carry

    lax.fori_loop(1, n, one, 0)


def all_here(n):
    pl.semaphore_wait(pltpu.get_barrier_semaphore(), n - 1)


def spread(n, width, me, src, dst, send_sem, recv_sem):
    def push(i, carry):
        peer = lax.rem(me + i, n)
        pltpu.make_async_remote_copy(
            src_ref=src(peer, i),
            dst_ref=dst(peer, i),
            send_sem=send_sem,
            recv_sem=recv_sem,
            device_id=coords(peer, width),
            device_id_type=MESH,
        ).start()
        return carry

    lax.fori_loop(1, n, push, 0)


def drain(ref, sem):
    pltpu.make_async_copy(ref, ref, sem).wait()


def flip(index, bits):
    moved = index
    weight = 1
    while weight <= bits:
        if bits & weight:
            moved = moved + weight * (1 - 2 * lax.rem(lax.div(index, weight), 2))
        weight *= 2
    return moved


class Relay:
    def __init__(self, n, width, me, blocks, own, send_sem, recv_sems, pair_sems):
        self.n, self.width, self.me = n, width, me
        self.blocks, self.own = blocks, own
        self.send_sem, self.recv_sems, self.pair_sems = send_sem, recv_sems, pair_sems
        self.plane = 2 * width
        self.lines = n // self.plane

    def hello(self):
        barrier = pltpu.get_barrier_semaphore()

        def signal(peer):
            pl.semaphore_signal(
                barrier, inc=1, device_id=coords(peer, self.width), device_id_type=MESH
            )

        def along(i, carry):
            signal(lax.rem(self.me + self.plane * i, self.n))
            return carry

        lax.fori_loop(1, self.lines, along, 0)
        for q in range(2, self.plane, 2):
            signal(flip(self.me, q))
        signal(flip(self.me, 1))

    def all_here(self):
        pl.semaphore_wait(
            pltpu.get_barrier_semaphore(), self.lines - 1 + self.plane // 2
        )

    def send(self, src_ref, source, peer, recv_sem):
        pltpu.make_async_remote_copy(
            src_ref=src_ref,
            dst_ref=self.blocks.at[source],
            send_sem=self.send_sem,
            recv_sem=recv_sem,
            device_id=coords(peer, self.width),
            device_id_type=MESH,
        ).start()

    def fan(self, src_ref, source, i):
        for q in range(2, self.plane, 2):
            sem = self.recv_sems.at[self.lines * (q // 2) + i]
            self.send(src_ref, source, flip(self.me, q), sem)
        self.send(src_ref, source, flip(self.me, 1), self.pair_sems.at[0])

    def start(self):
        def along(i, carry):
            peer = lax.rem(self.me + self.plane * i, self.n)
            self.send(self.own, self.me, peer, self.recv_sems.at[i])
            return carry

        lax.fori_loop(1, self.lines, along, 0)
        self.fan(self.own, self.me, 0)

    def relay_lines(self):
        def one(i, carry):
            source = lax.rem(self.me - self.plane * i + self.n, self.n)
            drain(self.blocks.at[source], self.recv_sems.at[i])
            self.fan(self.blocks.at[source], source, i)
            return carry

        lax.fori_loop(1, self.lines, one, 0)

    def relay_plane(self, *offsets):
        for q in offsets or range(2, self.plane, 2):

            def one(i, carry, q=q):
                source = lax.rem(flip(self.me, q) - self.plane * i + self.n, self.n)
                ref = self.blocks.at[source]
                drain(ref, self.recv_sems.at[self.lines * (q // 2) + i])
                self.send(ref, source, flip(self.me, 1), self.pair_sems.at[q // 2])
                return carry

            lax.fori_loop(0, self.lines, one, 0)

    def finish(self, *offsets):
        for q in offsets or range(0, self.plane, 2):
            drain(self.blocks.at[pl.ds(0, self.lines)], self.pair_sems.at[q // 2])

    def finish_sends(self):
        drain(self.blocks.at[pl.ds(0, self.n - 1)], self.send_sem)


def gather_kernel(
    n,
    width,
    points_ref,
    pivots_ref,
    all_points,
    picked_ref,
    send_sem,
    recv_sems,
    pair_sem,
    own_sem,
):
    me = here(width)
    relay = Relay(n, width, me, all_points, points_ref, send_sem, recv_sems, pair_sem)
    relay.hello()
    keep = pltpu.make_async_copy(points_ref, all_points.at[me], own_sem)
    keep.start()
    rows = points_ref.shape[0]
    order = picked_ref.shape[0]
    pivots = pivots_ref[...].astype(jnp.float32)
    in_row = jnp.concatenate([pivots[k : k + 1] for k in range(pivots.shape[0])], axis=1)
    in_column = jnp.broadcast_to(in_row, (8, order)).T
    chosen = jnp.broadcast_to(in_column[:, 0:1], (order, rows))
    row_at = lax.broadcasted_iota(jnp.int32, (order, rows), 1).astype(jnp.float32)
    together = min(4, relay.lines)
    picked_ref[...] = jnp.zeros_like(picked_ref)
    relay.all_here()
    relay.start()

    def pick(group):
        def one(i, carry):
            sources = [group + relay.plane * (together * i + t) for t in range(together)]
            hits = [
                jnp.where(chosen - (rows * source).astype(jnp.float32) == row_at, 1.0, 0.0).astype(jnp.bfloat16)
                for source in sources
            ]
            found = jnp.concatenate([all_points[source] for source in sources], axis=0)
            picked_ref[...] += jnp.dot(
                jnp.concatenate(hits, axis=1), found, preferred_element_type=jnp.float32
            )
            return carry

        lax.fori_loop(0, relay.lines // together, one, 0)

    def low(bits):
        return lax.rem(flip(me, bits), relay.plane)

    relay.relay_lines()
    keep.wait()
    pick(low(0))
    for q in range(2, relay.plane, 2):
        relay.relay_plane(q)
        pick(low(q))
    for q in range(0, relay.plane, 2):
        relay.finish(q)
        pick(low(q + 1))
    relay.finish_sends()


def gather_all(points, pivots, n, width):
    vmem = pl.BlockSpec(memory_space=pltpu.VMEM)
    order = pivots.shape[0] * pivots.shape[1]
    return pl.pallas_call(
        functools.partial(gather_kernel, n, width),
        out_shape=[
            jax.ShapeDtypeStruct((n,) + points.shape, points.dtype),
            jax.ShapeDtypeStruct((order, points.shape[1]), jnp.float32),
        ],
        in_specs=[vmem] * 2,
        out_specs=[vmem] * 2,
        scratch_shapes=[
            pltpu.SemaphoreType.DMA,
            pltpu.SemaphoreType.DMA((n // 2,)),
            pltpu.SemaphoreType.DMA((width,)),
            pltpu.SemaphoreType.DMA,
        ],
        compiler_params=pltpu.CompilerParams(collective_id=0, has_side_effects=True),
        name="gather_points",
    )(points, pivots)


def sweep_kernel(
    n,
    width,
    points_ref,
    targets_ref,
    picked_ref,
    inverse_ref,
    wide_ref,
    tile_ref,
    gram_ref,
    proj_ref,
    zed_ref,
    image_ref,
    square_ref,
    left_part,
    right_part,
    left_got,
    right_got,
    crossed,
    send_sem,
    recv_sem,
):
    me = here(width)
    core, pair = lax.rem(me, 2), lax.div(me, 2)
    other = 1 - core
    partner = flip(me, 1)
    barrier = pltpu.get_barrier_semaphore()
    pl.semaphore_signal(barrier, inc=1, device_id=coords(partner, width), device_id_type=MESH)
    order = inverse_ref.shape[0]
    half = order // 2
    chunk = min(4, n // 2)
    picked = picked_ref[...].astype(jnp.bfloat16)
    picked_column = column_norms(picked)
    own = points_ref[pair, core]
    beside = points_ref[pair, other]
    own_column, beside_column = column_norms(own), column_norms(beside)
    own_targets = targets_ref[pair, core]
    image_ref[...] = noise_level * own_targets
    square_ref[...] = jnp.zeros_like(square_ref)
    for ref in (left_part, right_part):
        ref[...] = jnp.zeros_like(ref)

    steps = n // 2 // chunk

    def cross_of(i):
        at = i * chunk
        near = jnp.concatenate([points_ref[at + t, core] for t in range(chunk)], axis=0)
        return kernel_block(picked, picked_column, near, row_norms(near))

    crossed[...] = cross_of(0)

    def step(i, carry):
        at = i * chunk
        cross = crossed[...]
        near = jnp.concatenate([points_ref[at + t, core] for t in range(chunk)], axis=0)
        far = jnp.concatenate([points_ref[at + t, other] for t in range(chunk)], axis=0)
        near_targets = jnp.concatenate([targets_ref[at + t, core] for t in range(chunk)], axis=1)
        far_targets = jnp.concatenate([targets_ref[at + t, other] for t in range(chunk)], axis=1)
        near_row, far_row = row_norms(near), row_norms(far)
        own_near = kernel_block(own, own_column, near, near_row)
        own_far = kernel_block(own, own_column, far, far_row)
        beside_near = kernel_block(beside, beside_column, near, near_row)
        size = own.shape[0]
        for t in range(chunk):
            tile_ref[at + t, core] = own_near[:, t * size : (t + 1) * size]
            tile_ref[at + t, other] = own_far[:, t * size : (t + 1) * size]
        first = jnp.dot(
            inverse_ref[:, :half],
            cross[:half],
            precision=highest,
            preferred_element_type=jnp.float32,
        )
        top = first[:half]
        low = first[half:] + jnp.dot(
            inverse_ref[half:, half:],
            cross[half:],
            precision=highest,
            preferred_element_type=jnp.float32,
        )
        crossed[...] = cross_of(jnp.minimum(i + 1, steps - 1))
        extra = [own_near, beside_near, near_targets]
        left_part[...] += dot_t(jnp.concatenate([top] + extra, axis=0), top)
        right_part[...] += dot_t(jnp.concatenate([top, low] + extra, axis=0), low)
        image_ref[...] += split_dot(
            stack(jnp.concatenate([near_targets, far_targets], axis=1)),
            pieces(jnp.concatenate([own_near, own_far], axis=1)),
            1,
        )
        squares = near_targets * near_targets + far_targets * far_targets
        for t in range(chunk):
            square_ref[...] += squares[:, t * size : (t + 1) * size]

        @pl.when(i == lax.div(pair, chunk))
        def _():
            for t in range(chunk):

                @pl.when(lax.rem(pair, chunk) == t)
                def _(t=t):
                    for rows, value in ((slice(0, half), top), (slice(half, order), low)):
                        wide_ref[:, rows] = value[:, t * size : (t + 1) * size].T

        return carry

    lax.fori_loop(0, steps, step, 0)
    pl.semaphore_wait(barrier, 1)
    size = own.shape[0]
    sides = [(left_part, left_got, half, 0), (right_part, right_got, order, half)]
    copies = []
    for part, got, tall, _ in sides:
        for rows in (pl.ds(0, tall), pl.ds(tall + size, part.shape[0] - tall - size)):
            copy = pltpu.make_async_remote_copy(
                src_ref=part.at[rows],
                dst_ref=got.at[rows],
                send_sem=send_sem.at[len(copies)],
                recv_sem=recv_sem.at[len(copies)],
                device_id=coords(partner, width),
                device_id_type=MESH,
            )
            copy.start()
            copies.append(copy)
    square_ref[...] = jnp.broadcast_to(
        jnp.sum(square_ref[...], axis=1, keepdims=True), square_ref.shape
    )
    gram_ref[half:, :half] = jnp.zeros((order - half, half), jnp.float32)
    for copy in copies:
        copy.wait_recv()
    for part, got, tall, at in sides:
        lanes = slice(at, at + part.shape[1])
        gram_ref[:tall, lanes] = part[:tall] + got[:tall]
        zed_ref[:, lanes] = (
            noise_level * wide_ref[:, lanes]
            + part[tall : tall + size]
            + got[tall + size : tall + 2 * size]
        )
        proj_ref[:, lanes] = part[tall + 2 * size :] + got[tall + 2 * size :]
    for copy in copies:
        copy.wait_send()


def sweep(all_points, all_targets, picked, inverse, n, width):
    rows, rhs_count, order = all_points.shape[1], all_targets.shape[1], picked.shape[0]
    vmem = pl.BlockSpec(memory_space=pltpu.VMEM)
    f32 = jnp.float32
    half = order // 2
    extra = 2 * rows + rhs_count
    partial = [
        pltpu.VMEM((half + extra, half), f32),
        pltpu.VMEM((order + extra, order - half), f32),
    ]
    wide, tile, *rest = pl.pallas_call(
        functools.partial(sweep_kernel, n, width),
        out_shape=[
            jax.ShapeDtypeStruct(shape, dtype)
            for shape, dtype in [
                ((rows, order), f32),
                ((n // 2, 2, rows, rows), f32),
                ((order, order), f32),
                ((rhs_count, order), f32),
                ((rows, order), f32),
                ((rhs_count, rows), f32),
                ((rhs_count, rows), f32),
            ]
        ],
        in_specs=[vmem] * 4,
        out_specs=[vmem] * 7,
        scratch_shapes=partial * 2
        + [pltpu.VMEM((order, min(4, n // 2) * rows), f32)]
        + [pltpu.SemaphoreType.DMA((4,))] * 2,
        compiler_params=pltpu.CompilerParams(
            collective_id=1, has_side_effects=True, vmem_limit_bytes=60 * 2**20
        ),
        name="sweep_points",
    )(
        all_points.reshape((n // 2, 2) + all_points.shape[1:]),
        all_targets.reshape((n // 2, 2) + all_targets.shape[1:]),
        picked,
        inverse,
    )
    return [wide, tile.reshape(n, rows, rows)] + rest


def cg_kernel(
    n,
    width,
    owners,
    tile_ref,
    rhs_ref,
    wide_ref,
    zed_ref,
    inverse_ref,
    proj_ref,
    image_ref,
    square_ref,
    sol_ref,
    res_ref,
    dirs,
    put,
    got,
    ans,
    kept_proj,
    kept_squares,
    kept_rz,
    all_rz,
    ends,
    narrow,
    wide_split,
    zed_split,
    dir_send,
    dir_recv,
    dir_pair,
    put_send,
    put_recv,
    ans_send,
    ans_recv,
    end_send,
    end_recv,
):
    me = here(width)
    rhs_count, row_count = rhs_ref.shape
    per = rhs_count // owners
    order = wide_ref.shape[1]
    lanes = order // LANES
    first_owner = (n - owners) // 2
    rank = me - first_owner
    owning = (rank >= 0) & (rank < owners)
    own_rows = pl.ds(rank * per, per)
    sent = pl.ds(0, lanes + 1)
    hello(n, width, me)

    def packed_row(values):
        lane_at = lax.broadcasted_iota(jnp.int32, values[0].shape, 1)
        row = values[-1]
        for s in range(len(values) - 1):
            row = jnp.where(lane_at == s, values[s], row)
        return row

    def unpacked(row, s):
        return jnp.broadcast_to(row[:, s : s + 1], row.shape)

    def only_owners(body):
        pl.when(owning)(body)

    def wide_sum(values):
        return jnp.broadcast_to(jnp.sum(values, axis=1, keepdims=True), (values.shape[0], LANES))

    def to_owners(k, proj, sums):
        for q in range(lanes):
            put[k, :, q, :] = proj[:, q * LANES : (q + 1) * LANES]
        put[k, :, lanes, :] = packed_row(sums)

        def push(i, carry):
            turn = lax.rem(me + i, owners)
            peer = first_owner + turn

            @pl.when(peer != me)
            def _():
                pltpu.make_async_remote_copy(
                    src_ref=put.at[k, pl.ds(turn * per, per), sent],
                    dst_ref=got.at[k, lax.rem(me - peer + n, n) - 1, :, sent],
                    send_sem=put_send.at[k],
                    recv_sem=put_recv.at[k],
                    device_id=coords(peer, width),
                    device_id_type=MESH,
                ).start()

            return carry

        lax.fori_loop(0, owners, push, 0)

    def drain_others(ref, sem):
        @pl.when(owning)
        def _():
            drain(ref.at[pl.ds(0, (owners - 1) * per)], sem)

        @pl.when(jnp.logical_not(owning))
        def _():
            drain(ref, sem)

    def finish_put(k):
        drain_others(put.at[k, :, sent], put_send.at[k])

    def collect(k):
        drain(got.at[k, :, :, sent], put_recv.at[k])
        start = put[k, own_rows, : lanes + 1]
        return lax.fori_loop(0, n - 1, lambda i, acc: acc + got[k, i, :, : lanes + 1], start)

    def answer(k, rows):
        for s, value in enumerate(rows):
            ans[k, own_rows, s, :] = value
        spread(
            n,
            width,
            me,
            lambda peer, i: ans.at[k, own_rows, sent],
            lambda peer, i: ans.at[k, own_rows, sent],
            ans_send.at[k],
            ans_recv.at[k],
        )

    def await_answer(k):
        drain_others(ans.at[k, :, sent], ans_recv.at[k])

    def finish_answer(k):
        def body():
            def one(i, carry):
                drain(ans.at[k, pl.ds(0, per), sent], ans_send.at[k])
                return carry

            lax.fori_loop(1, n, one, 0)

        only_owners(body)

    def solve(proj):
        def stacked(values):
            if values.shape[0] % 16 == 0:
                return stack(values)
            for t, piece in enumerate(pieces(values)):
                narrow[8 * t : 8 * t + values.shape[0], :] = piece.astype(jnp.float32)
            return narrow[...].astype(jnp.bfloat16)

        count = proj.shape[0]
        half = split_dot(stacked(proj), inverse_ref, 1)[:count]
        coef = split_dot(stacked(half), inverse_ref, 0)[:count]
        return coef, wide_sum(half * half)

    def split(row):
        return [row[:, q * LANES : (q + 1) * LANES] for q in range(lanes)]

    def project(rows):
        return split_dot(stack(rows), wide_split, 0)

    def joined(packed):
        return jnp.concatenate([packed[:, q, :] for q in range(lanes)], axis=1)

    def preconditioned(coef, residual, applied):
        stacked = stack(coef)
        direction = (residual - split_dot(stacked, wide_split, 1)) * (1.0 / noise_level)
        image = (applied - split_dot(stacked, zed_split, 1)) * (1.0 / noise_level)
        return direction, image

    def multiplied(k, core, start):
        def one(i, acc):
            return acc + dot_t(dirs[k, 2 * i + core], tile_ref[2 * i + core])

        return lax.fori_loop(0, n // 2, one, start, unroll=4)

    narrow[...] = jnp.zeros_like(narrow)
    for split_ref, ref in ((wide_split, wide_ref), (zed_split, zed_ref)):
        for t, piece in enumerate(pieces(ref[...])):
            split_ref[t] = piece
    residual = rhs_ref[...]
    applied = image_ref[...]
    solution = jnp.zeros_like(residual)
    coef, covered = solve(proj_ref[...])
    all_rz[...] = (square_ref[...] - covered) * (1.0 / noise_level)
    direction, image = preconditioned(coef, residual, applied)

    def keep_own():
        for t in range(per):
            row = pl.ds(rank * per + t, 1)
            kept_proj[t : t + 1, :] = proj_ref[row, :]
            kept_squares[t : t + 1, :] = square_ref[row, :]
            kept_rz[t : t + 1, :] = all_rz[row, :]

    only_owners(keep_own)
    all_here(n)

    def later_answer(k):
        total = collect(k)
        sums = total[:, lanes, :]
        size = kept_rz[...] / unpacked(sums, 0)
        along, image_squares = unpacked(sums, 1), unpacked(sums, 2)
        size_row = jnp.concatenate([size] * lanes, axis=1)
        proj = kept_proj[...] - size_row * joined(total)
        squares = kept_squares[...] - 2.0 * size * along + size * size * image_squares
        coef, covered = solve(proj)
        rz = (squares - covered) * (1.0 / noise_level)
        kept_proj[...] = proj
        kept_squares[...] = squares
        kept_rz[...] = rz
        answer(k, split(coef) + [packed_row([size, rz])])

    def last_sums(values):
        ends[me, 0:1, 0:rhs_count] = dot_t(jnp.ones((8, row_count), jnp.float32), values)[0:1]
        spread(
            n,
            width,
            me,
            lambda peer, i: ends.at[me, pl.ds(0, 1)],
            lambda peer, i: ends.at[me, pl.ds(0, 1)],
            end_send,
            end_recv,
        )
        others = ends.at[pl.ds(0, n - 1), pl.ds(0, 1)]
        drain(others, end_recv)
        total = lax.fori_loop(1, n, lambda i, acc: acc + ends[i, 0:1, :], ends[0, 0:1, :])
        lane_at = lax.broadcasted_iota(jnp.int32, (rhs_count, LANES), 1)
        row_at = lax.broadcasted_iota(jnp.int32, (rhs_count, LANES), 0)
        spread_out = jnp.broadcast_to(total, (rhs_count, LANES))
        drain(others, end_send)
        return wide_sum(jnp.where(lane_at == row_at, spread_out, 0.0))

    relays = []
    for k in range(ITERS - 1):
        dirs[k, me] = image
        relay = Relay(
            n,
            width,
            me,
            dirs.at[k],
            dirs.at[k, me],
            dir_send.at[k],
            dir_recv.at[k],
            dir_pair.at[k],
        )
        relays.append(relay)
        relay.start()
        to_owners(
            k,
            project(image),
            [wide_sum(direction * image), wide_sum(residual * image), wide_sum(image * image)],
        )
        relay.relay_lines()
        only_owners(functools.partial(later_answer, k))
        relay.relay_plane()
        twice = multiplied(k, lax.rem(me, 2), noise_level * image)
        relay.finish()
        twice = multiplied(k, 1 - lax.rem(me, 2), twice)
        await_answer(k)
        scalars = ans[k, :, lanes, :]
        size, rz = unpacked(scalars, 0), unpacked(scalars, 1)
        ratio = rz / all_rz[...]
        all_rz[...] = rz
        solution = solution + size * direction
        residual = residual - size * image
        applied = applied - size * twice
        fresh, fresh_image = preconditioned(joined(ans[k]), residual, applied)
        direction = fresh + ratio * direction
        image = fresh_image + ratio * image
    size = all_rz[...] / last_sums(direction * image)
    solution = solution + size * direction
    residual = residual - size * image
    sol_ref[...] = solution
    res_ref[...] = residual
    for relay in relays:
        relay.finish_sends()
    for k in range(ITERS - 1):
        finish_put(k)
        finish_answer(k)


def solve_cg(tile, targets_t, wide_factor, zed, inverse, proj, image, squares, n, width):
    rhs_count, row_count = targets_t.shape
    owners = min(n // 2, rhs_count)
    per = rhs_count // owners
    order = wide_factor.shape[1]
    rows = -(-(order // LANES + 3) // 8) * 8
    vmem = pl.BlockSpec(memory_space=pltpu.VMEM)
    f32 = jnp.float32
    return pl.pallas_call(
        functools.partial(cg_kernel, n, width, owners),
        out_shape=[jax.ShapeDtypeStruct((rhs_count, row_count), f32)] * 2,
        in_specs=[vmem] * 8,
        out_specs=[vmem] * 2,
        scratch_shapes=[
            pltpu.VMEM((ITERS - 1, n, rhs_count, row_count), f32),
            pltpu.VMEM((ITERS - 1, rhs_count, rows, LANES), f32),
            pltpu.VMEM((ITERS - 1, n - 1, per, rows, LANES), f32),
            pltpu.VMEM((ITERS - 1, rhs_count, rows, LANES), f32),
            pltpu.VMEM((per, order), f32),
            pltpu.VMEM((per, LANES), f32),
            pltpu.VMEM((per, LANES), f32),
            pltpu.VMEM((rhs_count, LANES), f32),
            pltpu.VMEM((n, 8, LANES), f32),
            pltpu.VMEM((24, order), f32),
            pltpu.VMEM((3,) + wide_factor.shape, jnp.bfloat16),
            pltpu.VMEM((3,) + wide_factor.shape, jnp.bfloat16),
            pltpu.SemaphoreType.DMA((ITERS - 1,)),
            pltpu.SemaphoreType.DMA((ITERS - 1, n // 2)),
            pltpu.SemaphoreType.DMA((ITERS - 1, width)),
        ]
        + [pltpu.SemaphoreType.DMA((ITERS - 1,))] * 4
        + [pltpu.SemaphoreType.DMA] * 2,
        compiler_params=pltpu.CompilerParams(
            collective_id=2, has_side_effects=True, vmem_limit_bytes=60 * 2**20
        ),
        name="conjugate_gradients",
    )(tile, targets_t, wide_factor, zed, inverse, proj, image, squares)


def finish_kernel(wide_ref, solution_ref, residual_ref, factor_ref, solution_out, residual_out):
    factor_ref[...] = wide_ref[...].astype(jnp.bfloat16)
    solution_out[...] = solution_ref[...]
    residual_out[...] = residual_ref[...]


def finish(wide, solution_t, residual_t):
    vmem = pl.BlockSpec(memory_space=pltpu.VMEM)
    flat = jax.ShapeDtypeStruct(solution_t.shape, jnp.float32)
    return pl.pallas_call(
        finish_kernel,
        out_shape=[jax.ShapeDtypeStruct(wide.shape, jnp.bfloat16), flat, flat],
        in_specs=[vmem] * 3,
        out_specs=[vmem] * 3,
        name="finish_outputs",
    )(wide, solution_t, residual_t)


def per_device(n, width, points, targets, pivots):
    targets_t = targets.T
    all_points, picked = gather_all(points, pivots, n, width)
    inverse, all_targets = pivot_inverse(picked, targets_t, n, width)
    wide, tile, gram, proj, zed, image, squares = sweep(
        all_points, all_targets, picked, inverse, n, width
    )
    solution_t, residual_t = solve_cg(
        tile, targets_t, wide, zed, gram_inverse(gram), proj, image, squares, n, width
    )
    factor, solution_t, residual_t = finish(wide, solution_t, residual_t)
    return (factor, solution_t.T, residual_t.T)


def solution(mesh):
    n, width = mesh.size, mesh.shape["col"]
    return jax.shard_map(
        functools.partial(per_device, n, width),
        mesh=mesh,
        in_specs=(P(("blk", "col"), None), P(("blk", "col"), None), P()),
        out_specs=(P(("blk", "col"), None), P(("blk", "col"), None), P(("blk", "col"), None)),
        check_vma=False,
    )
```
